32 devices in a mesh: px: 4 (over x, core), py: 8 (over z, y).
Axes of the slice: x: 2, y: 2, z: 4, core: 2. Of those that a mesh axis runs over, the one named last changes fastest.
Arguments:
- horiz_div: float32 [128, 1024, 1024], P('py', 'px'), may hold values from -6 to 6
- w_star: float32 [128, 1024, 1024], P('py', 'px'), may hold values from -6 to 6
- air_temp: bfloat16 [128, 1024, 1024], P('py', 'px'), may hold values from -6 to 6
- roof_level: int32 [1024, 1024], P('px'), may hold values from 0 to 63
- facet_cells: int32 [32, 1024], P(('px', 'py')), may hold values from -1 to 4194303, as said below
- facet_temp: float32 [32, 1024], P(('px', 'py')), may hold values from -6 to 6
- net_radiation: float32 [32, 1024], P(('px', 'py')), may hold values from -6 to 6
- heat_capacity: float32 [32, 1024], P(('px', 'py')), may hold values from 1 to 4
- drag_coef: float32 [32, 1024], P(('px', 'py')), may hold values from 0.05 to 0.5
- heat_coef: float32 [32, 1024], P(('px', 'py')), may hold values from 0.05 to 0.5
Outputs:
- w_new: float32 [128, 1024, 1024], P('py', 'px')
- theta_new: bfloat16 [128, 1024, 1024], P('py', 'px')
- facet_temp_new: float32 [32, 1024], P(('px', 'py'))
The draws below stay inside these ranges and needn't reach their ends.
Inputs may be any that keep to these rules, and one draw needn't show every extreme that they name: `facet_cells`: in each block of 32 rows the non-empty rows come first. For every device one owner's block is full, the same owner for all devices.
All inputs are finite; a program needn't handle non-finite values.
Results may differ from the reference program's by a relative error of at most 0.001.
Values sent between devices are 32-bit elements; how exact they have to be, the bound alone decides.
A program may use at most 320 MiB of HBM per device.

```python
import math
import jax
import jax.numpy as jnp
from jax import lax

NX = 1024
NY = 1024
NZ = 128
SLOT = 32
CELLS_DEV = 4194304
N_PX = 4
N_PY = 8
DEVICES = 32


def draw_facet_cells(key, part):
    key_counts, key_busy, key_cells = jax.random.split(jax.random.fold_in(key, 11), 3)
    counts = jax.random.randint(key_counts, (DEVICES, DEVICES), SLOT // 4, SLOT + 1)
    busy_owner = jax.random.randint(key_busy, (), 0, DEVICES)
    owner_ids = jnp.arange(DEVICES, dtype=jnp.int32)
    counts = jnp.where(owner_ids[None, :] == busy_owner, SLOT, counts)
    slot_ids = jnp.arange(SLOT, dtype=jnp.int32)
    is_live = slot_ids[None, None, :] < counts[:, :, None]
    cell_ids = jax.random.randint(key_cells, (DEVICES, DEVICES, SLOT), 0, CELLS_DEV)
    cell_ids = cell_ids.at[0, busy_owner, 0].set(CELLS_DEV - 1)
    return jnp.where(is_live, cell_ids, -1).reshape(DEVICES, DEVICES * SLOT).astype(jnp.int32)


def touch_ends(result, stream_key, least, high):
    longest = result.shape.index(max(result.shape))
    spots = []
    for shift in (0, 1):
        where = [jax.random.randint(jax.random.fold_in(stream_key, axis), (), 0, length) for axis, length in enumerate(result.shape)]
        where[longest] = (where[longest] + shift) % result.shape[longest]
        spots.append(tuple(where))
    return result.at[spots[0]].set(least).at[spots[1]].set(high)


def block_levels(own_key, shape, cuts, least, high):
    def one(axis_at, shards_of):
        steps = jax.random.uniform(jax.random.fold_in(jax.random.fold_in(own_key, 6), axis_at), (shards_of,), jnp.float32, least / len(cuts), high / len(cuts))
        return jnp.repeat(jnp.exp(steps), shape[axis_at] // shards_of).reshape((-1,) + (1,) * (len(shape) - axis_at - 1))

    loudness = one(*cuts[0])
    for cut in cuts[1:]:
        loudness = loudness * one(*cut)
    return loudness


def gaussian(stream_key, shape, width, limit, cuts=(), kind=jnp.bfloat16):
    array = width * jax.random.normal(stream_key, shape, jnp.float32)
    if cuts:
        array = array * block_levels(stream_key, shape, cuts, -0.22, 0.18)
    return jnp.clip(array, -limit, limit).astype(kind)


def setup_inputs(seed: int = 0) -> dict:
    streams_of = jax.random.split(jax.random.key(seed), 11)
    return {
        "horiz_div": gaussian(streams_of[0], (NZ, NY, NX), 1.0, 6.0, ((0, 8), (1, 4)), jnp.float32),
        "w_star": gaussian(streams_of[1], (NZ, NY, NX), 1.0, 6.0, ((0, 8), (1, 4)), jnp.float32),
        "air_temp": gaussian(streams_of[2], (NZ, NY, NX), 1.0, 6.0, ((0, 8), (1, 4))),
        "roof_level": touch_ends(jax.random.randint(streams_of[3], (NY, NX), 0, NZ // 2), jax.random.fold_in(streams_of[3], 1), 0, (NZ // 2) - 1).astype(jnp.int32),
        "facet_cells": draw_facet_cells(jax.random.fold_in(streams_of[10], 71), 0),
        "facet_temp": gaussian(streams_of[5], (DEVICES, DEVICES * SLOT), 1.0, 6.0, ((0, 32),), jnp.float32),
        "net_radiation": gaussian(streams_of[6], (DEVICES, DEVICES * SLOT), 1.0, 6.0, ((0, 32),), jnp.float32),
        "heat_capacity": jnp.clip(jnp.exp(math.log(4.0) - 1.3862944 * jax.random.uniform(streams_of[7], (DEVICES, DEVICES * SLOT), jnp.float32) ** block_levels(streams_of[7], (DEVICES, DEVICES * SLOT), ((0, 32),), -0.2, 0.2)), 1.0, 4.0),
        "drag_coef": jnp.clip(jnp.exp(math.log(0.5) - 2.3025851 * jax.random.uniform(streams_of[8], (DEVICES, DEVICES * SLOT), jnp.float32) ** block_levels(streams_of[8], (DEVICES, DEVICES * SLOT), ((0, 32),), -0.2, 0.2)), 0.05, 0.5),
        "heat_coef": jnp.clip(jnp.exp(math.log(0.5) - 2.3025851 * jax.random.uniform(streams_of[9], (DEVICES, DEVICES * SLOT), jnp.float32) ** block_levels(streams_of[9], (DEVICES, DEVICES * SLOT), ((0, 32),), -0.2, 0.2)), 0.05, 0.5),
    }


def to_devices(field):
    shaped = field.reshape(N_PY, NZ // N_PY, N_PX, NY // N_PX, NX)
    return shaped.transpose(2, 0, 1, 3, 4).reshape(DEVICES, -1)

def from_devices(device_rows):
    shaped = device_rows.reshape(N_PX, N_PY, NZ // N_PY, NY // N_PX, NX)
    return shaped.transpose(1, 2, 0, 3, 4).reshape(NZ, NY, NX)

def owner_major(values):
    return values.reshape(DEVICES, DEVICES, SLOT).transpose(1, 0, 2).reshape(DEVICES, DEVICES * SLOT)

def reference(horiz_div, w_star, air_temp, roof_level, facet_cells, facet_temp, net_radiation, heat_capacity, drag_coef, heat_coef):
    is_live = facet_cells >= 0
    safe_ids = jnp.maximum(facet_cells, 0).astype(jnp.int32)
    w_rows = to_devices(w_star)
    temp_rows = to_devices(air_temp.astype(jnp.float32))
    w_cell = jnp.where(is_live, jnp.take_along_axis(w_rows, safe_ids, axis=1), 0.0)
    temp_cell = jnp.where(is_live, jnp.take_along_axis(temp_rows, safe_ids, axis=1), 0.0)
    w_owner = owner_major(w_cell)
    temp_owner = owner_major(temp_cell)
    speeds = jnp.sqrt(w_owner * w_owner + 0.25)
    stress = drag_coef * speeds * w_owner
    heat_flux = heat_coef * speeds * (facet_temp - temp_owner)
    facet_temp_new = facet_temp + (net_radiation - heat_flux - 0.5 * facet_temp) / heat_capacity
    stress_src = jnp.where(is_live, owner_major(stress), 0.0)
    heat_src = jnp.where(is_live, owner_major(heat_flux), 0.0)
    device_ids = jnp.arange(DEVICES, dtype=jnp.int32)[:, None]
    w_rows = w_rows.at[device_ids, safe_ids].add(-stress_src)
    temp_rows = temp_rows.at[device_ids, safe_ids].add(heat_src)
    w_corr = from_devices(w_rows)
    theta_new = from_devices(temp_rows).astype(jnp.bfloat16)
    w_up = jnp.concatenate([w_corr[1:], jnp.zeros((1, NY, NX), jnp.float32)], axis=0)
    rhs = horiz_div + w_up - w_corr
    spectrum = jnp.fft.rfft2(rhs, axes=(1, 2))
    eigen_x = 2.0 * jnp.cos(2.0 * math.pi / NX * jnp.arange(NX // 2 + 1, dtype=jnp.float32)) - 2.0
    eigen_y = 2.0 * jnp.cos(2.0 * math.pi / NY * jnp.arange(NY, dtype=jnp.float32)) - 2.0
    stacked = jnp.stack([spectrum.real, spectrum.imag], axis=-1).transpose(1, 2, 0, 3)
    main_diag = jnp.full((NZ,), -2.0, jnp.float32).at[0].set(-1.0).at[NZ - 1].set(-3.0)
    lower_diag = jnp.ones((NZ,), jnp.float32).at[0].set(0.0)
    upper_diag = jnp.ones((NZ,), jnp.float32).at[NZ - 1].set(0.0)

    def solve_row(pieces):
        mode_row, shift_y = pieces
        diagonal = main_diag[None, :] + (shift_y + eigen_x)[:, None]
        lower_full = jnp.broadcast_to(lower_diag, diagonal.shape)
        upper_full = jnp.broadcast_to(upper_diag, diagonal.shape)
        return lax.linalg.tridiagonal_solve(lower_full, diagonal, upper_full, mode_row)
    solved = lax.map(solve_row, (stacked, eigen_y))
    spectrum_p = (solved[..., 0] + 1j * solved[..., 1]).transpose(2, 0, 1)
    potential = jnp.fft.irfft2(spectrum_p, s=(NY, NX), axes=(1, 2))
    slope = potential - jnp.concatenate([potential[:1], potential[:-1]], axis=0)
    level_ids = jnp.arange(NZ, dtype=jnp.int32)
    inside_solid = level_ids[:, None, None] < roof_level[None, :, :]
    w_new = jnp.where(inside_solid, 0.0, w_corr - slope).astype(w_corr.dtype)
    return (w_new, theta_new, facet_temp_new)
```

```python
import math

import jax
import jax.numpy as jnp
import ml_dtypes
import numpy as np
from jax import lax
from jax.experimental import pallas as pl
from jax.experimental.pallas import tpu as pltpu
from jax.sharding import PartitionSpec as P

F32 = jnp.float32
BF16 = jnp.bfloat16
HBM = pl.BlockSpec(memory_space=pl.ANY)
VMEM = pl.BlockSpec(memory_space=pltpu.VMEM)
SMEM = pl.BlockSpec(memory_space=pltpu.SMEM)
PARAMS = pltpu.CompilerParams(vmem_limit_bytes=58 * 2**20)


def two_halves(table):
    high = table.astype(ml_dtypes.bfloat16)
    low = (table - high.astype(np.float64)).astype(ml_dtypes.bfloat16)
    return (jnp.asarray(high), jnp.asarray(low))


def periodic_tables(size):
    half, quarter = size // 2, size // 4
    groups = (
        (np.arange(0, half + 1, 4), np.arange(4, half, 4), quarter),
        (np.arange(2, half, 4), np.arange(2, half, 4), quarter),
        (np.arange(1, half, 2), np.arange(1, half, 2), half),
    )
    tables, waves = [], []
    for cosines, sines, rows in groups:
        x = np.arange(rows)[:, None]
        norms = np.where((cosines == 0) | (cosines == half), np.sqrt(1.0 / size), np.sqrt(2.0 / size))
        tables.append(
            np.concatenate(
                [
                    norms * np.cos(2.0 * np.pi / size * (x * cosines % size)),
                    np.sqrt(2.0 / size) * np.sin(2.0 * np.pi / size * (x * sines % size)),
                ],
                axis=1,
            )
        )
        waves += [cosines, sines]
    waves = np.concatenate(waves)
    return (tables, 4.0 * np.sin(np.pi * waves / size) ** 2)


def cosine_table(size):
    modes = np.arange(size)[:, None]
    table = np.sqrt(2.0 / size) * np.cos(np.pi * modes * (2 * np.arange(size)[None, :] + 1) / (2 * size))
    table[0] = np.sqrt(1.0 / size)
    return (table, 4.0 * np.sin(np.pi * modes[:, 0] / (2 * size)) ** 2)


def level_tables(size):
    modes, levels = np.arange(size)[None, :], np.arange(size)[:, None]
    omegas = (
        np.pi * (2 * modes + 1) / (2 * size + 1),
        np.pi * (modes + 1) / (size + 1),
        np.pi * (modes + 1) / (size + 0.5),
    )
    vectors = (
        np.cos(omegas[0] * (levels + 0.5)),
        np.sin(omegas[1] * (levels + 1)),
        np.sin(omegas[2] * (levels + 1)),
    )
    vectors = [v / np.sqrt(np.sum(v * v, axis=0, keepdims=True)) for v in vectors]
    return (vectors, [4.0 * np.sin(o[0] / 2) ** 2 for o in omegas])


def split(value):
    high = value.astype(BF16)
    return (high, (value - high.astype(F32)).astype(BF16))


def dot3(left, right, dims=((1,), (0,))):
    one = lambda a, b: lax.dot_general(a, b, (dims, ((), ())), preferred_element_type=F32)
    return one(left[0], right[0]) + (one(left[1], right[0]) + one(left[0], right[1]))


def read_pair(refs):
    return (refs[0][...], refs[1][...])


def periodic_forward(value, tables):
    half, quarter = value.shape[1] // 2, value.shape[1] // 4
    even, odd = value[:, :half] + value[:, half:], value[:, :half] - value[:, half:]
    parts = (even[:, :quarter] + even[:, quarter:], even[:, :quarter] - even[:, quarter:], odd)
    return jnp.concatenate([dot3(split(p), read_pair(t)) for p, t in zip(parts, tables)], axis=1)


def periodic_inverse(value, tables):
    half, quarter = value.shape[1] // 2, value.shape[1] // 4
    parts = (value[:, :quarter], value[:, quarter:half], value[:, half:])
    four, two, odd = [dot3(split(p), read_pair(t), ((1,), (1,))) for p, t in zip(parts, tables)]
    even = jnp.concatenate([four + two, four - two], axis=1)
    return jnp.concatenate([even + odd, even - odd], axis=1)


def power(base, exponent):
    result = None
    while exponent:
        if exponent & 1:
            result = base if result is None else result * base
        base = base * base
        exponent >>= 1
    return result


def first_sweeps(load, root, top, above, store, levels):
    value = None
    for level in range(levels):
        value = load(level) if value is None else load(level) + root * value
        store[level] = value
    last = value
    value = top * value if above is None else top * value + above
    for level in range(levels - 1, -1, -1):
        value = root * (value - store[level])
    return (value, last)


def second_sweeps(load, start, root, top, above, store, levels, emit):
    value = start
    for level in range(levels):
        value = root * value if load is None else load(level) + root * value
        store[level] = value
    value = top * value if above is None else top * value + above
    for level in range(levels - 1, -1, -1):
        value = root * (value - store[level])
        emit(level, value)


def block_fluxes(ends, weights_ref, vectors_ref, levels, out_ref):
    blocks = len(ends)
    one = lambda dims, b: lax.dot_general(
        vectors_ref[...], b, (dims, ((), ())), precision=lax.Precision.HIGHEST, preferred_element_type=F32
    )
    upper = lower = None
    for block in range(blocks):
        even_next, odd_next = ends[(block + 1) % blocks]
        even, odd = ends[block]
        jump = one(((0,), (0,)), (even_next + odd_next) - (even - odd))
        up, low = weights_ref[0, block] * jump, weights_ref[1, block] * jump
        upper = up if upper is None else upper + up
        lower = low if lower is None else lower + low
    upper, lower = one(((1,), (0,)), upper), one(((1,), (0,)), lower)
    width = upper.shape[1]
    is_even = lax.broadcasted_iota(jnp.int32, (8, width), 0) % 2 == 0
    for level in range(levels):
        up, low = upper[level : level + 1], lower[level : level + 1]
        out_ref[level] = jnp.where(is_even, up - low, -up - low)


def fold_ends(total, out_ref, levels):
    is_even = lax.broadcasted_iota(jnp.int32, total.shape[1:], 0) % 2 == 0
    for level in range(levels):
        value = total[level]
        out_ref[0, level : level + 1] = jnp.sum(jnp.where(is_even, value, 0.0), axis=0, keepdims=True)
        out_ref[1, level : level + 1] = jnp.sum(jnp.where(is_even, 0.0, value), axis=0, keepdims=True)


def forward_kernel(
    levels, tile, div_ref, w_ref, t0h, t0l, t1h, t1l, t2h, t2l, ch, cl, root_ref, inv_ref, start_ref, top_ref,
    end_ref, field_ref, edge_ref, ends_ref, field, above, lowest, store, total,
):
    step = pl.program_id(0)
    tables = ((t0h, t0l), (t1h, t1l), (t2h, t2l))

    def transform(value):
        return dot3(read_pair((ch, cl)), split(periodic_forward(value, tables)))

    @pl.when(step == 0)
    def _():
        above[...] = jnp.zeros_like(above)
        total[...] = jnp.zeros_like(total)

    @pl.when(step < levels)
    def _():
        value = w_ref[0]
        field[levels - 1 - step] = transform(div_ref[0] + above[...] - value)
        above[...] = value

    @pl.when(step == levels - 1)
    def _():
        lowest[...] = transform(w_ref[0])

    @pl.when(step >= levels)
    def _():
        def rows_of(sub, _):
            here = pl.multiple_of(sub * 8, 8)
            rows = pl.ds(here, 8)
            full = pl.ds(pl.multiple_of((step - levels) * tile + here, 8), 8)
            root, top = root_ref[rows], top_ref[rows]
            load = lambda level: field[level, full]
            first, _ = first_sweeps(load, root, top, None, store, levels)
            edge_ref[0, rows] = first * inv_ref[rows] - lowest[full]
            weight = end_ref[rows, :1]

            def emit(level, value):
                total[level] += weight * value
                if level == levels - 1:
                    edge_ref[1, rows] = value

            second_sweeps(load, first * start_ref[rows], root, top, None, store, levels, emit)
            for level in range(levels):
                field_ref[level, rows] = load(level)
            return 0

        lax.fori_loop(0, tile // 8, rows_of, 0)

    @pl.when(step == pl.num_programs(0) - 1)
    def _():
        fold_ends(total, ends_ref, levels)


def edge_kernel(
    levels, edge_ref, ends_ref, weights_ref, vectors_ref, root_ref, inv_ref, start_ref, top_ref, end_ref, ch, cl,
    out_ref, pattern, store, fixed,
):
    block_fluxes(
        [(ends_ref[b, 0], ends_ref[b, 1]) for b in range(ends_ref.shape[0])], weights_ref, vectors_ref, levels, pattern
    )

    def rows_of(sub, _):
        rows = pl.ds(pl.multiple_of(sub * 8, 8), 8)
        root, top = root_ref[rows], top_ref[rows]
        first, last = first_sweeps(lambda level: pattern[level], root, top, None, store, levels)
        weight = end_ref[rows, :1]
        fixed[0, rows] = edge_ref[0, rows] - weight * (first * inv_ref[rows])
        last = last + power(root, levels) * (first * start_ref[rows])
        fixed[1, rows] = edge_ref[1, rows] - weight * (root * (top - 1.0) * last)
        return 0

    lax.fori_loop(0, edge_ref.shape[1] // 8, rows_of, 0)
    for side in range(2):
        value = dot3(split(fixed[side].T), read_pair((ch, cl)))
        out_ref[:, side] = value.reshape(out_ref.shape[0], out_ref.shape[2], out_ref.shape[3])


def join_kernel(
    levels, px_count, py_count, edge_ref, t0h, t0l, t1h, t1l, t2h, t2l, diag_ref, out_ref, modes
):
    tables = ((t0h, t0l), (t1h, t1l), (t2h, t2l))
    rows, width = edge_ref.shape[2:]
    for block in range(py_count):
        for side in range(2):
            whole = jnp.concatenate([edge_ref[i * py_count + block, side] for i in range(px_count)], axis=1)
            modes[block, side] = whole
    count = 2 * py_count * rows
    modes[...] = periodic_forward(modes[...].reshape(count, -1), tables).reshape(modes.shape)

    def rows_of(sub, _):
        here = pl.ds(pl.multiple_of(sub * 8, 8), 8)
        diag = diag_ref[here]
        near = 1.0 / diag
        far = near
        beta = 1.0 / (diag + 1.0)
        top = 1.0 / (diag - 1.0)
        for _ in range(1, levels):
            near = 1.0 / (diag - near)
            far = -far * near
            beta = 1.0 / (diag - beta)
            top = 1.0 / (diag - top)
        alpha = modes[0, 1, here]
        alphas, betas, heads, slopes = [alpha], [beta], [None], [None]
        for block in range(1, py_count - 1):
            scale = 1.0 / (1.0 - near * beta)
            head = (modes[block, 0, here] - near * alpha) * scale
            slope = far * scale
            alpha = modes[block, 1, here] - far * alpha + far * beta * head
            beta = near + far * beta * slope
            alphas.append(alpha)
            betas.append(beta)
            heads.append(head)
            slopes.append(slope)
        above = jnp.zeros_like(diag)
        first = (modes[py_count - 1, 0, here] - top * alpha) / (1.0 - top * beta)
        for block in range(py_count - 1, 0, -1):
            if block < py_count - 1:
                first = heads[block] - slopes[block] * above
            modes[block, 0, here] = alphas[block - 1] - betas[block - 1] * first
            modes[block, 1, here] = above
            above = first
        modes[0, 0, here] = jnp.zeros_like(diag)
        modes[0, 1, here] = above
        return 0

    lax.fori_loop(0, rows // 8, rows_of, 0)
    modes[...] = periodic_inverse(modes[...].reshape(count, -1), tables).reshape(modes.shape)
    for block in range(py_count):
        for side in range(2):
            for i in range(px_count):
                out_ref[i * py_count + block, side] = modes[block, side, :, i * width : (i + 1) * width]


def spread_kernel(levels, joined_ref, ch, cl, root_ref, start_ref, below_ref, top_ref, end_ref, out_ref, ends_ref, store, total):
    kx_width = joined_ref.shape[0] * joined_ref.shape[2]
    for side in range(2):
        value = joined_ref[:, side].reshape(kx_width, joined_ref.shape[3])
        out_ref[side] = dot3(read_pair((ch, cl)), split(value), ((1,), (1,)))
    total[...] = jnp.zeros_like(total)

    def rows_of(sub, _):
        rows = pl.ds(pl.multiple_of(sub * 8, 8), 8)
        root, top = root_ref[rows], top_ref[rows]
        below, above = out_ref[0, rows], out_ref[1, rows]
        start = start_ref[rows] * (power(root, levels) * above) - below_ref[rows] * below
        weight = end_ref[rows, :1]

        def emit(level, value):
            total[level] += weight * value

        second_sweeps(None, start, root, top, above, store, levels, emit)
        return 0

    lax.fori_loop(0, out_ref.shape[1] // 8, rows_of, 0)
    fold_ends(total, ends_ref, levels)


def inverse_kernel(
    levels, tile, place_ref, field_ref, sides_ref, ends_ref, more_ref, weights_ref, vectors_ref, root_ref, start_ref,
    below_ref, top_ref, end_ref, t0h, t0l, t1h, t1l, t2h, t2l, ch, cl, w_ref, roof_ref, out_ref, field, pattern, store,
):
    step = pl.program_id(0)
    tiles = pl.num_programs(0) - levels
    tables = ((t0h, t0l), (t1h, t1l), (t2h, t2l))

    @pl.when(step == 0)
    def _():
        ends = [
            (ends_ref[b, 0] + more_ref[b, 0], ends_ref[b, 1] + more_ref[b, 1]) for b in range(ends_ref.shape[0])
        ]
        block_fluxes(ends, weights_ref, vectors_ref, levels, pattern)

    @pl.when(step < tiles)
    def _():
        def rows_of(sub, _):
            here = pl.multiple_of(sub * 8, 8)
            rows = pl.ds(here, 8)
            full = pl.ds(pl.multiple_of(step * tile + here, 8), 8)
            root, top = root_ref[rows], top_ref[rows]
            below, above = sides_ref[0, rows], sides_ref[1, rows]
            weight = end_ref[rows, :1]
            load = lambda level: field_ref[level, rows] - weight * pattern[level]
            first, _ = first_sweeps(load, root, top, above, store, levels)
            start = start_ref[rows] * first - below_ref[rows] * below
            held = []

            def emit(level, value):
                if held:
                    field[level + 1, full] = held.pop() - value
                held.append(value)

            second_sweeps(load, start, root, top, above, store, levels, emit)
            field[0, full] = jnp.where(place_ref[0] == 0, 0.0, held[0] - below)
            return 0

        lax.fori_loop(0, tile // 8, rows_of, 0)

    @pl.when(step >= tiles)
    def _():
        level = step - tiles
        rows_y = dot3(read_pair((ch, cl)), split(field[level]))
        slope = periodic_inverse(rows_y, tables)
        solid = place_ref[0] * levels + level < roof_ref[...]
        out_ref[0] = jnp.where(solid, 0.0, w_ref[0] - slope)


def tile_at(cell, width, tall):
    row, column = cell // width, cell % width
    return (pl.ds(pl.multiple_of(row // tall * tall, tall), tall), pl.ds(pl.multiple_of(column // 128 * 128, 128), 128))


def gather_kernel(ids_ref, w_ref, temp_ref, w_out, temp_out):
    width = w_ref.shape[1]
    group = 8

    def pick(i, _):
        for lane in range(group):
            facet = i * group + lane
            cell = jnp.maximum(ids_ref[facet], 0)
            w_out[facet] = w_ref[tile_at(cell, width, 8)]
            temp_out[facet] = temp_ref[tile_at(cell, width, 16)]
        return 0

    lax.fori_loop(0, ids_ref.shape[0] // group, pick, 0)


def scatter_kernel(ids_ref, w_new_ref, temp_new_ref, w_hbm, temp_hbm, w_out, temp_out, sems):
    copies = [
        pltpu.make_async_copy(w_hbm, w_out, sems.at[0]),
        pltpu.make_async_copy(temp_hbm, temp_out, sems.at[1]),
    ]
    for copy in copies:
        copy.start()
    width = w_out.shape[1]

    def put(facet, new_ref, out, tall):
        cell = ids_ref[facet]
        safe = jnp.maximum(cell, 0)
        here = tile_at(safe, width, tall)
        row = jnp.where(cell < 0, -1, safe // width % tall)
        hit = lax.broadcasted_iota(jnp.int32, (tall, 128), 0) == row
        hit = hit & (lax.broadcasted_iota(jnp.int32, (tall, 128), 1) == safe % 128)
        out[here] = jnp.where(hit, new_ref[facet], out[here].astype(F32)).astype(out.dtype)
        return 0

    copies[0].wait()
    lax.fori_loop(0, ids_ref.shape[0], lambda facet, _: put(facet, w_new_ref, w_out, 8), 0)
    copies[1].wait()
    lax.fori_loop(0, ids_ref.shape[0], lambda facet, _: put(facet, temp_new_ref, temp_out, 16), 0)


def near_walls(w_rows, temp_rows, ids, facet_temp, net_radiation, heat_capacity, drag_coef, heat_coef):
    count = ids.shape[0]
    near = pl.pallas_call(
        gather_kernel,
        out_shape=(jax.ShapeDtypeStruct((count, 8, 128), F32), jax.ShapeDtypeStruct((count, 16, 128), BF16)),
        in_specs=[SMEM, VMEM, VMEM],
        out_specs=(VMEM, VMEM),
        compiler_params=PARAMS,
        name="facet_gather",
    )(ids, w_rows, temp_rows)

    def own_cell(tiles):
        hit = lax.broadcasted_iota(jnp.int32, tiles.shape, 1) == (ids // w_rows.shape[1] % tiles.shape[1])[:, None, None]
        hit = hit & (lax.broadcasted_iota(jnp.int32, tiles.shape, 2) == (ids % 128)[:, None, None])
        hit = hit & (ids >= 0)[:, None, None]
        return jnp.sum(jnp.where(hit, tiles.astype(F32), 0.0), axis=(1, 2))

    own = jnp.stack([own_cell(tiles) for tiles in near])
    arrived = lax.all_to_all(own, ("px", "py"), split_axis=1, concat_axis=1, tiled=True)
    w_cell, temp_cell = arrived[0], arrived[1]
    speeds = jnp.sqrt(w_cell * w_cell + 0.25)
    stress = drag_coef * speeds * w_cell
    heat_flux = heat_coef * speeds * (facet_temp - temp_cell)
    new_temp = facet_temp + (net_radiation - heat_flux - 0.5 * facet_temp) / heat_capacity
    returned = lax.all_to_all(
        jnp.stack([stress, heat_flux]), ("px", "py"), split_axis=1, concat_axis=1, tiled=True
    )
    same = ids[:, None] == ids[None, :]
    sums = [jnp.sum(jnp.where(same, returned[i][None, :], 0.0), axis=1) for i in range(2)]
    w_corr, theta = pl.pallas_call(
        scatter_kernel,
        out_shape=(jax.ShapeDtypeStruct(w_rows.shape, F32), jax.ShapeDtypeStruct(temp_rows.shape, BF16)),
        in_specs=[SMEM, SMEM, SMEM, HBM, HBM],
        out_specs=(VMEM, VMEM),
        scratch_shapes=[pltpu.SemaphoreType.DMA((2,))],
        compiler_params=PARAMS,
        name="facet_scatter",
    )(ids, own[0] - sums[0], own[1] + sums[1], w_rows, temp_rows)
    return (w_corr, theta, new_temp)


def body(
    horiz_div,
    w_star,
    air_temp,
    roof_level,
    facet_cells,
    facet_temp,
    net_radiation,
    heat_capacity,
    drag_coef,
    heat_coef,
):
    levels, rows, width = w_star.shape
    px_count, py_count = lax.axis_size("px"), lax.axis_size("py")
    devices = px_count * py_count
    place_x, place_y = lax.axis_index("px"), lax.axis_index("py")
    own_kx = width // devices
    y_cells = rows * px_count

    w_corr, theta_new, new_temp = near_walls(
        w_star.reshape(levels * rows, width),
        air_temp.reshape(levels * rows, width),
        facet_cells[0],
        facet_temp[0],
        net_radiation[0],
        heat_capacity[0],
        drag_coef[0],
        heat_coef[0],
    )
    w_corr = w_corr.reshape(w_star.shape)
    theta_new = theta_new.reshape(air_temp.shape)

    x_parts, sin_x = periodic_tables(width)
    y_parts, sin_y = periodic_tables(y_cells)
    cosines, sin_block = cosine_table(rows)
    x_tables = [t for part in x_parts for t in two_halves(part)]
    y_tables = [t for part in y_parts for t in two_halves(part)]
    to_modes, to_rows = two_halves(cosines), two_halves(np.ascontiguousarray(cosines.T))
    sin_x = jnp.asarray(sin_x, F32)

    sine = jnp.asarray(sin_block, F32)[:, None] + sin_x[None, :]
    half_root = 0.5 * jnp.sqrt(sine)
    root = jnp.sqrt(1.0 + half_root * half_root) - half_root
    root = root * root
    is_first, is_last = place_y == 0, place_y == py_count - 1
    top = jnp.where(is_last, root / (1.0 + root), 0.0)
    kappa = jnp.zeros_like(root)
    for _ in range(levels):
        kappa = root * root * (1.0 + kappa)
    decay = power(root, levels)
    bottom = jnp.where(is_first, 1.0 - 1.0 / root, 1.0)
    inv = 1.0 / (1.0 + bottom * (kappa - top * decay * decay))
    start = bottom * inv
    from_below = inv / root
    end = np.where(np.arange(rows) == 0, np.sqrt(1.0 / rows), cosines[:, 0])
    end = jnp.asarray(np.repeat(end[:, None], 128, axis=1), F32)

    vectors, sin_z = level_tables(levels)
    pick = lambda three: jnp.where(is_first, three[0], jnp.where(is_last, three[2], three[1])).astype(F32)
    vectors, sin_z = pick(vectors), pick(sin_z)
    sine_z = sin_z[:, None] + sin_x[None, :]
    size_z = jnp.sqrt(sine_z)
    half_z = 0.5 * size_z
    cosh_z = jnp.sqrt(1.0 + half_z * half_z)
    half_step = cosh_z - half_z
    across = jnp.exp(2.0 * rows * jnp.log(half_step))
    scale = 1.0 / ((1.0 - across * across) * size_z)
    same_end = -half_step * (1.0 + across * across / (half_step * half_step)) * scale
    far_end = -2.0 * across * cosh_z * scale
    turns = np.arange(px_count)
    circulant = jnp.stack(
        [1.0 / (1.0 - 2.0 * same_end + 2.0 * math.cos(2.0 * math.pi * s / px_count) * far_end) for s in turns]
    )
    phase_of = jnp.asarray(np.cos(2.0 * np.pi * turns[:, None] * turns[None, :] / px_count) / px_count, F32)
    offsets = jnp.stack([(place_x - turns) % px_count, (place_x - 1 - turns) % px_count])
    phases = phase_of[offsets]
    weights = jnp.sum(phases[:, :, :, None, None] * circulant[None, None], axis=2)

    mine = place_x * py_count + place_y
    own_sin = lax.dynamic_slice_in_dim(sin_x, mine * own_kx, own_kx)
    diag = -2.0 - own_sin[:, None] - jnp.asarray(sin_y, F32)[None, :]

    tile = math.gcd(rows, 32)
    tiles = rows // tile
    flat = lambda i: pl.BlockSpec((tile, width), i)
    fixed = lambda a: pl.BlockSpec(a.shape, lambda i: (0,) * a.ndim)
    late = lambda i: (jnp.maximum(i - levels, 0), 0)
    down = lambda i: (jnp.maximum(levels - 1 - i, 0), 0, 0)
    slab = pl.BlockSpec((1, rows, width), down)
    end_late = pl.BlockSpec((tile, 128), late)
    ends_shape = jax.ShapeDtypeStruct((2, levels, width), F32)
    field, edges, ends = pl.pallas_call(
        lambda *refs: forward_kernel(levels, tile, *refs),
        out_shape=(
            jax.ShapeDtypeStruct(w_star.shape, F32),
            jax.ShapeDtypeStruct((2, rows, width), F32),
            ends_shape,
        ),
        grid=(levels + tiles,),
        in_specs=[slab, slab] + [fixed(t) for t in (*x_tables, *to_modes)] + [flat(late)] * 4 + [end_late],
        out_specs=(
            pl.BlockSpec((levels, tile, width), lambda i: (0, *late(i))),
            pl.BlockSpec((2, tile, width), lambda i: (0, *late(i))),
            fixed(ends_shape),
        ),
        scratch_shapes=[
            pltpu.VMEM(w_star.shape, F32),
            pltpu.VMEM((rows, width), F32),
            pltpu.VMEM((rows, width), F32),
            pltpu.VMEM((levels, 8, width), F32),
            pltpu.VMEM((levels, 8, width), F32),
        ],
        compiler_params=PARAMS,
        name="forward",
    )(horiz_div, w_corr, *x_tables, *to_modes, root, inv, start, top, end)

    all_ends = lax.all_gather(ends, "px")
    packed = jax.ShapeDtypeStruct((devices, 2, own_kx, rows), F32)
    working = [pltpu.VMEM((levels, 8, width), F32)] * 2
    edges = pl.pallas_call(
        lambda *refs: edge_kernel(levels, *refs),
        out_shape=packed,
        in_specs=[VMEM] * 11,
        out_specs=VMEM,
        scratch_shapes=working + [pltpu.VMEM((2, rows, width), F32)],
        compiler_params=PARAMS,
        name="edges",
    )(edges, all_ends, weights, vectors, root, inv, start, top, end, *to_modes)
    edges = lax.all_to_all(edges, ("px", "py"), split_axis=0, concat_axis=0, tiled=True)
    joined = pl.pallas_call(
        lambda *refs: join_kernel(levels, px_count, py_count, *refs),
        out_shape=packed,
        in_specs=[VMEM] * 8,
        out_specs=VMEM,
        scratch_shapes=[pltpu.VMEM((py_count, 2, own_kx, y_cells), F32)],
        compiler_params=PARAMS,
        name="join",
    )(edges, *y_tables, diag)
    joined = lax.all_to_all(joined, ("px", "py"), split_axis=0, concat_axis=0, tiled=True)
    sides, more = pl.pallas_call(
        lambda *refs: spread_kernel(levels, *refs),
        out_shape=(jax.ShapeDtypeStruct((2, rows, width), F32), ends_shape),
        in_specs=[VMEM] * 8,
        out_specs=(VMEM, VMEM),
        scratch_shapes=working,
        compiler_params=PARAMS,
        name="spread",
    )(joined, *to_modes, root, start, from_below, top, end)
    more = lax.all_gather(more, "px")

    early = lambda i: (jnp.minimum(i, tiles - 1), 0)
    up = lambda i: (jnp.maximum(i - tiles, 0), 0, 0)
    slab = pl.BlockSpec((1, rows, width), up)
    w_new = pl.pallas_call(
        lambda *refs: inverse_kernel(levels, tile, *refs),
        out_shape=jax.ShapeDtypeStruct(w_star.shape, F32),
        grid=(tiles + levels,),
        in_specs=[
            SMEM,
            pl.BlockSpec((levels, tile, width), lambda i: (0, *early(i))),
            pl.BlockSpec((2, tile, width), lambda i: (0, *early(i))),
        ]
        + [fixed(a) for a in (all_ends, more, weights, vectors)]
        + [flat(early)] * 4
        + [pl.BlockSpec((tile, 128), early)]
        + [fixed(t) for t in (*x_tables, *to_rows)]
        + [slab, fixed(roof_level)],
        out_specs=slab,
        scratch_shapes=[pltpu.VMEM(w_star.shape, F32)] + working,
        compiler_params=PARAMS,
        name="inverse",
    )(
        place_y.astype(jnp.int32).reshape(1),
        field,
        sides,
        all_ends,
        more,
        weights,
        vectors,
        root,
        start,
        from_below,
        top,
        end,
        *x_tables,
        *to_rows,
        w_corr,
        roof_level,
    )
    return (w_new, theta_new, new_temp[None])


def solution(mesh):
    placed = (
        P("py", "px", None),
        P("py", "px", None),
        P("py", "px", None),
        P("px", None),
        P(("px", "py"), None),
        P(("px", "py"), None),
        P(("px", "py"), None),
        P(("px", "py"), None),
        P(("px", "py"), None),
        P(("px", "py"), None),
    )
    return jax.shard_map(
        body,
        mesh=mesh,
        in_specs=placed,
        out_specs=(P("py", "px", None), P("py", "px", None), P(("px", "py"), None)),
        check_vma=False,
    )
```

```python
import math

import jax
import jax.numpy as jnp
import ml_dtypes
import numpy as np
from jax import lax
from jax.experimental import pallas as pl
from jax.experimental.pallas import tpu as pltpu
from jax.sharding import PartitionSpec as P

F32 = jnp.float32
BF16 = jnp.bfloat16
HBM = pl.BlockSpec(memory_space=pl.ANY)
VMEM = pl.BlockSpec(memory_space=pltpu.VMEM)
SMEM = pl.BlockSpec(memory_space=pltpu.SMEM)
PARAMS = pltpu.CompilerParams(vmem_limit_bytes=58 * 2**20)


def two_halves(table):
    high = table.astype(ml_dtypes.bfloat16)
    low = (table - high.astype(np.float64)).astype(ml_dtypes.bfloat16)
    return (jnp.asarray(high), jnp.asarray(low))


def periodic_tables(size):
    half, quarter = size // 2, size // 4
    groups = (
        (np.arange(0, half + 1, 4), np.arange(4, half, 4), quarter),
        (np.arange(2, half, 4), np.arange(2, half, 4), quarter),
        (np.arange(1, half, 2), np.arange(1, half, 2), half),
    )
    tables, waves = [], []
    for cosines, sines, rows in groups:
        x = np.arange(rows)[:, None]
        norms = np.where((cosines == 0) | (cosines == half), np.sqrt(1.0 / size), np.sqrt(2.0 / size))
        tables.append(
            np.concatenate(
                [
                    norms * np.cos(2.0 * np.pi / size * (x * cosines % size)),
                    np.sqrt(2.0 / size) * np.sin(2.0 * np.pi / size * (x * sines % size)),
                ],
                axis=1,
            )
        )
        waves += [cosines, sines]
    waves = np.concatenate(waves)
    return (tables, 4.0 * np.sin(np.pi * waves / size) ** 2)


def cosine_table(size):
    modes = np.arange(size)[:, None]
    table = np.sqrt(2.0 / size) * np.cos(np.pi * modes * (2 * np.arange(size)[None, :] + 1) / (2 * size))
    table[0] = np.sqrt(1.0 / size)
    return (table, 4.0 * np.sin(np.pi * modes[:, 0] / (2 * size)) ** 2)


def level_tables(size):
    modes, levels = np.arange(size)[None, :], np.arange(size)[:, None]
    omegas = (
        np.pi * (2 * modes + 1) / (2 * size + 1),
        np.pi * (modes + 1) / (size + 1),
        np.pi * (modes + 1) / (size + 0.5),
    )
    vectors = (
        np.cos(omegas[0] * (levels + 0.5)),
        np.sin(omegas[1] * (levels + 1)),
        np.sin(omegas[2] * (levels + 1)),
    )
    vectors = [v / np.sqrt(np.sum(v * v, axis=0, keepdims=True)) for v in vectors]
    return (vectors, [4.0 * np.sin(o[0] / 2) ** 2 for o in omegas])


def split(value):
    high = value.astype(BF16)
    return (high, (value - high.astype(F32)).astype(BF16))


def dot3(left, right, dims=((1,), (0,))):
    one = lambda a, b: lax.dot_general(a, b, (dims, ((), ())), preferred_element_type=F32)
    return one(left[0], right[0]) + (one(left[1], right[0]) + one(left[0], right[1]))


def read_pair(refs):
    return (refs[0][...], refs[1][...])


def periodic_forward(value, tables):
    half, quarter = value.shape[1] // 2, value.shape[1] // 4
    even, odd = value[:, :half] + value[:, half:], value[:, :half] - value[:, half:]
    parts = (even[:, :quarter] + even[:, quarter:], even[:, :quarter] - even[:, quarter:], odd)
    return jnp.concatenate([dot3(split(p), read_pair(t)) for p, t in zip(parts, tables)], axis=1)


def periodic_inverse(value, tables):
    half, quarter = value.shape[1] // 2, value.shape[1] // 4
    parts = (value[:, :quarter], value[:, quarter:half], value[:, half:])
    four, two, odd = [dot3(split(p), read_pair(t), ((1,), (1,))) for p, t in zip(parts, tables)]
    even = jnp.concatenate([four + two, four - two], axis=1)
    return jnp.concatenate([even + odd, even - odd], axis=1)


def power(base, exponent):
    result = None
    while exponent:
        if exponent & 1:
            result = base if result is None else result * base
        base = base * base
        exponent >>= 1
    return result


def first_sweeps(load, root, top, above, store, levels):
    value = None
    for level in range(levels):
        value = load(level) if value is None else load(level) + root * value
        store[level] = value
    last = value
    value = top * value if above is None else top * value + above
    for level in range(levels - 1, -1, -1):
        value = root * (value - store[level])
    return (value, last)


def second_sweeps(load, start, root, top, above, store, levels, emit):
    value = start
    for level in range(levels):
        value = root * value if load is None else load(level) + root * value
        store[level] = value
    value = top * value if above is None else top * value + above
    for level in range(levels - 1, -1, -1):
        value = root * (value - store[level])
        emit(level, value)


def block_fluxes(ends, weights_ref, vectors_ref, levels, out_ref):
    blocks = len(ends)
    one = lambda dims, b: lax.dot_general(
        vectors_ref[...], b, (dims, ((), ())), precision=lax.Precision.HIGHEST, preferred_element_type=F32
    )
    upper = lower = None
    for block in range(blocks):
        even_next, odd_next = ends[(block + 1) % blocks]
        even, odd = ends[block]
        jump = one(((0,), (0,)), (even_next + odd_next) - (even - odd))
        up, low = weights_ref[0, block] * jump, weights_ref[1, block] * jump
        upper = up if upper is None else upper + up
        lower = low if lower is None else lower + low
    upper, lower = one(((1,), (0,)), upper), one(((1,), (0,)), lower)
    width = upper.shape[1]
    is_even = lax.broadcasted_iota(jnp.int32, (8, width), 0) % 2 == 0
    for level in range(levels):
        up, low = upper[level : level + 1], lower[level : level + 1]
        out_ref[level] = jnp.where(is_even, up - low, -up - low)


def fold_ends(total, out_ref, levels):
    is_even = lax.broadcasted_iota(jnp.int32, total.shape[1:], 0) % 2 == 0
    for level in range(levels):
        value = total[level]
        out_ref[0, level : level + 1] = jnp.sum(jnp.where(is_even, value, 0.0), axis=0, keepdims=True)
        out_ref[1, level : level + 1] = jnp.sum(jnp.where(is_even, 0.0, value), axis=0, keepdims=True)


def forward_kernel(
    levels, tile, ids_ref, w_new_ref, w_hbm, div_ref, t0h, t0l, t1h, t1l, t2h, t2l, ch, cl, root_ref, inv_ref,
    start_ref, top_ref, end_ref, field_ref, edge_ref, ends_ref, corr_hbm, field, w_rows, above, lowest, store, total,
    sems,
):
    step = pl.program_id(0)
    tables = ((t0h, t0l), (t1h, t1l), (t2h, t2l))

    def transform(value):
        return dot3(read_pair((ch, cl)), split(periodic_forward(value, tables)))

    @pl.when(step == 0)
    def _():
        load = pltpu.make_async_copy(w_hbm, w_rows, sems.at[0])
        load.start()
        above[...] = jnp.zeros_like(above)
        total[...] = jnp.zeros_like(total)
        load.wait()
        put_cells(ids_ref, w_new_ref, w_rows)
        pltpu.make_async_copy(w_rows, corr_hbm, sems.at[1]).start()

    row_count = above.shape[0]

    @pl.when(step < levels)
    def _():
        value = w_rows[pl.ds(pl.multiple_of((levels - 1 - step) * row_count, row_count), row_count)]
        field[levels - 1 - step] = transform(div_ref[0] + above[...] - value)
        above[...] = value

    @pl.when(step == levels - 1)
    def _():
        lowest[...] = transform(w_rows[:row_count])

    @pl.when(step >= levels)
    def _():
        def rows_of(sub, _):
            here = pl.multiple_of(sub * 8, 8)
            rows = pl.ds(here, 8)
            full = pl.ds(pl.multiple_of((step - levels) * tile + here, 8), 8)
            root, top = root_ref[rows], top_ref[rows]
            load = lambda level: field[level, full]
            first, _ = first_sweeps(load, root, top, None, store, levels)
            edge_ref[0, rows] = first * inv_ref[rows] - lowest[full]
            weight = end_ref[rows, :1]

            def emit(level, value):
                total[level] += weight * value
                if level == levels - 1:
                    edge_ref[1, rows] = value

            second_sweeps(load, first * start_ref[rows], root, top, None, store, levels, emit)
            for level in range(levels):
                field_ref[level, rows] = load(level)
            return 0

        lax.fori_loop(0, tile // 8, rows_of, 0)

    @pl.when(step == pl.num_programs(0) - 1)
    def _():
        fold_ends(total, ends_ref, levels)
        pltpu.make_async_copy(w_rows, corr_hbm, sems.at[1]).wait()


def edge_kernel(
    levels, edge_ref, ends_ref, weights_ref, vectors_ref, root_ref, inv_ref, start_ref, top_ref, end_ref, ch, cl,
    out_ref, pattern, store, fixed,
):
    block_fluxes(
        [(ends_ref[b, 0], ends_ref[b, 1]) for b in range(ends_ref.shape[0])], weights_ref, vectors_ref, levels, pattern
    )

    def rows_of(sub, _):
        rows = pl.ds(pl.multiple_of(sub * 8, 8), 8)
        root, top = root_ref[rows], top_ref[rows]
        first, last = first_sweeps(lambda level: pattern[level], root, top, None, store, levels)
        weight = end_ref[rows, :1]
        fixed[0, rows] = edge_ref[0, rows] - weight * (first * inv_ref[rows])
        last = last + power(root, levels) * (first * start_ref[rows])
        fixed[1, rows] = edge_ref[1, rows] - weight * (root * (top - 1.0) * last)
        return 0

    lax.fori_loop(0, edge_ref.shape[1] // 8, rows_of, 0)
    for side in range(2):
        value = dot3(split(fixed[side].T), read_pair((ch, cl)))
        out_ref[:, side] = value.reshape(out_ref.shape[0], out_ref.shape[2], out_ref.shape[3])


def join_kernel(
    levels, px_count, py_count, edge_ref, t0h, t0l, t1h, t1l, t2h, t2l, diag_ref, out_ref, modes
):
    tables = ((t0h, t0l), (t1h, t1l), (t2h, t2l))
    rows, width = edge_ref.shape[2:]
    for block in range(py_count):
        for side in range(2):
            whole = jnp.concatenate([edge_ref[i * py_count + block, side] for i in range(px_count)], axis=1)
            modes[block, side] = whole
    count = 2 * py_count * rows
    modes[...] = periodic_forward(modes[...].reshape(count, -1), tables).reshape(modes.shape)

    def rows_of(sub, _):
        here = pl.ds(pl.multiple_of(sub * 8, 8), 8)
        diag = diag_ref[here]
        near = 1.0 / diag
        far = near
        beta = 1.0 / (diag + 1.0)
        top = 1.0 / (diag - 1.0)
        for _ in range(1, levels):
            near = 1.0 / (diag - near)
            far = -far * near
            beta = 1.0 / (diag - beta)
            top = 1.0 / (diag - top)
        alpha = modes[0, 1, here]
        alphas, betas, heads, slopes = [alpha], [beta], [None], [None]
        for block in range(1, py_count - 1):
            scale = 1.0 / (1.0 - near * beta)
            head = (modes[block, 0, here] - near * alpha) * scale
            slope = far * scale
            alpha = modes[block, 1, here] - far * alpha + far * beta * head
            beta = near + far * beta * slope
            alphas.append(alpha)
            betas.append(beta)
            heads.append(head)
            slopes.append(slope)
        above = jnp.zeros_like(diag)
        first = (modes[py_count - 1, 0, here] - top * alpha) / (1.0 - top * beta)
        for block in range(py_count - 1, 0, -1):
            if block < py_count - 1:
                first = heads[block] - slopes[block] * above
            modes[block, 0, here] = alphas[block - 1] - betas[block - 1] * first
            modes[block, 1, here] = above
            above = first
        modes[0, 0, here] = jnp.zeros_like(diag)
        modes[0, 1, here] = above
        return 0

    lax.fori_loop(0, rows // 8, rows_of, 0)
    modes[...] = periodic_inverse(modes[...].reshape(count, -1), tables).reshape(modes.shape)
    for block in range(py_count):
        for side in range(2):
            for i in range(px_count):
                out_ref[i * py_count + block, side] = modes[block, side, :, i * width : (i + 1) * width]


def spread_kernel(levels, joined_ref, ch, cl, root_ref, start_ref, below_ref, top_ref, end_ref, out_ref, ends_ref, store, total):
    kx_width = joined_ref.shape[0] * joined_ref.shape[2]
    for side in range(2):
        value = joined_ref[:, side].reshape(kx_width, joined_ref.shape[3])
        out_ref[side] = dot3(read_pair((ch, cl)), split(value), ((1,), (1,)))
    total[...] = jnp.zeros_like(total)

    def rows_of(sub, _):
        rows = pl.ds(pl.multiple_of(sub * 8, 8), 8)
        root, top = root_ref[rows], top_ref[rows]
        below, above = out_ref[0, rows], out_ref[1, rows]
        start = start_ref[rows] * (power(root, levels) * above) - below_ref[rows] * below
        weight = end_ref[rows, :1]

        def emit(level, value):
            total[level] += weight * value

        second_sweeps(None, start, root, top, above, store, levels, emit)
        return 0

    lax.fori_loop(0, out_ref.shape[1] // 8, rows_of, 0)
    fold_ends(total, ends_ref, levels)


def inverse_kernel(
    levels, tile, place_ref, field_ref, sides_ref, ends_ref, more_ref, weights_ref, vectors_ref, root_ref, start_ref,
    below_ref, top_ref, end_ref, t0h, t0l, t1h, t1l, t2h, t2l, ch, cl, w_ref, roof_ref, out_ref, field, pattern, store,
):
    step = pl.program_id(0)
    tiles = pl.num_programs(0) - levels
    tables = ((t0h, t0l), (t1h, t1l), (t2h, t2l))

    @pl.when(step == 0)
    def _():
        ends = [
            (ends_ref[b, 0] + more_ref[b, 0], ends_ref[b, 1] + more_ref[b, 1]) for b in range(ends_ref.shape[0])
        ]
        block_fluxes(ends, weights_ref, vectors_ref, levels, pattern)

    @pl.when(step < tiles)
    def _():
        def rows_of(sub, _):
            here = pl.multiple_of(sub * 8, 8)
            rows = pl.ds(here, 8)
            full = pl.ds(pl.multiple_of(step * tile + here, 8), 8)
            root, top = root_ref[rows], top_ref[rows]
            below, above = sides_ref[0, rows], sides_ref[1, rows]
            weight = end_ref[rows, :1]
            load = lambda level: field_ref[level, rows] - weight * pattern[level]
            first, _ = first_sweeps(load, root, top, above, store, levels)
            start = start_ref[rows] * first - below_ref[rows] * below
            held = []

            def emit(level, value):
                if held:
                    field[level + 1, full] = held.pop() - value
                held.append(value)

            second_sweeps(load, start, root, top, above, store, levels, emit)
            field[0, full] = jnp.where(place_ref[0] == 0, 0.0, held[0] - below)
            return 0

        lax.fori_loop(0, tile // 8, rows_of, 0)

    @pl.when(step >= tiles)
    def _():
        level = step - tiles
        rows_y = dot3(read_pair((ch, cl)), split(field[level]))
        slope = periodic_inverse(rows_y, tables)
        solid = place_ref[0] * levels + level < roof_ref[...]
        out_ref[0] = jnp.where(solid, 0.0, w_ref[0] - slope)


def divide(value, size):
    if size & (size - 1):
        return lax.div(value, size)
    return lax.shift_right_logical(value, size.bit_length() - 1)


def remainder(value, size):
    return lax.rem(value, size) if size & (size - 1) else value & (size - 1)


def tile_at(cell, width, tall):
    row, column = divide(cell, width), remainder(cell, width)
    return (
        pl.ds(pl.multiple_of(divide(row, tall) * tall, tall), tall),
        pl.ds(pl.multiple_of(divide(column, 128) * 128, 128), 128),
    )


def gather_kernel(ids_ref, w_hbm, temp_hbm, w_out, temp_out, w_ref, temp_ref, sems):
    copies = [
        pltpu.make_async_copy(w_hbm, w_ref, sems.at[0]),
        pltpu.make_async_copy(temp_hbm, temp_ref, sems.at[1]),
    ]
    for copy in copies:
        copy.start()
    width = w_ref.shape[1]
    sublane = lax.broadcasted_iota(jnp.int32, (8, 128), 0)

    def pick(i, ref, out):
        rows = None
        for lane in range(8):
            cell = jnp.maximum(ids_ref[i * 8 + lane], 0)
            row = divide(cell, width)
            if ref.dtype == F32:
                tile = ref[tile_at(cell, width, 8)]
            else:
                both = ref[tile_at(cell, width, 16)].astype(F32)
                tile = jnp.where(remainder(row, 16) < 8, both[:8], both[8:])
            tile = pltpu.roll(tile, remainder(lane + 8 - remainder(row, 8), 8), 0)
            rows = tile if rows is None else jnp.where(sublane == lane, tile, rows)
        out[pl.ds(pl.multiple_of(i * 8, 8), 8)] = rows
        return 0

    groups = ids_ref.shape[0] // 8
    copies[0].wait()
    lax.fori_loop(0, groups, lambda i, _: pick(i, w_ref, w_out), 0)
    copies[1].wait()
    lax.fori_loop(0, groups, lambda i, _: pick(i, temp_ref, temp_out), 0)


def put_cells(ids_ref, new_ref, out):
    width = out.shape[1]
    sublane = lax.broadcasted_iota(jnp.int32, (8, 128), 0)
    lane = lax.broadcasted_iota(jnp.int32, (8, 128), 1)
    position = sublane * 128 + lane

    def put(i, _):
        for k in range(8):
            facet = i * 8 + k
            cell = ids_ref[facet]
            safe = jnp.maximum(cell, 0)
            at = remainder(divide(safe, width), 8) * 128 + remainder(safe, 128)
            hit = position == jnp.where(cell < 0, -1, at)
            pltpu.store(out.at[tile_at(safe, width, 8)], jnp.full((8, 128), new_ref[facet]), mask=hit)
        return 0

    lax.fori_loop(0, ids_ref.shape[0] // 8, put, 0)


def theta_kernel(ids_ref, new_ref, temp_ref, out_ref, wide):
    rows = temp_ref.shape[0]
    chunk = math.gcd(rows, 64)

    def widen(i, _):
        here = pl.ds(pl.multiple_of(i * chunk, chunk), chunk)
        wide[here] = temp_ref[here].astype(F32)
        return 0

    def narrow(i, _):
        here = pl.ds(pl.multiple_of(i * chunk, chunk), chunk)
        out_ref[here] = wide[here].astype(BF16)
        return 0

    lax.fori_loop(0, rows // chunk, widen, 0)
    put_cells(ids_ref, new_ref, wide)
    lax.fori_loop(0, rows // chunk, narrow, 0)


def near_walls(w_rows, temp_rows, ids, facet_temp, net_radiation, heat_capacity, drag_coef, heat_coef):
    count = ids.shape[0]
    shape = jax.ShapeDtypeStruct((count, 128), F32)
    near = pl.pallas_call(
        gather_kernel,
        out_shape=(shape, shape),
        in_specs=[SMEM, HBM, HBM],
        out_specs=(VMEM, VMEM),
        scratch_shapes=[
            pltpu.VMEM(w_rows.shape, F32),
            pltpu.VMEM(temp_rows.shape, BF16),
            pltpu.SemaphoreType.DMA((2,)),
        ],
        compiler_params=PARAMS,
        name="facet_gather",
    )(ids, w_rows, temp_rows)
    lane = jnp.where(ids < 0, -1, ids % 128)
    hit = lax.broadcasted_iota(jnp.int32, (count, 128), 1) == lane[:, None]
    own = jnp.stack([jnp.sum(jnp.where(hit, rows, 0.0), axis=1) for rows in near])
    arrived = lax.all_to_all(own, ("px", "py"), split_axis=1, concat_axis=1, tiled=True)
    w_cell, temp_cell = arrived[0], arrived[1]
    speeds = jnp.sqrt(w_cell * w_cell + 0.25)
    stress = drag_coef * speeds * w_cell
    heat_flux = heat_coef * speeds * (facet_temp - temp_cell)
    new_temp = facet_temp + (net_radiation - heat_flux - 0.5 * facet_temp) / heat_capacity
    returned = lax.all_to_all(
        jnp.stack([stress, heat_flux]), ("px", "py"), split_axis=1, concat_axis=1, tiled=True
    )
    same = ids[:, None] == ids[None, :]
    sums = [jnp.sum(jnp.where(same, returned[i][None, :], 0.0), axis=1) for i in range(2)]
    return (own[0] - sums[0], own[1] + sums[1], new_temp)


def body(
    horiz_div,
    w_star,
    air_temp,
    roof_level,
    facet_cells,
    facet_temp,
    net_radiation,
    heat_capacity,
    drag_coef,
    heat_coef,
):
    levels, rows, width = w_star.shape
    px_count, py_count = lax.axis_size("px"), lax.axis_size("py")
    devices = px_count * py_count
    place_x, place_y = lax.axis_index("px"), lax.axis_index("py")
    own_kx = width // devices
    y_cells = rows * px_count

    w_rows = w_star.reshape(levels * rows, width)
    temp_rows = air_temp.reshape(levels * rows, width)
    ids = facet_cells[0]
    w_near, temp_near, new_temp = near_walls(
        w_rows,
        temp_rows,
        ids,
        facet_temp[0],
        net_radiation[0],
        heat_capacity[0],
        drag_coef[0],
        heat_coef[0],
    )

    x_parts, sin_x = periodic_tables(width)
    y_parts, sin_y = periodic_tables(y_cells)
    cosines, sin_block = cosine_table(rows)
    x_tables = [t for part in x_parts for t in two_halves(part)]
    y_tables = [t for part in y_parts for t in two_halves(part)]
    to_modes, to_rows = two_halves(cosines), two_halves(np.ascontiguousarray(cosines.T))
    sin_x = jnp.asarray(sin_x, F32)

    sine = jnp.asarray(sin_block, F32)[:, None] + sin_x[None, :]
    half_root = 0.5 * jnp.sqrt(sine)
    root = jnp.sqrt(1.0 + half_root * half_root) - half_root
    root = root * root
    is_first, is_last = place_y == 0, place_y == py_count - 1
    top = jnp.where(is_last, root / (1.0 + root), 0.0)
    kappa = jnp.zeros_like(root)
    for _ in range(levels):
        kappa = root * root * (1.0 + kappa)
    decay = power(root, levels)
    bottom = jnp.where(is_first, 1.0 - 1.0 / root, 1.0)
    inv = 1.0 / (1.0 + bottom * (kappa - top * decay * decay))
    start = bottom * inv
    from_below = inv / root
    end = np.where(np.arange(rows) == 0, np.sqrt(1.0 / rows), cosines[:, 0])
    end = jnp.asarray(np.repeat(end[:, None], 128, axis=1), F32)

    vectors, sin_z = level_tables(levels)
    pick = lambda three: jnp.where(is_first, three[0], jnp.where(is_last, three[2], three[1])).astype(F32)
    vectors, sin_z = pick(vectors), pick(sin_z)
    sine_z = sin_z[:, None] + sin_x[None, :]
    size_z = jnp.sqrt(sine_z)
    half_z = 0.5 * size_z
    cosh_z = jnp.sqrt(1.0 + half_z * half_z)
    half_step = cosh_z - half_z
    across = jnp.exp(2.0 * rows * jnp.log(half_step))
    scale = 1.0 / ((1.0 - across * across) * size_z)
    same_end = -half_step * (1.0 + across * across / (half_step * half_step)) * scale
    far_end = -2.0 * across * cosh_z * scale
    turns = np.arange(px_count)
    circulant = jnp.stack(
        [1.0 / (1.0 - 2.0 * same_end + 2.0 * math.cos(2.0 * math.pi * s / px_count) * far_end) for s in turns]
    )
    phase_of = jnp.asarray(np.cos(2.0 * np.pi * turns[:, None] * turns[None, :] / px_count) / px_count, F32)
    offsets = jnp.stack([(place_x - turns) % px_count, (place_x - 1 - turns) % px_count])
    phases = phase_of[offsets]
    weights = jnp.sum(phases[:, :, :, None, None] * circulant[None, None], axis=2)

    mine = place_x * py_count + place_y
    own_sin = lax.dynamic_slice_in_dim(sin_x, mine * own_kx, own_kx)
    diag = -2.0 - own_sin[:, None] - jnp.asarray(sin_y, F32)[None, :]

    tile = math.gcd(rows, 32)
    tiles = rows // tile
    flat = lambda i: pl.BlockSpec((tile, width), i)
    fixed = lambda a: pl.BlockSpec(a.shape, lambda i: (0,) * a.ndim)
    late = lambda i: (jnp.maximum(i - levels, 0), 0)
    down = lambda i: (jnp.maximum(levels - 1 - i, 0), 0, 0)
    slab = pl.BlockSpec((1, rows, width), down)
    end_late = pl.BlockSpec((tile, 128), late)
    ends_shape = jax.ShapeDtypeStruct((2, levels, width), F32)
    field, edges, ends, w_corr = pl.pallas_call(
        lambda *refs: forward_kernel(levels, tile, *refs),
        out_shape=(
            jax.ShapeDtypeStruct(w_star.shape, F32),
            jax.ShapeDtypeStruct((2, rows, width), F32),
            ends_shape,
            jax.ShapeDtypeStruct(w_rows.shape, F32),
        ),
        grid=(levels + tiles,),
        in_specs=[SMEM, SMEM, HBM, slab] + [fixed(t) for t in (*x_tables, *to_modes)] + [flat(late)] * 4 + [end_late],
        out_specs=(
            pl.BlockSpec((levels, tile, width), lambda i: (0, *late(i))),
            pl.BlockSpec((2, tile, width), lambda i: (0, *late(i))),
            fixed(ends_shape),
            HBM,
        ),
        scratch_shapes=[
            pltpu.VMEM(w_star.shape, F32),
            pltpu.VMEM(w_rows.shape, F32),
            pltpu.VMEM((rows, width), F32),
            pltpu.VMEM((rows, width), F32),
            pltpu.VMEM((levels, 8, width), F32),
            pltpu.VMEM((levels, 8, width), F32),
            pltpu.SemaphoreType.DMA((2,)),
        ],
        compiler_params=PARAMS,
        name="forward",
    )(ids, w_near, w_rows, horiz_div, *x_tables, *to_modes, root, inv, start, top, end)

    all_ends = lax.all_gather(ends, "px")
    packed = jax.ShapeDtypeStruct((devices, 2, own_kx, rows), F32)
    working = [pltpu.VMEM((levels, 8, width), F32)] * 2
    edges = pl.pallas_call(
        lambda *refs: edge_kernel(levels, *refs),
        out_shape=packed,
        in_specs=[VMEM] * 11,
        out_specs=VMEM,
        scratch_shapes=working + [pltpu.VMEM((2, rows, width), F32)],
        compiler_params=PARAMS,
        name="edges",
    )(edges, all_ends, weights, vectors, root, inv, start, top, end, *to_modes)
    temp_near, edges = lax.optimization_barrier((temp_near, edges))
    theta_new = pl.pallas_call(
        theta_kernel,
        out_shape=jax.ShapeDtypeStruct(temp_rows.shape, BF16),
        in_specs=[SMEM, SMEM, VMEM],
        out_specs=VMEM,
        scratch_shapes=[pltpu.VMEM(temp_rows.shape, F32)],
        compiler_params=PARAMS,
        cost_estimate=pl.CostEstimate(flops=temp_rows.size, bytes_accessed=8 * temp_rows.size, transcendentals=0),
        name="theta",
    )(ids, temp_near, temp_rows).reshape(air_temp.shape)
    edges = lax.all_to_all(edges, ("px", "py"), split_axis=0, concat_axis=0, tiled=True)
    joined = pl.pallas_call(
        lambda *refs: join_kernel(levels, px_count, py_count, *refs),
        out_shape=packed,
        in_specs=[VMEM] * 8,
        out_specs=VMEM,
        scratch_shapes=[pltpu.VMEM((py_count, 2, own_kx, y_cells), F32)],
        compiler_params=PARAMS,
        name="join",
    )(edges, *y_tables, diag)
    joined = lax.all_to_all(joined, ("px", "py"), split_axis=0, concat_axis=0, tiled=True)
    sides, more = pl.pallas_call(
        lambda *refs: spread_kernel(levels, *refs),
        out_shape=(jax.ShapeDtypeStruct((2, rows, width), F32), ends_shape),
        in_specs=[VMEM] * 8,
        out_specs=(VMEM, VMEM),
        scratch_shapes=working,
        compiler_params=PARAMS,
        name="spread",
    )(joined, *to_modes, root, start, from_below, top, end)
    more = lax.all_gather(more, "px")

    early = lambda i: (jnp.minimum(i, tiles - 1), 0)
    up = lambda i: (jnp.maximum(i - tiles, 0), 0, 0)
    slab = pl.BlockSpec((1, rows, width), up)
    w_new = pl.pallas_call(
        lambda *refs: inverse_kernel(levels, tile, *refs),
        out_shape=jax.ShapeDtypeStruct(w_star.shape, F32),
        grid=(tiles + levels,),
        in_specs=[
            SMEM,
            pl.BlockSpec((levels, tile, width), lambda i: (0, *early(i))),
            pl.BlockSpec((2, tile, width), lambda i: (0, *early(i))),
        ]
        + [fixed(a) for a in (all_ends, more, weights, vectors)]
        + [flat(early)] * 4
        + [pl.BlockSpec((tile, 128), early)]
        + [fixed(t) for t in (*x_tables, *to_rows)]
        + [slab, fixed(roof_level)],
        out_specs=slab,
        scratch_shapes=[pltpu.VMEM(w_star.shape, F32)] + working,
        compiler_params=PARAMS,
        name="inverse",
    )(
        place_y.astype(jnp.int32).reshape(1),
        field,
        sides,
        all_ends,
        more,
        weights,
        vectors,
        root,
        start,
        from_below,
        top,
        end,
        *x_tables,
        *to_rows,
        w_corr.reshape(w_star.shape),
        roof_level,
    )
    return (w_new, theta_new, new_temp[None])


def solution(mesh):
    placed = (
        P("py", "px", None),
        P("py", "px", None),
        P("py", "px", None),
        P("px", None),
        P(("px", "py"), None),
        P(("px", "py"), None),
        P(("px", "py"), None),
        P(("px", "py"), None),
        P(("px", "py"), None),
        P(("px", "py"), None),
    )
    return jax.shard_map(
        body,
        mesh=mesh,
        in_specs=placed,
        out_specs=(P("py", "px", None), P("py", "px", None), P(("px", "py"), None)),
        check_vma=False,
    )
```

```python
import math

import jax
import jax.numpy as jnp
import ml_dtypes
import numpy as np
from jax import lax
from jax.experimental import pallas as pl
from jax.experimental.pallas import tpu as pltpu
from jax.sharding import PartitionSpec as P

F32 = jnp.float32
BF16 = jnp.bfloat16
HBM = pl.BlockSpec(memory_space=pl.ANY)
VMEM = pl.BlockSpec(memory_space=pltpu.VMEM)
SMEM = pl.BlockSpec(memory_space=pltpu.SMEM)
PARAMS = pltpu.CompilerParams(vmem_limit_bytes=58 * 2**20)


def two_halves(table):
    high = table.astype(ml_dtypes.bfloat16)
    low = (table - high.astype(np.float64)).astype(ml_dtypes.bfloat16)
    return (jnp.asarray(high), jnp.asarray(low))


def periodic_tables(size):
    half, quarter = size // 2, size // 4
    groups = (
        (np.arange(0, half + 1, 4), np.arange(4, half, 4), quarter),
        (np.arange(2, half, 4), np.arange(2, half, 4), quarter),
        (np.arange(1, half, 2), np.arange(1, half, 2), half),
    )
    tables, waves = [], []
    for cosines, sines, rows in groups:
        x = np.arange(rows)[:, None]
        norms = np.where((cosines == 0) | (cosines == half), np.sqrt(1.0 / size), np.sqrt(2.0 / size))
        tables.append(
            np.concatenate(
                [
                    norms * np.cos(2.0 * np.pi / size * (x * cosines % size)),
                    np.sqrt(2.0 / size) * np.sin(2.0 * np.pi / size * (x * sines % size)),
                ],
                axis=1,
            )
        )
        waves += [cosines, sines]
    waves = np.concatenate(waves)
    return (tables, 4.0 * np.sin(np.pi * waves / size) ** 2)


def cosine_table(size):
    modes = np.arange(size)[:, None]
    table = np.sqrt(2.0 / size) * np.cos(np.pi * modes * (2 * np.arange(size)[None, :] + 1) / (2 * size))
    table[0] = np.sqrt(1.0 / size)
    return (table, 4.0 * np.sin(np.pi * modes[:, 0] / (2 * size)) ** 2)


def level_tables(size):
    modes, levels = np.arange(size)[None, :], np.arange(size)[:, None]
    omegas = (
        np.pi * (2 * modes + 1) / (2 * size + 1),
        np.pi * (modes + 1) / (size + 1),
        np.pi * (modes + 1) / (size + 0.5),
    )
    vectors = (
        np.cos(omegas[0] * (levels + 0.5)),
        np.sin(omegas[1] * (levels + 1)),
        np.sin(omegas[2] * (levels + 1)),
    )
    vectors = [v / np.sqrt(np.sum(v * v, axis=0, keepdims=True)) for v in vectors]
    return (vectors, [4.0 * np.sin(o[0] / 2) ** 2 for o in omegas])


def split(value):
    high = value.astype(BF16)
    return (high, (value - high.astype(F32)).astype(BF16))


def dot3(left, right, dims=((1,), (0,))):
    one = lambda a, b: lax.dot_general(a, b, (dims, ((), ())), preferred_element_type=F32)
    return one(left[0], right[0]) + (one(left[1], right[0]) + one(left[0], right[1]))


def read_pair(refs):
    return (refs[0][...], refs[1][...])


def periodic_forward(value, tables):
    half, quarter = value.shape[1] // 2, value.shape[1] // 4
    even, odd = value[:, :half] + value[:, half:], value[:, :half] - value[:, half:]
    parts = (even[:, :quarter] + even[:, quarter:], even[:, :quarter] - even[:, quarter:], odd)
    return jnp.concatenate([dot3(split(p), read_pair(t)) for p, t in zip(parts, tables)], axis=1)


def periodic_inverse(value, tables):
    half, quarter = value.shape[1] // 2, value.shape[1] // 4
    parts = (value[:, :quarter], value[:, quarter:half], value[:, half:])
    four, two, odd = [dot3(split(p), read_pair(t), ((1,), (1,))) for p, t in zip(parts, tables)]
    even = jnp.concatenate([four + two, four - two], axis=1)
    return jnp.concatenate([even + odd, even - odd], axis=1)


def power(base, exponent):
    result = None
    while exponent:
        if exponent & 1:
            result = base if result is None else result * base
        base = base * base
        exponent >>= 1
    return result


def first_sweeps(load, root, top, above, store, levels):
    value = None
    for level in range(levels):
        value = load(level) if value is None else load(level) + root * value
        store[level] = value
    last = value
    value = top * value if above is None else top * value + above
    for level in range(levels - 1, -1, -1):
        value = root * (value - store[level])
    return (value, last)


def second_sweeps(load, start, root, top, above, store, levels, emit):
    value = start
    for level in range(levels):
        value = root * value if load is None else load(level) + root * value
        store[level] = value
    value = top * value if above is None else top * value + above
    for level in range(levels - 1, -1, -1):
        value = root * (value - store[level])
        emit(level, value)


def block_fluxes(ends, weights_ref, vectors_ref, levels, out_ref):
    blocks = len(ends)
    one = lambda dims, b: lax.dot_general(
        vectors_ref[...], b, (dims, ((), ())), precision=lax.Precision.HIGHEST, preferred_element_type=F32
    )
    upper = lower = None
    for block in range(blocks):
        even_next, odd_next = ends[(block + 1) % blocks]
        even, odd = ends[block]
        jump = one(((0,), (0,)), (even_next + odd_next) - (even - odd))
        up, low = weights_ref[0, block] * jump, weights_ref[1, block] * jump
        upper = up if upper is None else upper + up
        lower = low if lower is None else lower + low
    upper, lower = one(((1,), (0,)), upper), one(((1,), (0,)), lower)
    width = upper.shape[1]
    is_even = lax.broadcasted_iota(jnp.int32, (8, width), 0) % 2 == 0
    for level in range(levels):
        up, low = upper[level : level + 1], lower[level : level + 1]
        out_ref[level] = jnp.where(is_even, up - low, -up - low)


def fold_ends(total, out_ref, levels):
    is_even = lax.broadcasted_iota(jnp.int32, total.shape[1:], 0) % 2 == 0
    for level in range(levels):
        value = total[level]
        out_ref[0, level : level + 1] = jnp.sum(jnp.where(is_even, value, 0.0), axis=0, keepdims=True)
        out_ref[1, level : level + 1] = jnp.sum(jnp.where(is_even, 0.0, value), axis=0, keepdims=True)


def forward_kernel(
    levels, tile, ids_ref, w_new_ref, w_hbm, div_ref, t0h, t0l, t1h, t1l, t2h, t2l, ch, cl, root_ref, inv_ref,
    start_ref, top_ref, end_ref, field_ref, edge_ref, ends_ref, corr_hbm, field, w_rows, above, lowest, store, total,
    sems,
):
    step = pl.program_id(0)
    tables = ((t0h, t0l), (t1h, t1l), (t2h, t2l))

    def transform(value):
        return dot3(read_pair((ch, cl)), split(periodic_forward(value, tables)))

    @pl.when(step == 0)
    def _():
        load = pltpu.make_async_copy(w_hbm, w_rows, sems.at[0])
        load.start()
        above[...] = jnp.zeros_like(above)
        total[...] = jnp.zeros_like(total)
        load.wait()
        put_cells(ids_ref, w_new_ref, w_rows)
        pltpu.make_async_copy(w_rows, corr_hbm, sems.at[1]).start()

    row_count = above.shape[0]

    @pl.when(step < levels)
    def _():
        value = w_rows[pl.ds(pl.multiple_of((levels - 1 - step) * row_count, row_count), row_count)]
        field[levels - 1 - step] = transform(div_ref[0] + above[...] - value)
        above[...] = value

    @pl.when(step == levels - 1)
    def _():
        lowest[...] = transform(w_rows[:row_count])

    @pl.when(step >= levels)
    def _():
        def rows_of(sub, _):
            here = pl.multiple_of(sub * 8, 8)
            rows = pl.ds(here, 8)
            full = pl.ds(pl.multiple_of((step - levels) * tile + here, 8), 8)
            root, top = root_ref[rows], top_ref[rows]
            load = lambda level: field[level, full]
            first, _ = first_sweeps(load, root, top, None, store, levels)
            edge_ref[0, rows] = first * inv_ref[rows] - lowest[full]
            weight = end_ref[rows, :1]

            def emit(level, value):
                total[level] += weight * value
                if level == levels - 1:
                    edge_ref[1, rows] = value

            second_sweeps(load, first * start_ref[rows], root, top, None, store, levels, emit)
            for level in range(levels):
                field_ref[level, rows] = load(level)
            return 0

        lax.fori_loop(0, tile // 8, rows_of, 0)

    @pl.when(step == pl.num_programs(0) - 1)
    def _():
        fold_ends(total, ends_ref, levels)
        pltpu.make_async_copy(w_rows, corr_hbm, sems.at[1]).wait()


def edge_kernel(
    levels, edge_ref, ends_ref, weights_ref, vectors_ref, root_ref, inv_ref, start_ref, top_ref, end_ref, ch, cl,
    out_ref, pattern, store, fixed,
):
    block_fluxes(
        [(ends_ref[b, 0], ends_ref[b, 1]) for b in range(ends_ref.shape[0])], weights_ref, vectors_ref, levels, pattern
    )

    def rows_of(sub, _):
        rows = pl.ds(pl.multiple_of(sub * 8, 8), 8)
        root, top = root_ref[rows], top_ref[rows]
        first, last = first_sweeps(lambda level: pattern[level], root, top, None, store, levels)
        weight = end_ref[rows, :1]
        fixed[0, rows] = edge_ref[0, rows] - weight * (first * inv_ref[rows])
        last = last + power(root, levels) * (first * start_ref[rows])
        fixed[1, rows] = edge_ref[1, rows] - weight * (root * (top - 1.0) * last)
        return 0

    lax.fori_loop(0, edge_ref.shape[1] // 8, rows_of, 0)
    for side in range(2):
        value = dot3(split(fixed[side].T), read_pair((ch, cl)))
        out_ref[:, side] = value.reshape(out_ref.shape[0], out_ref.shape[2], out_ref.shape[3])


def join_start(levels, near_top, diag):
    near = 1.0 / diag
    far = near
    ends = [1.0 / (diag + 1.0), 1.0 / (diag - 1.0)]
    for _ in range(1, levels):
        near = 1.0 / (diag - near)
        far = -far * near
        ends = [1.0 / (diag - e) for e in ends]
    own = jnp.where(near_top, ends[1], ends[0])
    other = jnp.where(near_top, ends[0], ends[1])
    return (near, far, own, other)


def join_chain(load, blocks, near, far, beta):
    alpha = load(0, 1)
    alphas, betas, heads, slopes = [alpha], [beta], [None], [None]
    for block in range(1, blocks):
        scale = 1.0 / (1.0 - near * beta)
        head = (load(block, 0) - near * alpha) * scale
        slope = far * scale
        alpha = load(block, 1) - far * alpha + far * beta * head
        beta = near + far * beta * slope
        alphas.append(alpha)
        betas.append(beta)
        heads.append(head)
        slopes.append(slope)
    return (alphas, betas, heads, slopes)


def chain_place(block, blocks, half):
    return block + half * (blocks - 1 - 2 * block)


def gather_modes_kernel(levels, px_count, half_ref, edge_ref, t0h, t0l, t1h, t1l, t2h, t2l, diag_ref, out_ref, alpha_ref):
    blocks, _, rows, _ = out_ref.shape
    half = half_ref[0]
    for block in range(blocks):
        for side in range(2):
            whole = jnp.concatenate([edge_ref[i * blocks + block, side] for i in range(px_count)], axis=1)
            out_ref[block, side] = periodic_forward(whole, ((t0h, t0l), (t1h, t1l), (t2h, t2l)))

    def rows_of(sub, _):
        here = pl.ds(pl.multiple_of(sub * 8, 8), 8)
        near, far, own, _ = join_start(levels, half == 1, diag_ref[here])
        load = lambda block, outer: out_ref[chain_place(block, blocks, half), jnp.abs(outer - half), here]
        alpha_ref[here] = join_chain(load, blocks, near, far, own)[0][-1]
        return 0

    lax.fori_loop(0, rows // 8, rows_of, 0)


def join_kernel(
    levels, px_count, half_ref, modes_ref, alpha_ref, t0h, t0l, t1h, t1l, t2h, t2l, diag_ref, out_ref, modes
):
    blocks, _, rows, _ = modes_ref.shape
    half = half_ref[0]
    width = out_ref.shape[3]

    def rows_of(sub, _):
        here = pl.ds(pl.multiple_of(sub * 8, 8), 8)
        near, far, own, other = join_start(levels, half == 1, diag_ref[here])
        load = lambda block, outer: modes_ref[chain_place(block, blocks, half), jnp.abs(outer - half), here]
        alphas, betas, heads, slopes = join_chain(load, blocks, near, far, own)
        for _ in range(1, blocks):
            other = near + far * other * (far / (1.0 - near * other))
        met = alpha_ref[here]
        outer = (met - other * alphas[-1]) / (1.0 - other * betas[-1])
        for block in range(blocks - 1, -1, -1):
            place = chain_place(block, blocks, half)
            modes[place, 1 - half, here] = outer
            if block:
                outer = heads[block] - slopes[block] * outer
                modes[place, half, here] = alphas[block - 1] - betas[block - 1] * outer
            else:
                modes[place, half, here] = jnp.zeros_like(outer)
        return 0

    lax.fori_loop(0, rows // 8, rows_of, 0)
    for block in range(blocks):
        for side in range(2):
            whole = periodic_inverse(modes[block, side], ((t0h, t0l), (t1h, t1l), (t2h, t2l)))
            for i in range(px_count):
                out_ref[i * blocks + block, side] = whole[:, i * width : (i + 1) * width]


def spread_kernel(levels, joined_ref, ch, cl, root_ref, start_ref, below_ref, top_ref, end_ref, out_ref, ends_ref, store, total):
    kx_width = joined_ref.shape[0] * joined_ref.shape[2]
    for side in range(2):
        value = joined_ref[:, side].reshape(kx_width, joined_ref.shape[3])
        out_ref[side] = dot3(read_pair((ch, cl)), split(value), ((1,), (1,)))
    total[...] = jnp.zeros_like(total)

    def rows_of(sub, _):
        rows = pl.ds(pl.multiple_of(sub * 8, 8), 8)
        root, top = root_ref[rows], top_ref[rows]
        below, above = out_ref[0, rows], out_ref[1, rows]
        start = start_ref[rows] * (power(root, levels) * above) - below_ref[rows] * below
        weight = end_ref[rows, :1]

        def emit(level, value):
            total[level] += weight * value

        second_sweeps(None, start, root, top, above, store, levels, emit)
        return 0

    lax.fori_loop(0, out_ref.shape[1] // 8, rows_of, 0)
    fold_ends(total, ends_ref, levels)


def inverse_kernel(
    levels, tile, place_ref, field_ref, sides_ref, ends_ref, more_ref, weights_ref, vectors_ref, root_ref, start_ref,
    below_ref, top_ref, end_ref, t0h, t0l, t1h, t1l, t2h, t2l, ch, cl, w_ref, roof_ref, out_ref, field, pattern, store,
):
    step = pl.program_id(0)
    tiles = pl.num_programs(0) - levels
    tables = ((t0h, t0l), (t1h, t1l), (t2h, t2l))

    @pl.when(step == 0)
    def _():
        ends = [
            (ends_ref[b, 0] + more_ref[b, 0], ends_ref[b, 1] + more_ref[b, 1]) for b in range(ends_ref.shape[0])
        ]
        block_fluxes(ends, weights_ref, vectors_ref, levels, pattern)

    @pl.when(step < tiles)
    def _():
        def rows_of(sub, _):
            here = pl.multiple_of(sub * 8, 8)
            rows = pl.ds(here, 8)
            full = pl.ds(pl.multiple_of(step * tile + here, 8), 8)
            root, top = root_ref[rows], top_ref[rows]
            below, above = sides_ref[0, rows], sides_ref[1, rows]
            weight = end_ref[rows, :1]
            load = lambda level: field_ref[level, rows] - weight * pattern[level]
            first, _ = first_sweeps(load, root, top, above, store, levels)
            start = start_ref[rows] * first - below_ref[rows] * below
            held = []

            def emit(level, value):
                if held:
                    field[level + 1, full] = held.pop() - value
                held.append(value)

            second_sweeps(load, start, root, top, above, store, levels, emit)
            field[0, full] = jnp.where(place_ref[0] == 0, 0.0, held[0] - below)
            return 0

        lax.fori_loop(0, tile // 8, rows_of, 0)

    @pl.when(step >= tiles)
    def _():
        level = step - tiles
        rows_y = dot3(read_pair((ch, cl)), split(field[level]))
        slope = periodic_inverse(rows_y, tables)
        solid = place_ref[0] * levels + level < roof_ref[...]
        out_ref[0] = jnp.where(solid, 0.0, w_ref[0] - slope)


def divide(value, size):
    if size & (size - 1):
        return lax.div(value, size)
    return lax.shift_right_logical(value, size.bit_length() - 1)


def remainder(value, size):
    return lax.rem(value, size) if size & (size - 1) else value & (size - 1)


def tile_at(cell, width, tall):
    row, column = divide(cell, width), remainder(cell, width)
    return (
        pl.ds(pl.multiple_of(divide(row, tall) * tall, tall), tall),
        pl.ds(pl.multiple_of(divide(column, 128) * 128, 128), 128),
    )


def gather_kernel(ids_ref, w_hbm, temp_hbm, w_out, temp_out, w_ref, temp_ref, sems):
    copies = [
        pltpu.make_async_copy(w_hbm, w_ref, sems.at[0]),
        pltpu.make_async_copy(temp_hbm, temp_ref, sems.at[1]),
    ]
    for copy in copies:
        copy.start()
    width = w_ref.shape[1]
    sublane = lax.broadcasted_iota(jnp.int32, (8, 128), 0)

    def pick(i, ref, out):
        rows = None
        for lane in range(8):
            cell = jnp.maximum(ids_ref[i * 8 + lane], 0)
            row = divide(cell, width)
            if ref.dtype == F32:
                tile = ref[tile_at(cell, width, 8)]
            else:
                both = ref[tile_at(cell, width, 16)].astype(F32)
                tile = jnp.where(remainder(row, 16) < 8, both[:8], both[8:])
            tile = pltpu.roll(tile, remainder(lane + 8 - remainder(row, 8), 8), 0)
            rows = tile if rows is None else jnp.where(sublane == lane, tile, rows)
        out[pl.ds(pl.multiple_of(i * 8, 8), 8)] = rows
        return 0

    groups = ids_ref.shape[0] // 8
    copies[0].wait()
    lax.fori_loop(0, groups, lambda i, _: pick(i, w_ref, w_out), 0)
    copies[1].wait()
    lax.fori_loop(0, groups, lambda i, _: pick(i, temp_ref, temp_out), 0)


def put_cells(ids_ref, new_ref, out):
    width = out.shape[1]
    sublane = lax.broadcasted_iota(jnp.int32, (8, 128), 0)
    lane = lax.broadcasted_iota(jnp.int32, (8, 128), 1)
    position = sublane * 128 + lane

    def put(i, _):
        for k in range(8):
            facet = i * 8 + k
            cell = ids_ref[facet]
            safe = jnp.maximum(cell, 0)
            at = remainder(divide(safe, width), 8) * 128 + remainder(safe, 128)
            hit = position == jnp.where(cell < 0, -1, at)
            pltpu.store(out.at[tile_at(safe, width, 8)], jnp.full((8, 128), new_ref[facet]), mask=hit)
        return 0

    lax.fori_loop(0, ids_ref.shape[0] // 8, put, 0)


def theta_kernel(ids_ref, new_ref, temp_ref, out_ref, wide):
    rows = temp_ref.shape[0]
    chunk = math.gcd(rows, 64)

    def widen(i, _):
        here = pl.ds(pl.multiple_of(i * chunk, chunk), chunk)
        wide[here] = temp_ref[here].astype(F32)
        return 0

    def narrow(i, _):
        here = pl.ds(pl.multiple_of(i * chunk, chunk), chunk)
        out_ref[here] = wide[here].astype(BF16)
        return 0

    lax.fori_loop(0, rows // chunk, widen, 0)
    put_cells(ids_ref, new_ref, wide)
    lax.fori_loop(0, rows // chunk, narrow, 0)


def near_walls(w_rows, temp_rows, ids, facet_temp, net_radiation, heat_capacity, drag_coef, heat_coef):
    count = ids.shape[0]
    shape = jax.ShapeDtypeStruct((count, 128), F32)
    near = pl.pallas_call(
        gather_kernel,
        out_shape=(shape, shape),
        in_specs=[SMEM, HBM, HBM],
        out_specs=(VMEM, VMEM),
        scratch_shapes=[
            pltpu.VMEM(w_rows.shape, F32),
            pltpu.VMEM(temp_rows.shape, BF16),
            pltpu.SemaphoreType.DMA((2,)),
        ],
        compiler_params=PARAMS,
        name="facet_gather",
    )(ids, w_rows, temp_rows)
    lane = jnp.where(ids < 0, -1, ids % 128)
    hit = lax.broadcasted_iota(jnp.int32, (count, 128), 1) == lane[:, None]
    own = jnp.stack([jnp.sum(jnp.where(hit, rows, 0.0), axis=1) for rows in near])
    arrived = lax.all_to_all(own, ("px", "py_half", "py_low"), split_axis=1, concat_axis=1, tiled=True)
    w_cell, temp_cell = arrived[0], arrived[1]
    speeds = jnp.sqrt(w_cell * w_cell + 0.25)
    stress = drag_coef * speeds * w_cell
    heat_flux = heat_coef * speeds * (facet_temp - temp_cell)
    new_temp = facet_temp + (net_radiation - heat_flux - 0.5 * facet_temp) / heat_capacity
    returned = lax.all_to_all(
        jnp.stack([stress, heat_flux]), ("px", "py_half", "py_low"), split_axis=1, concat_axis=1, tiled=True
    )
    same = ids[:, None] == ids[None, :]
    sums = [jnp.sum(jnp.where(same, returned[i][None, :], 0.0), axis=1) for i in range(2)]
    return (own[0] - sums[0], own[1] + sums[1], new_temp)


def body(
    horiz_div,
    w_star,
    air_temp,
    roof_level,
    facet_cells,
    facet_temp,
    net_radiation,
    heat_capacity,
    drag_coef,
    heat_coef,
):
    levels, rows, width = w_star.shape
    px_count, blocks = lax.axis_size("px"), lax.axis_size("py_low")
    py_count = 2 * blocks
    group = px_count * blocks
    place_x, place_y, half = lax.axis_index("px"), lax.axis_index(("py_half", "py_low")), lax.axis_index("py_half")
    own_kx = width // group
    y_cells = rows * px_count

    w_rows = w_star.reshape(levels * rows, width)
    temp_rows = air_temp.reshape(levels * rows, width)
    ids = facet_cells[0]
    w_near, temp_near, new_temp = near_walls(
        w_rows,
        temp_rows,
        ids,
        facet_temp[0],
        net_radiation[0],
        heat_capacity[0],
        drag_coef[0],
        heat_coef[0],
    )

    x_parts, sin_x = periodic_tables(width)
    y_parts, sin_y = periodic_tables(y_cells)
    cosines, sin_block = cosine_table(rows)
    x_tables = [t for part in x_parts for t in two_halves(part)]
    y_tables = [t for part in y_parts for t in two_halves(part)]
    to_modes, to_rows = two_halves(cosines), two_halves(np.ascontiguousarray(cosines.T))
    sin_x = jnp.asarray(sin_x, F32)

    sine = jnp.asarray(sin_block, F32)[:, None] + sin_x[None, :]
    half_root = 0.5 * jnp.sqrt(sine)
    root = jnp.sqrt(1.0 + half_root * half_root) - half_root
    root = root * root
    is_first, is_last = place_y == 0, place_y == py_count - 1
    top = jnp.where(is_last, root / (1.0 + root), 0.0)
    kappa = jnp.zeros_like(root)
    for _ in range(levels):
        kappa = root * root * (1.0 + kappa)
    decay = power(root, levels)
    bottom = jnp.where(is_first, 1.0 - 1.0 / root, 1.0)
    inv = 1.0 / (1.0 + bottom * (kappa - top * decay * decay))
    start = bottom * inv
    from_below = inv / root
    end = np.where(np.arange(rows) == 0, np.sqrt(1.0 / rows), cosines[:, 0])
    end = jnp.asarray(np.repeat(end[:, None], 128, axis=1), F32)

    vectors, sin_z = level_tables(levels)
    pick = lambda three: jnp.where(is_first, three[0], jnp.where(is_last, three[2], three[1])).astype(F32)
    vectors, sin_z = pick(vectors), pick(sin_z)
    sine_z = sin_z[:, None] + sin_x[None, :]
    size_z = jnp.sqrt(sine_z)
    half_z = 0.5 * size_z
    cosh_z = jnp.sqrt(1.0 + half_z * half_z)
    half_step = cosh_z - half_z
    across = jnp.exp(2.0 * rows * jnp.log(half_step))
    scale = 1.0 / ((1.0 - across * across) * size_z)
    same_end = -half_step * (1.0 + across * across / (half_step * half_step)) * scale
    far_end = -2.0 * across * cosh_z * scale
    turns = np.arange(px_count)
    circulant = jnp.stack(
        [1.0 / (1.0 - 2.0 * same_end + 2.0 * math.cos(2.0 * math.pi * s / px_count) * far_end) for s in turns]
    )
    phase_of = jnp.asarray(np.cos(2.0 * np.pi * turns[:, None] * turns[None, :] / px_count) / px_count, F32)
    offsets = jnp.stack([(place_x - turns) % px_count, (place_x - 1 - turns) % px_count])
    phases = phase_of[offsets]
    weights = jnp.sum(phases[:, :, :, None, None] * circulant[None, None], axis=2)

    mine = place_x * blocks + lax.axis_index("py_low")
    own_sin = lax.dynamic_slice_in_dim(sin_x, mine * own_kx, own_kx)
    diag = -2.0 - own_sin[:, None] - jnp.asarray(sin_y, F32)[None, :]

    tile = math.gcd(rows, 32)
    tiles = rows // tile
    flat = lambda i: pl.BlockSpec((tile, width), i)
    fixed = lambda a: pl.BlockSpec(a.shape, lambda i: (0,) * a.ndim)
    late = lambda i: (jnp.maximum(i - levels, 0), 0)
    down = lambda i: (jnp.maximum(levels - 1 - i, 0), 0, 0)
    slab = pl.BlockSpec((1, rows, width), down)
    end_late = pl.BlockSpec((tile, 128), late)
    ends_shape = jax.ShapeDtypeStruct((2, levels, width), F32)
    field, edges, ends, w_corr = pl.pallas_call(
        lambda *refs: forward_kernel(levels, tile, *refs),
        out_shape=(
            jax.ShapeDtypeStruct(w_star.shape, F32),
            jax.ShapeDtypeStruct((2, rows, width), F32),
            ends_shape,
            jax.ShapeDtypeStruct(w_rows.shape, F32),
        ),
        grid=(levels + tiles,),
        in_specs=[SMEM, SMEM, HBM, slab] + [fixed(t) for t in (*x_tables, *to_modes)] + [flat(late)] * 4 + [end_late],
        out_specs=(
            pl.BlockSpec((levels, tile, width), lambda i: (0, *late(i))),
            pl.BlockSpec((2, tile, width), lambda i: (0, *late(i))),
            fixed(ends_shape),
            HBM,
        ),
        scratch_shapes=[
            pltpu.VMEM(w_star.shape, F32),
            pltpu.VMEM(w_rows.shape, F32),
            pltpu.VMEM((rows, width), F32),
            pltpu.VMEM((rows, width), F32),
            pltpu.VMEM((levels, 8, width), F32),
            pltpu.VMEM((levels, 8, width), F32),
            pltpu.SemaphoreType.DMA((2,)),
        ],
        compiler_params=PARAMS,
        name="forward",
    )(ids, w_near, w_rows, horiz_div, *x_tables, *to_modes, root, inv, start, top, end)

    all_ends = lax.all_gather(ends, "px")
    packed = jax.ShapeDtypeStruct((group, 2, own_kx, rows), F32)
    working = [pltpu.VMEM((levels, 8, width), F32)] * 2
    edges = pl.pallas_call(
        lambda *refs: edge_kernel(levels, *refs),
        out_shape=packed,
        in_specs=[VMEM] * 11,
        out_specs=VMEM,
        scratch_shapes=working + [pltpu.VMEM((2, rows, width), F32)],
        compiler_params=PARAMS,
        name="edges",
    )(edges, all_ends, weights, vectors, root, inv, start, top, end, *to_modes)
    temp_near, edges = lax.optimization_barrier((temp_near, edges))
    theta_new = pl.pallas_call(
        theta_kernel,
        out_shape=jax.ShapeDtypeStruct(temp_rows.shape, BF16),
        in_specs=[SMEM, SMEM, VMEM],
        out_specs=VMEM,
        scratch_shapes=[pltpu.VMEM(temp_rows.shape, F32)],
        compiler_params=PARAMS,
        cost_estimate=pl.CostEstimate(flops=temp_rows.size, bytes_accessed=8 * temp_rows.size, transcendentals=0),
        name="theta",
    )(ids, temp_near, temp_rows).reshape(air_temp.shape)
    edges = lax.all_to_all(edges, ("px", "py_low"), split_axis=0, concat_axis=0, tiled=True)
    half_id = half.astype(jnp.int32).reshape(1)
    modes, alpha = pl.pallas_call(
        lambda *refs: gather_modes_kernel(levels, px_count, *refs),
        out_shape=(
            jax.ShapeDtypeStruct((blocks, 2, own_kx, y_cells), F32),
            jax.ShapeDtypeStruct((own_kx, y_cells), F32),
        ),
        in_specs=[SMEM] + [VMEM] * 8,
        out_specs=(VMEM, VMEM),
        compiler_params=PARAMS,
        name="gather_modes",
    )(half_id, edges, *y_tables, diag)
    alpha = lax.ppermute(alpha, "py_half", [(0, 1), (1, 0)])
    joined = pl.pallas_call(
        lambda *refs: join_kernel(levels, px_count, *refs),
        out_shape=packed,
        in_specs=[SMEM] + [VMEM] * 9,
        out_specs=VMEM,
        scratch_shapes=[pltpu.VMEM((blocks, 2, own_kx, y_cells), F32)],
        compiler_params=PARAMS,
        name="join",
    )(half_id, modes, alpha, *y_tables, diag)
    joined = lax.all_to_all(joined, ("px", "py_low"), split_axis=0, concat_axis=0, tiled=True)
    sides, more = pl.pallas_call(
        lambda *refs: spread_kernel(levels, *refs),
        out_shape=(jax.ShapeDtypeStruct((2, rows, width), F32), ends_shape),
        in_specs=[VMEM] * 8,
        out_specs=(VMEM, VMEM),
        scratch_shapes=working,
        compiler_params=PARAMS,
        name="spread",
    )(joined, *to_modes, root, start, from_below, top, end)
    more = lax.all_gather(more, "px")

    early = lambda i: (jnp.minimum(i, tiles - 1), 0)
    up = lambda i: (jnp.maximum(i - tiles, 0), 0, 0)
    slab = pl.BlockSpec((1, rows, width), up)
    w_new = pl.pallas_call(
        lambda *refs: inverse_kernel(levels, tile, *refs),
        out_shape=jax.ShapeDtypeStruct(w_star.shape, F32),
        grid=(tiles + levels,),
        in_specs=[
            SMEM,
            pl.BlockSpec((levels, tile, width), lambda i: (0, *early(i))),
            pl.BlockSpec((2, tile, width), lambda i: (0, *early(i))),
        ]
        + [fixed(a) for a in (all_ends, more, weights, vectors)]
        + [flat(early)] * 4
        + [pl.BlockSpec((tile, 128), early)]
        + [fixed(t) for t in (*x_tables, *to_rows)]
        + [slab, fixed(roof_level)],
        out_specs=slab,
        scratch_shapes=[pltpu.VMEM(w_star.shape, F32)] + working,
        compiler_params=PARAMS,
        name="inverse",
    )(
        place_y.astype(jnp.int32).reshape(1),
        field,
        sides,
        all_ends,
        more,
        weights,
        vectors,
        root,
        start,
        from_below,
        top,
        end,
        *x_tables,
        *to_rows,
        w_corr.reshape(w_star.shape),
        roof_level,
    )
    return (w_new, theta_new, new_temp[None])


def solution(mesh):
    px_count, py_count = mesh.devices.shape
    split_mesh = jax.sharding.Mesh(
        mesh.devices.reshape(px_count, 2, py_count // 2), ("px", "py_half", "py_low")
    )
    py, every = ("py_half", "py_low"), ("px", "py_half", "py_low")
    placed = (P(py, "px", None),) * 3 + (P("px", None),) + (P(every, None),) * 6
    return jax.shard_map(
        body,
        mesh=split_mesh,
        in_specs=placed,
        out_specs=(P(py, "px", None), P(py, "px", None), P(every, None)),
        check_vma=False,
    )
```

```python
import math

import jax
import jax.numpy as jnp
import ml_dtypes
import numpy as np
from jax import lax
from jax.experimental import pallas as pl
from jax.experimental.pallas import tpu as pltpu
from jax.sharding import PartitionSpec as P

F32 = jnp.float32
BF16 = jnp.bfloat16
HBM = pl.BlockSpec(memory_space=pl.ANY)
VMEM = pl.BlockSpec(memory_space=pltpu.VMEM)
SMEM = pl.BlockSpec(memory_space=pltpu.SMEM)
PARAMS = pltpu.CompilerParams(vmem_limit_bytes=58 * 2**20)


def two_halves(table):
    high = table.astype(ml_dtypes.bfloat16)
    low = (table - high.astype(np.float64)).astype(ml_dtypes.bfloat16)
    return (jnp.asarray(high), jnp.asarray(low))


def periodic_tables(size):
    half, quarter = size // 2, size // 4
    groups = (
        (np.arange(0, half + 1, 4), np.arange(4, half, 4), quarter),
        (np.arange(2, half, 4), np.arange(2, half, 4), quarter),
        (np.arange(1, half, 2), np.arange(1, half, 2), half),
    )
    tables, waves = [], []
    for cosines, sines, rows in groups:
        x = np.arange(rows)[:, None]
        norms = np.where((cosines == 0) | (cosines == half), np.sqrt(1.0 / size), np.sqrt(2.0 / size))
        tables.append(
            np.concatenate(
                [
                    norms * np.cos(2.0 * np.pi / size * (x * cosines % size)),
                    np.sqrt(2.0 / size) * np.sin(2.0 * np.pi / size * (x * sines % size)),
                ],
                axis=1,
            )
        )
        waves += [cosines, sines]
    waves = np.concatenate(waves)
    return (tables, 4.0 * np.sin(np.pi * waves / size) ** 2)


def cosine_table(size):
    modes = np.arange(size)[:, None]
    table = np.sqrt(2.0 / size) * np.cos(np.pi * modes * (2 * np.arange(size)[None, :] + 1) / (2 * size))
    table[0] = np.sqrt(1.0 / size)
    return (table, 4.0 * np.sin(np.pi * modes[:, 0] / (2 * size)) ** 2)


def level_tables(size):
    modes, levels = np.arange(size)[None, :], np.arange(size)[:, None]
    omegas = (
        np.pi * (2 * modes + 1) / (2 * size + 1),
        np.pi * (modes + 1) / (size + 1),
        np.pi * (modes + 1) / (size + 0.5),
    )
    vectors = (
        np.cos(omegas[0] * (levels + 0.5)),
        np.sin(omegas[1] * (levels + 1)),
        np.sin(omegas[2] * (levels + 1)),
    )
    vectors = [v / np.sqrt(np.sum(v * v, axis=0, keepdims=True)) for v in vectors]
    return (vectors, [4.0 * np.sin(o[0] / 2) ** 2 for o in omegas])


def split(value):
    high = value.astype(BF16)
    return (high, (value - high.astype(F32)).astype(BF16))


def dot3(left, right, dims=((1,), (0,))):
    one = lambda a, b: lax.dot_general(a, b, (dims, ((), ())), preferred_element_type=F32)
    free = 1 - dims[0][0]
    size = left[0].shape[free]
    both = one(jnp.concatenate(left, axis=free), right[0])
    return both[:size] + (both[size:] + one(left[0], right[1]))


def read_pair(refs):
    return (refs[0][...], refs[1][...])


def periodic_forward(value, tables):
    half, quarter = value.shape[1] // 2, value.shape[1] // 4
    even, odd = value[:, :half] + value[:, half:], value[:, :half] - value[:, half:]
    parts = (even[:, :quarter] + even[:, quarter:], even[:, :quarter] - even[:, quarter:], odd)
    return jnp.concatenate([dot3(split(p), read_pair(t)) for p, t in zip(parts, tables)], axis=1)


def periodic_inverse(value, tables):
    half, quarter = value.shape[1] // 2, value.shape[1] // 4
    parts = (value[:, :quarter], value[:, quarter:half], value[:, half:])
    four, two, odd = [dot3(split(p), read_pair(t), ((1,), (1,))) for p, t in zip(parts, tables)]
    even = jnp.concatenate([four + two, four - two], axis=1)
    return jnp.concatenate([even + odd, even - odd], axis=1)


def power(base, exponent):
    result = None
    while exponent:
        if exponent & 1:
            result = base if result is None else result * base
        base = base * base
        exponent >>= 1
    return result


def recurrence_root(sine):
    half = 0.5 * jnp.sqrt(sine)
    root = jnp.sqrt(1.0 + half * half) - half
    return root * root


def first_sweeps(load, root, top, above, store, levels):
    value = None
    for level in range(levels):
        value = load(level) if value is None else load(level) + root * value
        store[level] = value
    last = value
    value = top * value if above is None else top * value + above
    for level in range(levels - 1, -1, -1):
        value = root * (value - store[level])
    return (value, last)


def second_sweeps(load, start, root, top, above, store, levels, emit):
    value = start
    for level in range(levels):
        value = root * value if load is None else load(level) + root * value
        store[level] = value
    value = top * value if above is None else top * value + above
    for level in range(levels - 1, -1, -1):
        value = root * (value - store[level])
        emit(level, value)


def block_fluxes(ends, weights_ref, vectors_ref, levels, out_ref):
    blocks = len(ends)
    one = lambda dims, b: lax.dot_general(
        vectors_ref[...], b, (dims, ((), ())), precision=lax.Precision.HIGHEST, preferred_element_type=F32
    )
    upper = lower = None
    for block in range(blocks):
        even_next, odd_next = ends[(block + 1) % blocks]
        even, odd = ends[block]
        jump = one(((0,), (0,)), (even_next + odd_next) - (even - odd))
        up, low = weights_ref[0, block] * jump, weights_ref[1, block] * jump
        upper = up if upper is None else upper + up
        lower = low if lower is None else lower + low
    upper, lower = one(((1,), (0,)), upper), one(((1,), (0,)), lower)
    width = upper.shape[1]
    is_even = lax.broadcasted_iota(jnp.int32, (8, width), 0) % 2 == 0
    for level in range(levels):
        up, low = upper[level : level + 1], lower[level : level + 1]
        out_ref[level] = jnp.where(is_even, up - low, -up - low)


def fold_ends(total, out_ref, levels):
    is_even = lax.broadcasted_iota(jnp.int32, total.shape[1:], 0) % 2 == 0
    for level in range(levels):
        value = total[level]
        out_ref[0, level : level + 1] = jnp.sum(jnp.where(is_even, value, 0.0), axis=0, keepdims=True)
        out_ref[1, level : level + 1] = jnp.sum(jnp.where(is_even, 0.0, value), axis=0, keepdims=True)


def forward_kernel(
    levels, tile, ids_ref, w_new_ref, w_hbm, div_ref, t0h, t0l, t1h, t1l, t2h, t2l, ch, cl, root_ref, inv_ref,
    start_ref, top_ref, end_ref, field_hbm, edge_ref, ends_ref, corr_hbm, field, w_rows, above, lowest, store, total,
    sems, w_sems,
):
    step = pl.program_id(0)
    tables = ((t0h, t0l), (t1h, t1l), (t2h, t2l))

    pairs = levels // 2

    @pl.when(step == 0)
    def _():
        loads = chunk_copies(w_hbm, w_rows, w_sems)
        for load in loads:
            load.start()
        above[...] = jnp.zeros_like(above)
        total[...] = jnp.zeros_like(total)
        for load in loads:
            load.wait()
        put_cells(ids_ref, w_new_ref, w_rows)
        pltpu.make_async_copy(w_rows, corr_hbm, sems.at[1]).start()

    row_count = above.shape[0]

    @pl.when(step < pairs)
    def _():
        low = pl.multiple_of((pairs - 1 - step) * 2 * row_count, 2 * row_count)
        value = w_rows[pl.ds(low, 2 * row_count)]
        lower, upper = value[:row_count], value[row_count:]
        source = jnp.concatenate([div_ref[0] + (upper - lower), div_ref[1] + (above[...] - upper)], axis=0)
        modes = periodic_forward(source, tables)
        for k in range(2):
            part = modes[k * row_count : (k + 1) * row_count]
            field[(pairs - 1 - step) * 2 + k] = dot3(read_pair((ch, cl)), split(part))
        above[...] = lower

    @pl.when(step == pairs - 1)
    def _():
        pltpu.make_async_copy(field, field_hbm, sems.at[0]).start()
        lowest[...] = dot3(read_pair((ch, cl)), split(periodic_forward(w_rows[:row_count], tables)))

    @pl.when(step >= pairs)
    def _():
        def rows_of(sub, _):
            here = pl.multiple_of(sub * 8, 8)
            rows = pl.ds(here, 8)
            full = pl.ds(pl.multiple_of((step - pairs) * tile + here, 8), 8)
            root, top = root_ref[rows], top_ref[rows]
            load = lambda level: field[level, full]
            first, _ = first_sweeps(load, root, top, None, store, levels)
            edge_ref[0, rows] = first * inv_ref[rows] - lowest[full]
            weight = end_ref[rows, :1]

            def emit(level, value):
                total[level] += weight * value
                if level == levels - 1:
                    edge_ref[1, rows] = value

            second_sweeps(load, first * start_ref[rows], root, top, None, store, levels, emit)
            return 0

        lax.fori_loop(0, tile // 8, rows_of, 0)

    @pl.when(step == pl.num_programs(0) - 1)
    def _():
        fold_ends(total, ends_ref, levels)
        pltpu.make_async_copy(w_rows, corr_hbm, sems.at[1]).wait()
        pltpu.make_async_copy(field, field_hbm, sems.at[0]).wait()


def edge_kernel(
    levels, edge_ref, ends_ref, weights_ref, vectors_ref, root_ref, inv_ref, start_ref, top_ref, end_ref, ch, cl,
    out_ref, pattern, store, fixed,
):
    block_fluxes(
        [(ends_ref[b, 0], ends_ref[b, 1]) for b in range(ends_ref.shape[0])], weights_ref, vectors_ref, levels, pattern
    )

    def rows_of(sub, _):
        rows = pl.ds(pl.multiple_of(sub * 8, 8), 8)
        root, top = root_ref[rows], top_ref[rows]
        first, last = first_sweeps(lambda level: pattern[level], root, top, None, store, levels)
        weight = end_ref[rows, :1]
        fixed[0, rows] = edge_ref[0, rows] - weight * (first * inv_ref[rows])
        last = last + power(root, levels) * (first * start_ref[rows])
        fixed[1, rows] = edge_ref[1, rows] - weight * (root * (top - 1.0) * last)
        return 0

    lax.fori_loop(0, edge_ref.shape[1] // 8, rows_of, 0)
    for side in range(2):
        value = dot3(split(fixed[side].T), read_pair((ch, cl)))
        out_ref[:, side] = value.reshape(out_ref.shape[0], out_ref.shape[2], out_ref.shape[3])


def join_start(levels, near_top, root):
    square = root * root
    sums = jnp.ones_like(root)
    for _ in range(1, levels):
        sums = 1.0 + square * sums
    whole = power(root, 2 * levels)
    one = 1.0 / (sums + whole)
    near = -root * sums * one
    far = -power(root, levels) * one
    part = power(root, 2 * levels - 1)
    bottom = -root * (1.0 + part) / (1.0 + whole * root)
    pairs = (1.0 + root) * sums
    top = -root * (pairs - part) / (pairs + whole)
    return (near, far, jnp.where(near_top, top, bottom), jnp.where(near_top, bottom, top))


def join_chain(load, blocks, near, far, beta):
    alpha = load(0, 1)
    alphas, betas, heads, slopes = [alpha], [beta], [None], [None]
    for block in range(1, blocks):
        scale = 1.0 / (1.0 - near * beta)
        head = (load(block, 0) - near * alpha) * scale
        slope = far * scale
        alpha = load(block, 1) - far * alpha + far * beta * head
        beta = near + far * beta * slope
        alphas.append(alpha)
        betas.append(beta)
        heads.append(head)
        slopes.append(slope)
    return (alphas, betas, heads, slopes)


def chain_place(block, blocks, half):
    return block + half * (blocks - 1 - 2 * block)


def gather_modes_kernel(levels, px_count, half_ref, edge_ref, t0h, t0l, t1h, t1l, t2h, t2l, root_ref, out_ref, alpha_ref):
    blocks, _, rows, _ = out_ref.shape
    half = half_ref[0]
    for block in range(blocks):
        for side in range(2):
            whole = jnp.concatenate([edge_ref[i * blocks + block, side] for i in range(px_count)], axis=1)
            out_ref[block, side] = whole
    flat = out_ref[...].reshape(blocks * 2 * rows, out_ref.shape[3])
    out_ref[...] = periodic_forward(flat, ((t0h, t0l), (t1h, t1l), (t2h, t2l))).reshape(out_ref.shape)

    def rows_of(sub, _):
        here = pl.ds(pl.multiple_of(sub * 8, 8), 8)
        near, far, own, _ = join_start(levels, half == 1, root_ref[here])
        load = lambda block, outer: out_ref[chain_place(block, blocks, half), jnp.abs(outer - half), here]
        alpha_ref[here] = join_chain(load, blocks, near, far, own)[0][-1]
        return 0

    lax.fori_loop(0, rows // 8, rows_of, 0)


def join_kernel(
    levels, px_count, half_ref, modes_ref, alpha_ref, t0h, t0l, t1h, t1l, t2h, t2l, root_ref, out_ref, modes
):
    blocks, _, rows, _ = modes_ref.shape
    half = half_ref[0]
    width = out_ref.shape[3]

    def rows_of(sub, _):
        here = pl.ds(pl.multiple_of(sub * 8, 8), 8)
        near, far, own, other = join_start(levels, half == 1, root_ref[here])
        load = lambda block, outer: modes_ref[chain_place(block, blocks, half), jnp.abs(outer - half), here]
        alphas, betas, heads, slopes = join_chain(load, blocks, near, far, own)
        for _ in range(1, blocks):
            other = near + far * other * (far / (1.0 - near * other))
        met = alpha_ref[here]
        outer = (met - other * alphas[-1]) / (1.0 - other * betas[-1])
        for block in range(blocks - 1, -1, -1):
            place = chain_place(block, blocks, half)
            modes[place, 1 - half, here] = outer
            if block:
                outer = heads[block] - slopes[block] * outer
                modes[place, half, here] = alphas[block - 1] - betas[block - 1] * outer
            else:
                modes[place, half, here] = jnp.zeros_like(outer)
        return 0

    lax.fori_loop(0, rows // 8, rows_of, 0)
    flat = modes[...].reshape(blocks * 2 * rows, modes.shape[3])
    whole = periodic_inverse(flat, ((t0h, t0l), (t1h, t1l), (t2h, t2l))).reshape(modes.shape)
    for block in range(blocks):
        for side in range(2):
            for i in range(px_count):
                out_ref[i * blocks + block, side] = whole[block, side, :, i * width : (i + 1) * width]


def spread_kernel(levels, joined_ref, ch, cl, root_ref, start_ref, below_ref, top_ref, end_ref, out_ref, ends_ref, store, total):
    kx_width = joined_ref.shape[0] * joined_ref.shape[2]
    for side in range(2):
        value = joined_ref[:, side].reshape(kx_width, joined_ref.shape[3])
        out_ref[side] = dot3(read_pair((ch, cl)), split(value), ((1,), (1,)))
    total[...] = jnp.zeros_like(total)

    def rows_of(sub, _):
        rows = pl.ds(pl.multiple_of(sub * 8, 8), 8)
        root, top = root_ref[rows], top_ref[rows]
        below, above = out_ref[0, rows], out_ref[1, rows]
        start = start_ref[rows] * (power(root, levels) * above) - below_ref[rows] * below
        weight = end_ref[rows, :1]

        def emit(level, value):
            total[level] += weight * value

        second_sweeps(None, start, root, top, above, store, levels, emit)
        return 0

    lax.fori_loop(0, out_ref.shape[1] // 8, rows_of, 0)
    fold_ends(total, ends_ref, levels)


def inverse_kernel(
    levels, tile, place_ref, field_ref, sides_ref, ends_ref, more_ref, weights_ref, vectors_ref, root_ref, start_ref,
    below_ref, top_ref, end_ref, t0h, t0l, t1h, t1l, t2h, t2l, ch, cl, w_ref, roof_ref, out_ref, field, pattern, store,
):
    step = pl.program_id(0)
    tiles = pl.num_programs(0) - levels // 2
    tables = ((t0h, t0l), (t1h, t1l), (t2h, t2l))

    @pl.when(step == 0)
    def _():
        ends = [
            (ends_ref[b, 0] + more_ref[b, 0], ends_ref[b, 1] + more_ref[b, 1]) for b in range(ends_ref.shape[0])
        ]
        block_fluxes(ends, weights_ref, vectors_ref, levels, pattern)

    @pl.when(step < tiles)
    def _():
        def rows_of(sub, _):
            here = pl.multiple_of(sub * 8, 8)
            rows = pl.ds(here, 8)
            full = pl.ds(pl.multiple_of(step * tile + here, 8), 8)
            root, top = root_ref[rows], top_ref[rows]
            below, above = sides_ref[0, rows], sides_ref[1, rows]
            weight = end_ref[rows, :1]
            load = lambda level: field_ref[level, rows] - weight * pattern[level]
            first, _ = first_sweeps(load, root, top, above, store, levels)
            start = start_ref[rows] * first - below_ref[rows] * below
            held = []

            def emit(level, value):
                if held:
                    field[level + 1, full] = held.pop() - value
                held.append(value)

            second_sweeps(load, start, root, top, above, store, levels, emit)
            field[0, full] = jnp.where(place_ref[0] == 0, 0.0, held[0] - below)
            return 0

        lax.fori_loop(0, tile // 8, rows_of, 0)

    @pl.when(step >= tiles)
    def _():
        level = (step - tiles) * 2
        rows_y = [dot3(read_pair((ch, cl)), split(field[level + k])) for k in range(2)]
        slope = periodic_inverse(jnp.concatenate(rows_y, axis=0), tables)
        count = roof_ref.shape[0]
        for k in range(2):
            solid = place_ref[0] * levels + level + k < roof_ref[...]
            out_ref[k] = jnp.where(solid, 0.0, w_ref[k] - slope[k * count : (k + 1) * count])


def facet_places(ids, width):
    safe = jnp.maximum(ids, 0)
    row, column = safe // width, safe % width
    return jnp.stack([row // 8, column // 128, jnp.where(ids < 0, -1, row % 8 * 128 + column % 128)])


def tile_at(places_ref, facet):
    return (
        pl.ds(pl.multiple_of(places_ref[0, facet] * 8, 8), 8),
        pl.ds(pl.multiple_of(places_ref[1, facet] * 128, 128), 128),
    )


def pair_at(places_ref, facet):
    return (
        pl.ds(pl.multiple_of(lax.shift_right_logical(places_ref[0, facet], 1) * 16, 16), 16),
        pl.ds(pl.multiple_of(places_ref[1, facet] * 128, 128), 128),
    )


def pick_cells(ids_ref, ref, rows_ref, flat_ref):
    sublane = lax.broadcasted_iota(jnp.int32, (8, 128), 0)
    position = sublane * 128 + lax.broadcasted_iota(jnp.int32, (8, 128), 1)

    def pick(i, _):
        rows = None
        for lane in range(8):
            facet = i * 8 + lane
            mark = ids_ref[2, facet]
            if ref.dtype == F32:
                tile = ref[tile_at(ids_ref, facet)]
            else:
                both = ref[pair_at(ids_ref, facet)].astype(F32)
                tile = jnp.where(ids_ref[0, facet] & 1 == 0, both[:8], both[8:])
            tile = jnp.where(position == mark, tile, 0.0)
            tile = pltpu.roll(tile, (lane - lax.shift_right_arithmetic(mark, 7)) & 7, 0)
            rows = tile if rows is None else jnp.where(sublane == lane, tile, rows)
        rows_ref[pl.ds(pl.multiple_of(i * 8, 8), 8)] = rows
        return 0

    lax.fori_loop(0, rows_ref.shape[0] // 8, pick, 0)
    ones = jnp.ones((8, 128), F32)
    for group in range(flat_ref.shape[0]):
        rows = rows_ref[group * 128 : (group + 1) * 128]
        flat = lax.dot_general(
            ones, rows, (((1,), (1,)), ((), ())), precision=lax.Precision.HIGHEST, preferred_element_type=F32
        )
        flat_ref[group : group + 1] = flat[:1]


def level_solve_tables(sine, levels, is_first, is_last):
    root = recurrence_root(sine)
    top = jnp.where(is_last, root / (1.0 + root), 0.0)
    square = root * root
    kappa = jnp.zeros_like(root)
    for _ in range(levels):
        kappa = square * (1.0 + kappa)
    decay = power(root, levels)
    inverse = 1.0 / root
    bottom = jnp.where(is_first, 1.0 - inverse, 1.0)
    inv = 1.0 / (1.0 + bottom * (kappa - top * decay * decay))
    return (root, inv, bottom * inv, inv * inverse, top)


CHUNKS = 8


def chunk_copies(source, target, sems):
    rows = source.shape[0] // CHUNKS
    parts = [pl.ds(i * rows, rows) for i in range(CHUNKS)]
    return [pltpu.make_async_copy(source.at[p], target.at[p], sems.at[i]) for i, p in enumerate(parts)]


def gather_kernel(
    levels, ids_ref, ends_ref, w_hbm, temp_hbm, sin_x_ref, sin_y_ref, out_ref, o0, o1, o2, o3, o4, rows_ref, w_ref,
    temp_ref, tables, sems, w_sems, temp_sems,
):
    w_parts, temp_parts = chunk_copies(w_hbm, w_ref, w_sems), chunk_copies(temp_hbm, temp_ref, temp_sems)
    for copy in w_parts:
        copy.start()

    def fill(i, _):
        rows = pl.ds(pl.multiple_of(i * 8, 8), 8)
        sine = sin_y_ref[rows, :1] + sin_x_ref[...]
        for k, value in enumerate(level_solve_tables(sine, levels, ends_ref[0] == 1, ends_ref[1] == 1)):
            tables[k, rows] = value
        return 0

    lax.fori_loop(0, sin_y_ref.shape[0] // 8, fill, 0)
    leaving = [pltpu.make_async_copy(tables.at[k], o, sems.at[k]) for k, o in enumerate((o0, o1, o2, o3, o4))]
    for copy in w_parts:
        copy.wait()
    for copy in temp_parts + leaving:
        copy.start()
    pick_cells(ids_ref, w_ref, rows_ref, out_ref.at[0])
    for copy in temp_parts:
        copy.wait()
    pick_cells(ids_ref, temp_ref, rows_ref, out_ref.at[1])
    for copy in leaving:
        copy.wait()


def put_cells(ids_ref, new_ref, out):
    sublane = lax.broadcasted_iota(jnp.int32, (8, 128), 0)
    position = sublane * 128 + lax.broadcasted_iota(jnp.int32, (8, 128), 1)

    def put(i, _):
        for k in range(8):
            facet = i * 8 + k
            hit = position == ids_ref[2, facet]
            pltpu.store(out.at[tile_at(ids_ref, facet)], jnp.full((8, 128), new_ref[facet]), mask=hit)
        return 0

    lax.fori_loop(0, new_ref.shape[0] // 8, put, 0)


def theta_kernel(ids_ref, new_ref, temp_ref, out_ref, wide):
    rows = temp_ref.shape[0]
    chunk = math.gcd(rows, 64)

    def widen(i, _):
        here = pl.ds(pl.multiple_of(i * chunk, chunk), chunk)
        wide[here] = temp_ref[here].astype(F32)
        return 0

    def narrow(i, _):
        here = pl.ds(pl.multiple_of(i * chunk, chunk), chunk)
        out_ref[here] = wide[here].astype(BF16)
        return 0

    lax.fori_loop(0, rows // chunk, widen, 0)
    put_cells(ids_ref, new_ref, wide)
    lax.fori_loop(0, rows // chunk, narrow, 0)


def by_owner(flat, slots):
    shares = 128 // slots
    return jnp.stack([pltpu.roll(flat, (128 - k * slots) % 128, 1) if k else flat for k in range(shares)])


def exchange_kernel(
    sizes, slots, own_ref, facet_ref, radiation_ref, capacity_ref, drag_ref, heat_ref, back_ref, new_ref, sample, got,
    flux, back, sent, received,
):
    names = ("px", "py_half", "py_low")
    count = sizes[0] * sizes[1] * sizes[2]
    shares = 128 // slots
    places = [lax.axis_index(name) for name in names]
    me = (places[0] * sizes[1] + places[1]) * sizes[2] + places[2]

    def each_peer(act):
        def one(step, _):
            low = lax.rem(places[2] + step, sizes[2])
            rest = lax.div(step, sizes[2])
            middle = lax.rem(places[1] + rest, sizes[1])
            first = lax.rem(places[0] + lax.div(rest, sizes[1]), sizes[0])
            act((first * sizes[1] + middle) * sizes[2] + low, (first, middle, low))
            return 0

        lax.fori_loop(1, count, one, 0)

    def at(ref, device):
        return ref.at[lax.rem(device, shares), lax.div(device, shares)]

    def copy(phase, source, target, peer, device, landing):
        return pltpu.make_async_remote_copy(
            at(source, peer),
            at(target, landing),
            sent.at[phase, peer],
            received.at[phase, landing],
            device_id=device,
            device_id_type=pl.DeviceIdType.MESH,
        )

    def start(phase, source, target):
        each_peer(lambda peer, device: copy(phase, source, target, peer, device, me).start())

    def finish(phase, source, target):
        each_peer(lambda peer, device: copy(phase, source, target, peer, device, peer).wait())

    barrier = pltpu.get_barrier_semaphore()
    each_peer(
        lambda peer, device: pl.semaphore_signal(
            barrier, inc=1, device_id=device, device_id_type=pl.DeviceIdType.MESH
        )
    )
    for i in range(2):
        sample[:, :, i] = by_owner(own_ref[i], slots)
    pl.semaphore_wait(barrier, count - 1)
    start(0, sample, got)
    mine = (lax.rem(me, shares), lax.div(me, shares))
    got[mine] = sample[mine]
    facet, radiation, capacity, drag, heat = [
        by_owner(ref[...], slots) for ref in (facet_ref, radiation_ref, capacity_ref, drag_ref, heat_ref)
    ]
    finish(0, sample, got)
    w_cell, temp_cell = got[:, :, 0], got[:, :, 1]
    speeds = jnp.sqrt(w_cell * w_cell + 0.25)
    heat_flux = heat * speeds * (facet - temp_cell)
    flux[:, :, 0] = drag * speeds * w_cell
    flux[:, :, 1] = heat_flux
    start(1, flux, back)
    back[mine] = flux[mine]
    new_temp = facet + (radiation - heat_flux - 0.5 * facet) / capacity
    finish(1, flux, back)
    lane = lax.broadcasted_iota(jnp.int32, new_temp.shape[1:], 1)
    for target, parts in ((new_ref, new_temp), (back_ref.at[0], back[:, :, 0]), (back_ref.at[1], back[:, :, 1])):
        total = None
        for k in range(shares):
            part = jnp.where(lane < slots, parts[k], 0.0)
            part = pltpu.roll(part, k * slots, 1) if k else part
            total = part if total is None else total + part
        target[...] = total


def near_walls(w_rows, temp_rows, sin_x, sin_y, ends, ids, places, facet_temp, net_radiation, heat_capacity, drag_coef, heat_coef):
    count = ids.shape[0]
    sizes = tuple(lax.axis_size(name) for name in ("px", "py_half", "py_low"))
    slots = count // (sizes[0] * sizes[1] * sizes[2])
    flat = (count // 128, 128)
    rows, width = sin_y.shape[0], sin_x.shape[1]
    own, *tables = pl.pallas_call(
        lambda *refs: gather_kernel(w_rows.shape[0] // rows, *refs),
        out_shape=[jax.ShapeDtypeStruct((2, *flat), F32)] + [jax.ShapeDtypeStruct((rows, width), F32)] * 5,
        in_specs=[SMEM, SMEM, HBM, HBM, VMEM, VMEM],
        out_specs=[VMEM] + [HBM] * 5,
        scratch_shapes=[
            pltpu.VMEM((count, 128), F32),
            pltpu.VMEM(w_rows.shape, F32),
            pltpu.VMEM(temp_rows.shape, BF16),
            pltpu.VMEM((5, rows, width), F32),
            pltpu.SemaphoreType.DMA((5,)),
            pltpu.SemaphoreType.DMA((CHUNKS,)),
            pltpu.SemaphoreType.DMA((CHUNKS,)),
        ],
        compiler_params=PARAMS,
        name="facet_gather",
    )(places, ends, w_rows, temp_rows, sin_x, sin_y)
    tall = (128 // slots, flat[0], 2, 128)
    devices = sizes[0] * sizes[1] * sizes[2]
    returned, new_temp = pl.pallas_call(
        lambda *refs: exchange_kernel(sizes, slots, *refs),
        out_shape=(jax.ShapeDtypeStruct((2, *flat), F32), jax.ShapeDtypeStruct(flat, F32)),
        in_specs=[VMEM] * 6,
        out_specs=(VMEM, VMEM),
        scratch_shapes=[pltpu.VMEM(tall, F32)] * 4 + [pltpu.SemaphoreType.DMA((2, devices))] * 2,
        compiler_params=pltpu.CompilerParams(collective_id=1, has_side_effects=True),
        name="facet_exchange",
    )(own, *[a.reshape(flat) for a in (facet_temp, net_radiation, heat_capacity, drag_coef, heat_coef)])
    own, returned = own.reshape(2, count), returned.reshape(2, count)
    same = ids[:, None] == ids[None, :]
    sums = [jnp.sum(jnp.where(same, returned[i][None, :], 0.0), axis=1) for i in range(2)]
    return (own[0] - sums[0], own[1] + sums[1], new_temp.reshape(count), tables)


def body(
    horiz_div,
    w_star,
    air_temp,
    roof_level,
    facet_cells,
    facet_temp,
    net_radiation,
    heat_capacity,
    drag_coef,
    heat_coef,
):
    levels, rows, width = w_star.shape
    px_count, blocks = lax.axis_size("px"), lax.axis_size("py_low")
    py_count = 2 * blocks
    group = px_count * blocks
    place_x, place_y, half = lax.axis_index("px"), lax.axis_index(("py_half", "py_low")), lax.axis_index("py_half")
    own_kx = width // group
    y_cells = rows * px_count

    w_rows = w_star.reshape(levels * rows, width)
    temp_rows = air_temp.reshape(levels * rows, width)
    ids = facet_cells[0]
    places = facet_places(ids, width)
    x_parts, sin_x = periodic_tables(width)
    y_parts, sin_y = periodic_tables(y_cells)
    cosines, sin_block = cosine_table(rows)
    x_tables = [t for part in x_parts for t in two_halves(part)]
    y_tables = [t for part in y_parts for t in two_halves(part)]
    to_modes, to_rows = two_halves(cosines), two_halves(np.ascontiguousarray(cosines.T))
    sin_x = jnp.asarray(sin_x, F32)

    is_first, is_last = place_y == 0, place_y == py_count - 1
    w_near, temp_near, new_temp, (root, inv, start, from_below, top) = near_walls(
        w_rows,
        temp_rows,
        sin_x[None, :],
        jnp.asarray(np.repeat(sin_block[:, None], 128, axis=1), F32),
        jnp.stack([is_first, is_last]).astype(jnp.int32),
        ids,
        places,
        facet_temp[0],
        net_radiation[0],
        heat_capacity[0],
        drag_coef[0],
        heat_coef[0],
    )

    end = np.where(np.arange(rows) == 0, np.sqrt(1.0 / rows), cosines[:, 0])
    end = jnp.asarray(np.repeat(end[:, None], 128, axis=1), F32)

    vectors, sin_z = level_tables(levels)
    pick = lambda three: jnp.where(is_first, three[0], jnp.where(is_last, three[2], three[1])).astype(F32)
    vectors, sin_z = pick(vectors), pick(sin_z)
    sine_z = sin_z[:, None] + sin_x[None, :]
    size_z = jnp.sqrt(sine_z)
    half_z = 0.5 * size_z
    cosh_z = jnp.sqrt(1.0 + half_z * half_z)
    half_step = cosh_z - half_z
    across = jnp.exp(2.0 * rows * jnp.log(half_step))
    scale = 1.0 / ((1.0 - across * across) * size_z)
    same_end = -half_step * (1.0 + across * across / (half_step * half_step)) * scale
    far_end = -2.0 * across * cosh_z * scale
    turns = np.arange(px_count)
    circulant = jnp.stack(
        [1.0 / (1.0 - 2.0 * same_end + 2.0 * math.cos(2.0 * math.pi * s / px_count) * far_end) for s in turns]
    )
    circulant = lax.optimization_barrier(circulant)
    phase_of = jnp.asarray(np.cos(2.0 * np.pi * turns[:, None] * turns[None, :] / px_count) / px_count, F32)
    offsets = jnp.stack([(place_x - turns) % px_count, (place_x - 1 - turns) % px_count])
    phases = phase_of[offsets]
    weights = jnp.sum(phases[:, :, :, None, None] * circulant[None, None], axis=2)

    mine = place_x * blocks + lax.axis_index("py_low")
    own_sin = lax.dynamic_slice_in_dim(sin_x, mine * own_kx, own_kx)
    join_root = recurrence_root(own_sin[:, None] + jnp.asarray(sin_y, F32)[None, :])

    tile = math.gcd(rows, 32)
    tiles = rows // tile
    flat = lambda i: pl.BlockSpec((tile, width), i)
    fixed = lambda a: pl.BlockSpec(a.shape, lambda i: (0,) * a.ndim)
    pairs = levels // 2
    late = lambda i: (jnp.maximum(i - pairs, 0), 0)
    down = lambda i: (jnp.maximum(pairs - 1 - i, 0), 0, 0)
    slab = pl.BlockSpec((2, rows, width), down)
    end_late = pl.BlockSpec((tile, 128), late)
    ends_shape = jax.ShapeDtypeStruct((2, levels, width), F32)
    field, edges, ends, w_corr = pl.pallas_call(
        lambda *refs: forward_kernel(levels, tile, *refs),
        out_shape=(
            jax.ShapeDtypeStruct(w_star.shape, F32),
            jax.ShapeDtypeStruct((2, rows, width), F32),
            ends_shape,
            jax.ShapeDtypeStruct(w_rows.shape, F32),
        ),
        grid=(pairs + tiles,),
        in_specs=[SMEM, SMEM, HBM, slab] + [fixed(t) for t in (*x_tables, *to_modes)] + [flat(late)] * 4 + [end_late],
        out_specs=(
            HBM,
            pl.BlockSpec((2, tile, width), lambda i: (0, *late(i))),
            fixed(ends_shape),
            HBM,
        ),
        scratch_shapes=[
            pltpu.VMEM(w_star.shape, F32),
            pltpu.VMEM(w_rows.shape, F32),
            pltpu.VMEM((rows, width), F32),
            pltpu.VMEM((rows, width), F32),
            pltpu.VMEM((levels, 8, width), F32),
            pltpu.VMEM((levels, 8, width), F32),
            pltpu.SemaphoreType.DMA((2,)),
            pltpu.SemaphoreType.DMA((CHUNKS,)),
        ],
        compiler_params=PARAMS,
        name="forward",
    )(places, w_near, w_rows, horiz_div, *x_tables, *to_modes, root, inv, start, top, end)

    all_ends = lax.all_gather(ends, "px")
    packed = jax.ShapeDtypeStruct((group, 2, own_kx, rows), F32)
    working = [pltpu.VMEM((levels, 8, width), F32)] * 2
    edges = pl.pallas_call(
        lambda *refs: edge_kernel(levels, *refs),
        out_shape=packed,
        in_specs=[VMEM] * 11,
        out_specs=VMEM,
        scratch_shapes=working + [pltpu.VMEM((2, rows, width), F32)],
        compiler_params=PARAMS,
        name="edges",
    )(edges, all_ends, weights, vectors, root, inv, start, top, end, *to_modes)
    temp_near, edges = lax.optimization_barrier((temp_near, edges))
    theta_new = pl.pallas_call(
        theta_kernel,
        out_shape=jax.ShapeDtypeStruct(temp_rows.shape, BF16),
        in_specs=[SMEM, SMEM, VMEM],
        out_specs=VMEM,
        scratch_shapes=[pltpu.VMEM(temp_rows.shape, F32)],
        compiler_params=PARAMS,
        cost_estimate=pl.CostEstimate(flops=temp_rows.size, bytes_accessed=8 * temp_rows.size, transcendentals=0),
        name="theta",
    )(places, temp_near, temp_rows).reshape(air_temp.shape)
    edges = lax.all_to_all(edges, ("px", "py_low"), split_axis=0, concat_axis=0, tiled=True)
    half_id = half.astype(jnp.int32).reshape(1)
    modes, alpha = pl.pallas_call(
        lambda *refs: gather_modes_kernel(levels, px_count, *refs),
        out_shape=(
            jax.ShapeDtypeStruct((blocks, 2, own_kx, y_cells), F32),
            jax.ShapeDtypeStruct((own_kx, y_cells), F32),
        ),
        in_specs=[SMEM] + [VMEM] * 8,
        out_specs=(VMEM, VMEM),
        compiler_params=PARAMS,
        name="gather_modes",
    )(half_id, edges, *y_tables, join_root)
    alpha = lax.ppermute(alpha, "py_half", [(0, 1), (1, 0)])
    joined = pl.pallas_call(
        lambda *refs: join_kernel(levels, px_count, *refs),
        out_shape=packed,
        in_specs=[SMEM] + [VMEM] * 9,
        out_specs=VMEM,
        scratch_shapes=[pltpu.VMEM((blocks, 2, own_kx, y_cells), F32)],
        compiler_params=PARAMS,
        name="join",
    )(half_id, modes, alpha, *y_tables, join_root)
    joined = lax.all_to_all(joined, ("px", "py_low"), split_axis=0, concat_axis=0, tiled=True)
    sides, more = pl.pallas_call(
        lambda *refs: spread_kernel(levels, *refs),
        out_shape=(jax.ShapeDtypeStruct((2, rows, width), F32), ends_shape),
        in_specs=[VMEM] * 8,
        out_specs=(VMEM, VMEM),
        scratch_shapes=working,
        compiler_params=PARAMS,
        name="spread",
    )(joined, *to_modes, root, start, from_below, top, end)
    more = lax.all_gather(more, "px")

    early = lambda i: (jnp.minimum(i, tiles - 1), 0)
    up = lambda i: (jnp.maximum(i - tiles, 0), 0, 0)
    slab = pl.BlockSpec((2, rows, width), up)
    w_new = pl.pallas_call(
        lambda *refs: inverse_kernel(levels, tile, *refs),
        out_shape=jax.ShapeDtypeStruct(w_star.shape, F32),
        grid=(tiles + pairs,),
        in_specs=[
            SMEM,
            pl.BlockSpec((levels, tile, width), lambda i: (0, *early(i))),
            pl.BlockSpec((2, tile, width), lambda i: (0, *early(i))),
        ]
        + [fixed(a) for a in (all_ends, more, weights, vectors)]
        + [flat(early)] * 4
        + [pl.BlockSpec((tile, 128), early)]
        + [fixed(t) for t in (*x_tables, *to_rows)]
        + [slab, fixed(roof_level)],
        out_specs=slab,
        scratch_shapes=[pltpu.VMEM(w_star.shape, F32)] + working,
        compiler_params=PARAMS,
        name="inverse",
    )(
        place_y.astype(jnp.int32).reshape(1),
        field,
        sides,
        all_ends,
        more,
        weights,
        vectors,
        root,
        start,
        from_below,
        top,
        end,
        *x_tables,
        *to_rows,
        w_corr.reshape(w_star.shape),
        roof_level,
    )
    return (w_new, theta_new, new_temp[None])


def solution(mesh):
    px_count, py_count = mesh.devices.shape
    split_mesh = jax.sharding.Mesh(
        mesh.devices.reshape(px_count, 2, py_count // 2), ("px", "py_half", "py_low")
    )
    py, every = ("py_half", "py_low"), ("px", "py_half", "py_low")
    placed = (P(py, "px", None),) * 3 + (P("px", None),) + (P(every, None),) * 6
    return jax.shard_map(
        body,
        mesh=split_mesh,
        in_specs=placed,
        out_specs=(P(py, "px", None), P(py, "px", None), P(every, None)),
        check_vma=False,
    )
```

```python
import math

import jax
import jax.numpy as jnp
import ml_dtypes
import numpy as np
from jax import lax
from jax.experimental import pallas as pl
from jax.experimental.pallas import tpu as pltpu
from jax.sharding import PartitionSpec as P

F32 = jnp.float32
BF16 = jnp.bfloat16
HBM = pl.BlockSpec(memory_space=pl.ANY)
VMEM = pl.BlockSpec(memory_space=pltpu.VMEM)
SMEM = pl.BlockSpec(memory_space=pltpu.SMEM)
PARAMS = pltpu.CompilerParams(vmem_limit_bytes=58 * 2**20)


def two_halves(table):
    high = table.astype(ml_dtypes.bfloat16)
    low = (table - high.astype(np.float64)).astype(ml_dtypes.bfloat16)
    return (jnp.asarray(high), jnp.asarray(low))


def periodic_tables(size):
    half, quarter = size // 2, size // 4
    groups = (
        (np.arange(0, half + 1, 4), np.arange(4, half, 4), quarter),
        (np.arange(2, half, 4), np.arange(2, half, 4), quarter),
        (np.arange(1, half, 2), np.arange(1, half, 2), half),
    )
    tables, waves = [], []
    for cosines, sines, rows in groups:
        x = np.arange(rows)[:, None]
        norms = np.where((cosines == 0) | (cosines == half), np.sqrt(1.0 / size), np.sqrt(2.0 / size))
        tables.append(
            np.concatenate(
                [
                    norms * np.cos(2.0 * np.pi / size * (x * cosines % size)),
                    np.sqrt(2.0 / size) * np.sin(2.0 * np.pi / size * (x * sines % size)),
                ],
                axis=1,
            )
        )
        waves += [cosines, sines]
    waves = np.concatenate(waves)
    return (tables, 4.0 * np.sin(np.pi * waves / size) ** 2)


def cosine_table(size):
    modes = np.arange(size)[:, None]
    table = np.sqrt(2.0 / size) * np.cos(np.pi * modes * (2 * np.arange(size)[None, :] + 1) / (2 * size))
    table[0] = np.sqrt(1.0 / size)
    return (table, 4.0 * np.sin(np.pi * modes[:, 0] / (2 * size)) ** 2)


def level_tables(size):
    modes, levels = np.arange(size)[None, :], np.arange(size)[:, None]
    omegas = (
        np.pi * (2 * modes + 1) / (2 * size + 1),
        np.pi * (modes + 1) / (size + 1),
        np.pi * (modes + 1) / (size + 0.5),
    )
    vectors = (
        np.cos(omegas[0] * (levels + 0.5)),
        np.sin(omegas[1] * (levels + 1)),
        np.sin(omegas[2] * (levels + 1)),
    )
    vectors = [v / np.sqrt(np.sum(v * v, axis=0, keepdims=True)) for v in vectors]
    return (vectors, [4.0 * np.sin(o[0] / 2) ** 2 for o in omegas])


def split(value):
    high = value.astype(BF16)
    return (high, (value - high.astype(F32)).astype(BF16))


def dot3(left, right, dims=((1,), (0,))):
    one = lambda a, b: lax.dot_general(a, b, (dims, ((), ())), preferred_element_type=F32)
    free = 1 - dims[0][0]
    size = left[0].shape[free]
    both = one(jnp.concatenate(left, axis=free), right[0])
    return both[:size] + (both[size:] + one(left[0], right[1]))


def read_pair(refs):
    return (refs[0][...], refs[1][...])


def periodic_forward(value, tables):
    half, quarter = value.shape[1] // 2, value.shape[1] // 4
    even, odd = value[:, :half] + value[:, half:], value[:, :half] - value[:, half:]
    parts = (even[:, :quarter] + even[:, quarter:], even[:, :quarter] - even[:, quarter:], odd)
    return jnp.concatenate([dot3(split(p), read_pair(t)) for p, t in zip(parts, tables)], axis=1)


def periodic_inverse(value, tables):
    half, quarter = value.shape[1] // 2, value.shape[1] // 4
    parts = (value[:, :quarter], value[:, quarter:half], value[:, half:])
    four, two, odd = [dot3(split(p), read_pair(t), ((1,), (1,))) for p, t in zip(parts, tables)]
    even = jnp.concatenate([four + two, four - two], axis=1)
    return jnp.concatenate([even + odd, even - odd], axis=1)


def power(base, exponent):
    result = None
    while exponent:
        if exponent & 1:
            result = base if result is None else result * base
        base = base * base
        exponent >>= 1
    return result


def recurrence_root(sine):
    half = 0.5 * jnp.sqrt(sine)
    root = jnp.sqrt(1.0 + half * half) - half
    return root * root


def first_sweeps(load, root, top, above, store, levels):
    value = None
    for level in range(levels):
        value = load(level) if value is None else load(level) + root * value
        store[level] = value
    last = value
    value = top * value if above is None else top * value + above
    for level in range(levels - 1, -1, -1):
        value = root * (value - store[level])
    return (value, last)


def second_sweeps(load, start, root, top, above, store, levels, emit):
    value = start
    for level in range(levels):
        value = root * value if load is None else load(level) + root * value
        store[level] = value
    value = top * value if above is None else top * value + above
    for level in range(levels - 1, -1, -1):
        value = root * (value - store[level])
        emit(level, value)


def block_fluxes(ends, weights_ref, vectors_ref, levels, out_ref):
    blocks = len(ends)
    one = lambda dims, b: lax.dot_general(
        vectors_ref[...], b, (dims, ((), ())), precision=lax.Precision.HIGHEST, preferred_element_type=F32
    )
    upper = lower = None
    for block in range(blocks):
        even_next, odd_next = ends[(block + 1) % blocks]
        even, odd = ends[block]
        jump = one(((0,), (0,)), (even_next + odd_next) - (even - odd))
        up, low = weights_ref[0, block] * jump, weights_ref[1, block] * jump
        upper = up if upper is None else upper + up
        lower = low if lower is None else lower + low
    upper, lower = one(((1,), (0,)), upper), one(((1,), (0,)), lower)
    width = upper.shape[1]
    is_even = lax.broadcasted_iota(jnp.int32, (8, width), 0) % 2 == 0
    for level in range(levels):
        up, low = upper[level : level + 1], lower[level : level + 1]
        out_ref[level] = jnp.where(is_even, up - low, -up - low)


def fold_ends(total, out_ref, levels):
    is_even = lax.broadcasted_iota(jnp.int32, total.shape[1:], 0) % 2 == 0
    for level in range(levels):
        value = total[level]
        out_ref[0, level : level + 1] = jnp.sum(jnp.where(is_even, value, 0.0), axis=0, keepdims=True)
        out_ref[1, level : level + 1] = jnp.sum(jnp.where(is_even, 0.0, value), axis=0, keepdims=True)


def forward_kernel(
    levels, tile, ids_ref, w_new_ref, w_hbm, div_ref, t0h, t0l, t1h, t1l, t2h, t2l, ch, cl, root_ref, inv_ref,
    start_ref, top_ref, end_ref, field_hbm, edge_ref, ends_ref, corr_hbm, field, w_rows, above, lowest, store, total,
    sems, w_sems,
):
    step = pl.program_id(0)
    tables = ((t0h, t0l), (t1h, t1l), (t2h, t2l))

    pairs = levels // 2

    @pl.when(step == 0)
    def _():
        loads = chunk_copies(w_hbm, w_rows, w_sems)
        for load in loads:
            load.start()
        above[...] = jnp.zeros_like(above)
        total[...] = jnp.zeros_like(total)
        for load in loads:
            load.wait()
        put_cells(ids_ref, w_new_ref, w_rows)
        pltpu.make_async_copy(w_rows, corr_hbm, sems.at[1]).start()

    row_count = above.shape[0]

    @pl.when(step < pairs)
    def _():
        low = pl.multiple_of((pairs - 1 - step) * 2 * row_count, 2 * row_count)
        value = w_rows[pl.ds(low, 2 * row_count)]
        lower, upper = value[:row_count], value[row_count:]
        source = jnp.concatenate([div_ref[0] + (upper - lower), div_ref[1] + (above[...] - upper)], axis=0)
        modes = periodic_forward(source, tables)
        for k in range(2):
            part = modes[k * row_count : (k + 1) * row_count]
            field[(pairs - 1 - step) * 2 + k] = dot3(read_pair((ch, cl)), split(part))
        above[...] = lower

    @pl.when(step == pairs - 1)
    def _():
        pltpu.make_async_copy(field, field_hbm, sems.at[0]).start()
        lowest[...] = dot3(read_pair((ch, cl)), split(periodic_forward(w_rows[:row_count], tables)))

    @pl.when(step >= pairs)
    def _():
        def rows_of(sub, _):
            here = pl.multiple_of(sub * 8, 8)
            rows = pl.ds(here, 8)
            full = pl.ds(pl.multiple_of((step - pairs) * tile + here, 8), 8)
            root, top = root_ref[rows], top_ref[rows]
            load = lambda level: field[level, full]
            first, _ = first_sweeps(load, root, top, None, store, levels)
            edge_ref[0, rows] = first * inv_ref[rows] - lowest[full]
            weight = end_ref[rows, :1]

            def emit(level, value):
                total[level] += weight * value
                if level == levels - 1:
                    edge_ref[1, rows] = value

            second_sweeps(load, first * start_ref[rows], root, top, None, store, levels, emit)
            return 0

        lax.fori_loop(0, tile // 8, rows_of, 0)

    @pl.when(step == pl.num_programs(0) - 1)
    def _():
        fold_ends(total, ends_ref, levels)
        pltpu.make_async_copy(w_rows, corr_hbm, sems.at[1]).wait()
        pltpu.make_async_copy(field, field_hbm, sems.at[0]).wait()


def edge_kernel(
    levels, edge_ref, ends_ref, weights_ref, vectors_ref, root_ref, inv_ref, start_ref, top_ref, end_ref, ch, cl,
    out_ref, pattern, store, fixed,
):
    block_fluxes(
        [(ends_ref[b, 0], ends_ref[b, 1]) for b in range(ends_ref.shape[0])], weights_ref, vectors_ref, levels, pattern
    )

    def rows_of(sub, _):
        rows = pl.ds(pl.multiple_of(sub * 8, 8), 8)
        root, top = root_ref[rows], top_ref[rows]
        first, last = first_sweeps(lambda level: pattern[level], root, top, None, store, levels)
        weight = end_ref[rows, :1]
        fixed[0, rows] = edge_ref[0, rows] - weight * (first * inv_ref[rows])
        last = last + power(root, levels) * (first * start_ref[rows])
        fixed[1, rows] = edge_ref[1, rows] - weight * (root * (top - 1.0) * last)
        return 0

    lax.fori_loop(0, edge_ref.shape[1] // 8, rows_of, 0)
    for side in range(2):
        value = dot3(split(fixed[side].T), read_pair((ch, cl)))
        out_ref[:, side] = value.reshape(out_ref.shape[0], out_ref.shape[2], out_ref.shape[3])


def join_start(levels, near_top, root):
    square = root * root
    sums = jnp.ones_like(root)
    for _ in range(1, levels):
        sums = 1.0 + square * sums
    whole = power(root, 2 * levels)
    one = 1.0 / (sums + whole)
    near = -root * sums * one
    far = -power(root, levels) * one
    part = power(root, 2 * levels - 1)
    bottom = -root * (1.0 + part) / (1.0 + whole * root)
    pairs = (1.0 + root) * sums
    top = -root * (pairs - part) / (pairs + whole)
    return (near, far, jnp.where(near_top, top, bottom), jnp.where(near_top, bottom, top))


def join_chain(load, blocks, near, far, beta):
    alpha = load(0, 1)
    alphas, betas, heads, slopes = [alpha], [beta], [None], [None]
    for block in range(1, blocks):
        scale = 1.0 / (1.0 - near * beta)
        head = (load(block, 0) - near * alpha) * scale
        slope = far * scale
        alpha = load(block, 1) - far * alpha + far * beta * head
        beta = near + far * beta * slope
        alphas.append(alpha)
        betas.append(beta)
        heads.append(head)
        slopes.append(slope)
    return (alphas, betas, heads, slopes)


def chain_place(block, blocks, half):
    return block + half * (blocks - 1 - 2 * block)


def gather_modes_kernel(levels, px_count, half_ref, edge_ref, t0h, t0l, t1h, t1l, t2h, t2l, root_ref, out_ref, alpha_ref):
    blocks, _, rows, _ = out_ref.shape
    half = half_ref[0]
    for block in range(blocks):
        for side in range(2):
            whole = jnp.concatenate([edge_ref[i * blocks + block, side] for i in range(px_count)], axis=1)
            out_ref[block, side] = whole
    flat = out_ref[...].reshape(blocks * 2 * rows, out_ref.shape[3])
    out_ref[...] = periodic_forward(flat, ((t0h, t0l), (t1h, t1l), (t2h, t2l))).reshape(out_ref.shape)

    def rows_of(sub, _):
        here = pl.ds(pl.multiple_of(sub * 8, 8), 8)
        near, far, own, _ = join_start(levels, half == 1, root_ref[here])
        load = lambda block, outer: out_ref[chain_place(block, blocks, half), jnp.abs(outer - half), here]
        alpha_ref[here] = join_chain(load, blocks, near, far, own)[0][-1]
        return 0

    lax.fori_loop(0, rows // 8, rows_of, 0)


def join_kernel(
    levels, px_count, half_ref, modes_ref, alpha_ref, t0h, t0l, t1h, t1l, t2h, t2l, root_ref, out_ref, modes
):
    blocks, _, rows, _ = modes_ref.shape
    half = half_ref[0]
    width = out_ref.shape[3]

    def rows_of(sub, _):
        here = pl.ds(pl.multiple_of(sub * 8, 8), 8)
        near, far, own, other = join_start(levels, half == 1, root_ref[here])
        load = lambda block, outer: modes_ref[chain_place(block, blocks, half), jnp.abs(outer - half), here]
        alphas, betas, heads, slopes = join_chain(load, blocks, near, far, own)
        for _ in range(1, blocks):
            other = near + far * other * (far / (1.0 - near * other))
        met = alpha_ref[here]
        outer = (met - other * alphas[-1]) / (1.0 - other * betas[-1])
        for block in range(blocks - 1, -1, -1):
            place = chain_place(block, blocks, half)
            modes[place, 1 - half, here] = outer
            if block:
                outer = heads[block] - slopes[block] * outer
                modes[place, half, here] = alphas[block - 1] - betas[block - 1] * outer
            else:
                modes[place, half, here] = jnp.zeros_like(outer)
        return 0

    lax.fori_loop(0, rows // 8, rows_of, 0)
    flat = modes[...].reshape(blocks * 2 * rows, modes.shape[3])
    whole = periodic_inverse(flat, ((t0h, t0l), (t1h, t1l), (t2h, t2l))).reshape(modes.shape)
    for block in range(blocks):
        for side in range(2):
            for i in range(px_count):
                out_ref[i * blocks + block, side] = whole[block, side, :, i * width : (i + 1) * width]


def spread_kernel(levels, joined_ref, ch, cl, root_ref, start_ref, below_ref, top_ref, end_ref, out_ref, ends_ref, store, total):
    kx_width = joined_ref.shape[0] * joined_ref.shape[2]
    for side in range(2):
        value = joined_ref[:, side].reshape(kx_width, joined_ref.shape[3])
        out_ref[side] = dot3(read_pair((ch, cl)), split(value), ((1,), (1,)))
    total[...] = jnp.zeros_like(total)

    def rows_of(sub, _):
        rows = pl.ds(pl.multiple_of(sub * 8, 8), 8)
        root, top = root_ref[rows], top_ref[rows]
        below, above = out_ref[0, rows], out_ref[1, rows]
        start = start_ref[rows] * (power(root, levels) * above) - below_ref[rows] * below
        weight = end_ref[rows, :1]

        def emit(level, value):
            total[level] += weight * value

        second_sweeps(None, start, root, top, above, store, levels, emit)
        return 0

    lax.fori_loop(0, out_ref.shape[1] // 8, rows_of, 0)
    fold_ends(total, ends_ref, levels)


def inverse_kernel(
    levels, tile, place_ref, field_ref, sides_ref, ends_ref, more_ref, weights_ref, vectors_ref, root_ref, start_ref,
    below_ref, top_ref, end_ref, t0h, t0l, t1h, t1l, t2h, t2l, ch, cl, w_ref, roof_ref, out_ref, field, pattern, store,
):
    step = pl.program_id(0)
    tiles = pl.num_programs(0) - levels // 2
    tables = ((t0h, t0l), (t1h, t1l), (t2h, t2l))

    @pl.when(step == 0)
    def _():
        ends = [
            (ends_ref[b, 0] + more_ref[b, 0], ends_ref[b, 1] + more_ref[b, 1]) for b in range(ends_ref.shape[0])
        ]
        block_fluxes(ends, weights_ref, vectors_ref, levels, pattern)

    @pl.when(step < tiles)
    def _():
        def rows_of(sub, _):
            here = pl.multiple_of(sub * 8, 8)
            rows = pl.ds(here, 8)
            full = pl.ds(pl.multiple_of(step * tile + here, 8), 8)
            root, top = root_ref[rows], top_ref[rows]
            below, above = sides_ref[0, rows], sides_ref[1, rows]
            weight = end_ref[rows, :1]
            load = lambda level: field_ref[level, rows] - weight * pattern[level]
            first, _ = first_sweeps(load, root, top, above, store, levels)
            start = start_ref[rows] * first - below_ref[rows] * below
            held = []

            def emit(level, value):
                if held:
                    field[level + 1, full] = held.pop() - value
                held.append(value)

            second_sweeps(load, start, root, top, above, store, levels, emit)
            field[0, full] = jnp.where(place_ref[0] == 0, 0.0, held[0] - below)
            return 0

        lax.fori_loop(0, tile // 8, rows_of, 0)

    @pl.when(step >= tiles)
    def _():
        level = (step - tiles) * 2
        rows_y = [dot3(read_pair((ch, cl)), split(field[level + k])) for k in range(2)]
        slope = periodic_inverse(jnp.concatenate(rows_y, axis=0), tables)
        count = roof_ref.shape[0]
        for k in range(2):
            solid = place_ref[0] * levels + level + k < roof_ref[...]
            out_ref[k] = jnp.where(solid, 0.0, w_ref[k] - slope[k * count : (k + 1) * count])


def facet_places(ids, width):
    safe = jnp.maximum(ids, 0)
    row, column = safe // width, safe % width
    return jnp.stack([row // 8, column // 128, jnp.where(ids < 0, -1, row % 8 * 128 + column % 128)])


def tile_at(places_ref, facet):
    return (
        pl.ds(pl.multiple_of(places_ref[0, facet] * 8, 8), 8),
        pl.ds(pl.multiple_of(places_ref[1, facet] * 128, 128), 128),
    )


def pair_at(places_ref, facet):
    return (
        pl.ds(pl.multiple_of(lax.shift_right_logical(places_ref[0, facet], 1) * 16, 16), 16),
        pl.ds(pl.multiple_of(places_ref[1, facet] * 128, 128), 128),
    )


def pick_cells(ids_ref, ref, rows_ref, flat_ref):
    sublane = lax.broadcasted_iota(jnp.int32, (8, 128), 0)
    position = sublane * 128 + lax.broadcasted_iota(jnp.int32, (8, 128), 1)

    def pick(i, _):
        rows = None
        for lane in range(8):
            facet = i * 8 + lane
            mark = ids_ref[2, facet]
            if ref.dtype == F32:
                tile = ref[tile_at(ids_ref, facet)]
            else:
                both = ref[pair_at(ids_ref, facet)].astype(F32)
                tile = jnp.where(ids_ref[0, facet] & 1 == 0, both[:8], both[8:])
            tile = jnp.where(position == mark, tile, 0.0)
            tile = pltpu.roll(tile, (lane - lax.shift_right_arithmetic(mark, 7)) & 7, 0)
            rows = tile if rows is None else jnp.where(sublane == lane, tile, rows)
        rows_ref[pl.ds(pl.multiple_of(i * 8, 8), 8)] = rows

    group_count = rows_ref.shape[0] // 8
    per_trip = math.gcd(group_count, 8)

    def trip(i, _):
        for k in range(per_trip):
            pick(i * per_trip + k, None)
        return 0

    lax.fori_loop(0, group_count // per_trip, trip, 0)
    ones = jnp.ones((8, 128), F32)
    for group in range(flat_ref.shape[0]):
        rows = rows_ref[group * 128 : (group + 1) * 128]
        flat = lax.dot_general(
            ones, rows, (((1,), (1,)), ((), ())), precision=lax.Precision.HIGHEST, preferred_element_type=F32
        )
        flat_ref[group : group + 1] = flat[:1]


def level_solve_tables(sine, levels, is_first, is_last):
    root = recurrence_root(sine)
    top = jnp.where(is_last, root / (1.0 + root), 0.0)
    square = root * root
    kappa = jnp.zeros_like(root)
    for _ in range(levels):
        kappa = square * (1.0 + kappa)
    decay = power(root, levels)
    inverse = 1.0 / root
    bottom = jnp.where(is_first, 1.0 - inverse, 1.0)
    inv = 1.0 / (1.0 + bottom * (kappa - top * decay * decay))
    return (root, inv, bottom * inv, inv * inverse, top)


CHUNKS = 8


def chunk_copies(source, target, sems):
    rows = source.shape[0] // CHUNKS
    parts = [pl.ds(i * rows, rows) for i in range(CHUNKS)]
    return [pltpu.make_async_copy(source.at[p], target.at[p], sems.at[i]) for i, p in enumerate(parts)]


def gather_kernel(
    levels, ids_ref, ends_ref, w_hbm, sin_x_ref, sin_y_ref, out_ref, o0, o1, o2, o3, o4, rows_ref, w_ref, tables, sems,
    w_sems,
):
    w_parts = chunk_copies(w_hbm, w_ref, w_sems)
    for copy in w_parts:
        copy.start()

    def fill(i, _):
        rows = pl.ds(pl.multiple_of(i * 8, 8), 8)
        sine = sin_y_ref[rows, :1] + sin_x_ref[...]
        for k, value in enumerate(level_solve_tables(sine, levels, ends_ref[0] == 1, ends_ref[1] == 1)):
            tables[k, rows] = value
        return 0

    lax.fori_loop(0, sin_y_ref.shape[0] // 8, fill, 0)
    leaving = [pltpu.make_async_copy(tables.at[k], o, sems.at[k]) for k, o in enumerate((o0, o1, o2, o3, o4))]
    for copy in w_parts:
        copy.wait()
    for copy in leaving:
        copy.start()
    pick_cells(ids_ref, w_ref, rows_ref, out_ref)
    for copy in leaving:
        copy.wait()


def gather_temp_kernel(ids_ref, temp_ref, out_ref, rows_ref):
    pick_cells(ids_ref, temp_ref, rows_ref, out_ref)


def put_cells(ids_ref, new_ref, out):
    sublane = lax.broadcasted_iota(jnp.int32, (8, 128), 0)
    position = sublane * 128 + lax.broadcasted_iota(jnp.int32, (8, 128), 1)

    per_trip = math.gcd(new_ref.shape[0], 32)

    def put(i, _):
        for k in range(per_trip):
            facet = i * per_trip + k
            hit = position == ids_ref[2, facet]
            pltpu.store(out.at[tile_at(ids_ref, facet)], jnp.full((8, 128), new_ref[facet]), mask=hit)
        return 0

    lax.fori_loop(0, new_ref.shape[0] // per_trip, put, 0)


def theta_kernel(ids_ref, new_ref, temp_ref, out_ref, wide):
    rows = temp_ref.shape[0]
    chunk = math.gcd(rows, 64)

    def widen(i, _):
        here = pl.ds(pl.multiple_of(i * chunk, chunk), chunk)
        wide[here] = temp_ref[here].astype(F32)
        return 0

    def narrow(i, _):
        here = pl.ds(pl.multiple_of(i * chunk, chunk), chunk)
        out_ref[here] = wide[here].astype(BF16)
        return 0

    lax.fori_loop(0, rows // chunk, widen, 0)
    put_cells(ids_ref, new_ref, wide)
    lax.fori_loop(0, rows // chunk, narrow, 0)


def by_owner(flat, slots):
    shares = 128 // slots
    return jnp.stack([pltpu.roll(flat, (128 - k * slots) % 128, 1) if k else flat for k in range(shares)])


class Links:
    def __init__(self, sizes, slots, sent, received):
        names = ("px", "py_half", "py_low")
        self.sizes, self.shares = sizes, 128 // slots
        self.count = sizes[0] * sizes[1] * sizes[2]
        self.places = [lax.axis_index(name) for name in names]
        self.me = (self.places[0] * sizes[1] + self.places[1]) * sizes[2] + self.places[2]
        self.mine = (lax.rem(self.me, self.shares), lax.div(self.me, self.shares))
        self.sent, self.received = sent, received

    def each_peer(self, act):
        sizes, places = self.sizes, self.places

        def one(step, _):
            low = lax.rem(places[2] + step, sizes[2])
            rest = lax.div(step, sizes[2])
            middle = lax.rem(places[1] + rest, sizes[1])
            first = lax.rem(places[0] + lax.div(rest, sizes[1]), sizes[0])
            act((first * sizes[1] + middle) * sizes[2] + low, (first, middle, low))
            return 0

        lax.fori_loop(1, self.count, one, 0)

    def copy(self, phase, source, target, peer, device, landing):
        at = lambda ref, index: ref.at[lax.rem(index, self.shares), lax.div(index, self.shares)]
        return pltpu.make_async_remote_copy(
            at(source, peer),
            at(target, landing),
            self.sent.at[phase, peer],
            self.received.at[phase, landing],
            device_id=device,
            device_id_type=pl.DeviceIdType.MESH,
        )

    def greet(self):
        barrier = pltpu.get_barrier_semaphore()
        self.each_peer(
            lambda peer, device: pl.semaphore_signal(
                barrier, inc=1, device_id=device, device_id_type=pl.DeviceIdType.MESH
            )
        )
        return barrier

    def start(self, phase, source, target):
        self.each_peer(lambda peer, device: self.copy(phase, source, target, peer, device, self.me).start())
        target[self.mine] = source[self.mine]

    def finish(self, phase, source, target):
        self.each_peer(lambda peer, device: self.copy(phase, source, target, peer, device, peer).wait())


def from_owners(parts, slots):
    lane = lax.broadcasted_iota(jnp.int32, parts.shape[1:], 1)
    total = None
    for k in range(parts.shape[0]):
        part = jnp.where(lane < slots, parts[k], 0.0)
        part = pltpu.roll(part, k * slots, 1) if k else part
        total = part if total is None else total + part
    return total


def stress_kernel(
    sizes, slots, own_ref, facet_ref, drag_ref, heat_ref, back_ref, w_ref, sample, got, flux, back, sent, received
):
    links = Links(sizes, slots, sent, received)
    barrier = links.greet()
    sample[:, :, 0] = by_owner(own_ref[...], slots)
    pl.semaphore_wait(barrier, links.count - 1)
    links.start(0, sample, got)
    facet, drag, heat = [by_owner(ref[...], slots) for ref in (facet_ref, drag_ref, heat_ref)]
    links.finish(0, sample, got)
    w_cell = got[:, :, 0]
    speeds = jnp.sqrt(w_cell * w_cell + 0.25)
    flux[:, :, 0] = drag * speeds * w_cell
    flux[:, :, 1] = heat * speeds
    flux[:, :, 2] = facet
    links.start(1, flux, back)
    w_ref[...] = w_cell
    links.finish(1, flux, back)
    for k in range(3):
        back_ref[k] = from_owners(back[:, :, k], slots)


def facet_temp_kernel(
    sizes, slots, own_ref, facet_ref, radiation_ref, capacity_ref, heat_ref, w_ref, new_ref, sample, got, sent, received
):
    links = Links(sizes, slots, sent, received)
    barrier = links.greet()
    sample[:, :, 0] = by_owner(own_ref[...], slots)
    pl.semaphore_wait(barrier, links.count - 1)
    links.start(0, sample, got)
    facet, radiation, capacity, heat = [
        by_owner(ref[...], slots) for ref in (facet_ref, radiation_ref, capacity_ref, heat_ref)
    ]
    w_cell = w_ref[...]
    scale = heat * jnp.sqrt(w_cell * w_cell + 0.25)
    links.finish(0, sample, got)
    flux = scale * (facet - got[:, :, 0])
    new_ref[...] = from_owners(facet + (radiation - flux - 0.5 * facet) / capacity, slots)


def facet_sums(ids, returned):
    same = ids[:, None] == ids[None, :]
    return jnp.sum(jnp.where(same, returned.reshape(1, -1), 0.0), axis=1)


def near_walls(w_rows, sin_x, sin_y, ends, ids, places, facet_temp, drag_coef, heat_coef):
    count = ids.shape[0]
    sizes = tuple(lax.axis_size(name) for name in ("px", "py_half", "py_low"))
    slots = count // (sizes[0] * sizes[1] * sizes[2])
    flat = (count // 128, 128)
    rows, width = sin_y.shape[0], sin_x.shape[1]
    own, *tables = pl.pallas_call(
        lambda *refs: gather_kernel(w_rows.shape[0] // rows, *refs),
        out_shape=[jax.ShapeDtypeStruct(flat, F32)] + [jax.ShapeDtypeStruct((rows, width), F32)] * 5,
        in_specs=[SMEM, SMEM, HBM, VMEM, VMEM],
        out_specs=[VMEM] + [HBM] * 5,
        scratch_shapes=[
            pltpu.VMEM((count, 128), F32),
            pltpu.VMEM(w_rows.shape, F32),
            pltpu.VMEM((5, rows, width), F32),
            pltpu.SemaphoreType.DMA((5,)),
            pltpu.SemaphoreType.DMA((CHUNKS,)),
        ],
        compiler_params=PARAMS,
        name="facet_gather",
    )(places, ends, w_rows, sin_x, sin_y)
    by_rows = (128 // slots, flat[0], 128)
    tall = lambda values: pltpu.VMEM((128 // slots, flat[0], values, 128), F32)
    returned, w_cell = pl.pallas_call(
        lambda *refs: stress_kernel(sizes, slots, *refs),
        out_shape=(jax.ShapeDtypeStruct((3, *flat), F32), jax.ShapeDtypeStruct(by_rows, F32)),
        in_specs=[VMEM] * 4,
        out_specs=(VMEM, VMEM),
        scratch_shapes=[tall(1), tall(1), tall(3), tall(3)]
        + [pltpu.SemaphoreType.DMA((2, sizes[0] * sizes[1] * sizes[2]))] * 2,
        compiler_params=pltpu.CompilerParams(collective_id=1, has_side_effects=True),
        name="stress_exchange",
    )(own, facet_temp.reshape(flat), drag_coef.reshape(flat), heat_coef.reshape(flat))
    return (own.reshape(count) - facet_sums(ids, returned[0]), returned, w_cell, tables)


def warm_air(temp_rows, ids, places, returned, w_cell, facet_temp, net_radiation, heat_capacity, heat_coef):
    count = ids.shape[0]
    sizes = tuple(lax.axis_size(name) for name in ("px", "py_half", "py_low"))
    slots = count // (sizes[0] * sizes[1] * sizes[2])
    flat = (count // 128, 128)
    own = pl.pallas_call(
        gather_temp_kernel,
        out_shape=jax.ShapeDtypeStruct(flat, F32),
        in_specs=[SMEM, VMEM],
        out_specs=VMEM,
        scratch_shapes=[pltpu.VMEM((count, 128), F32)],
        compiler_params=PARAMS,
        cost_estimate=pl.CostEstimate(flops=0, bytes_accessed=4 * temp_rows.size, transcendentals=0),
        name="temp_gather",
    )(places, temp_rows)
    tall = pltpu.VMEM((128 // slots, flat[0], 1, 128), F32)
    new_temp = pl.pallas_call(
        lambda *refs: facet_temp_kernel(sizes, slots, *refs),
        out_shape=jax.ShapeDtypeStruct(flat, F32),
        in_specs=[VMEM] * 6,
        out_specs=VMEM,
        scratch_shapes=[tall] * 2 + [pltpu.SemaphoreType.DMA((1, sizes[0] * sizes[1] * sizes[2]))] * 2,
        compiler_params=pltpu.CompilerParams(collective_id=2, has_side_effects=True),
        cost_estimate=pl.CostEstimate(flops=0, bytes_accessed=2**24, transcendentals=0),
        name="facet_temp",
    )(own, *[a.reshape(flat) for a in (facet_temp, net_radiation, heat_capacity, heat_coef)], w_cell)
    heat_flux = returned[1] * (returned[2] - own)
    return (own.reshape(count) + facet_sums(ids, heat_flux), new_temp.reshape(count))


def body(
    horiz_div,
    w_star,
    air_temp,
    roof_level,
    facet_cells,
    facet_temp,
    net_radiation,
    heat_capacity,
    drag_coef,
    heat_coef,
):
    levels, rows, width = w_star.shape
    px_count, blocks = lax.axis_size("px"), lax.axis_size("py_low")
    py_count = 2 * blocks
    group = px_count * blocks
    place_x, place_y, half = lax.axis_index("px"), lax.axis_index(("py_half", "py_low")), lax.axis_index("py_half")
    own_kx = width // group
    y_cells = rows * px_count

    w_rows = w_star.reshape(levels * rows, width)
    temp_rows = air_temp.reshape(levels * rows, width)
    ids = facet_cells[0]
    places = facet_places(ids, width)
    x_parts, sin_x = periodic_tables(width)
    y_parts, sin_y = periodic_tables(y_cells)
    cosines, sin_block = cosine_table(rows)
    x_tables = [t for part in x_parts for t in two_halves(part)]
    y_tables = [t for part in y_parts for t in two_halves(part)]
    to_modes, to_rows = two_halves(cosines), two_halves(np.ascontiguousarray(cosines.T))
    sin_x = jnp.asarray(sin_x, F32)

    is_first, is_last = place_y == 0, place_y == py_count - 1
    w_near, returned, w_cell, (root, inv, start, from_below, top) = near_walls(
        w_rows,
        sin_x[None, :],
        jnp.asarray(np.repeat(sin_block[:, None], 128, axis=1), F32),
        jnp.stack([is_first, is_last]).astype(jnp.int32),
        ids,
        places,
        facet_temp[0],
        drag_coef[0],
        heat_coef[0],
    )

    end = np.where(np.arange(rows) == 0, np.sqrt(1.0 / rows), cosines[:, 0])
    end = jnp.asarray(np.repeat(end[:, None], 128, axis=1), F32)

    vectors, sin_z = level_tables(levels)
    pick = lambda three: jnp.where(is_first, three[0], jnp.where(is_last, three[2], three[1])).astype(F32)
    vectors, sin_z = pick(vectors), pick(sin_z)
    sine_z = sin_z[:, None] + sin_x[None, :]
    size_z = jnp.sqrt(sine_z)
    half_z = 0.5 * size_z
    cosh_z = jnp.sqrt(1.0 + half_z * half_z)
    half_step = cosh_z - half_z
    across = jnp.exp(2.0 * rows * jnp.log(half_step))
    scale = 1.0 / ((1.0 - across * across) * size_z)
    same_end = -half_step * (1.0 + across * across / (half_step * half_step)) * scale
    far_end = -2.0 * across * cosh_z * scale
    turns = np.arange(px_count)
    circulant = jnp.stack(
        [1.0 / (1.0 - 2.0 * same_end + 2.0 * math.cos(2.0 * math.pi * s / px_count) * far_end) for s in turns]
    )
    circulant = lax.optimization_barrier(circulant)
    phase_of = jnp.asarray(np.cos(2.0 * np.pi * turns[:, None] * turns[None, :] / px_count) / px_count, F32)
    offsets = jnp.stack([(place_x - turns) % px_count, (place_x - 1 - turns) % px_count])
    phases = phase_of[offsets]
    weights = jnp.sum(phases[:, :, :, None, None] * circulant[None, None], axis=2)

    mine = place_x * blocks + lax.axis_index("py_low")
    own_sin = lax.dynamic_slice_in_dim(sin_x, mine * own_kx, own_kx)
    join_root = recurrence_root(own_sin[:, None] + jnp.asarray(sin_y, F32)[None, :])

    tile = math.gcd(rows, 32)
    tiles = rows // tile
    flat = lambda i: pl.BlockSpec((tile, width), i)
    fixed = lambda a: pl.BlockSpec(a.shape, lambda i: (0,) * a.ndim)
    pairs = levels // 2
    late = lambda i: (jnp.maximum(i - pairs, 0), 0)
    down = lambda i: (jnp.maximum(pairs - 1 - i, 0), 0, 0)
    slab = pl.BlockSpec((2, rows, width), down)
    end_late = pl.BlockSpec((tile, 128), late)
    ends_shape = jax.ShapeDtypeStruct((2, levels, width), F32)
    field, edges, ends, w_corr = pl.pallas_call(
        lambda *refs: forward_kernel(levels, tile, *refs),
        out_shape=(
            jax.ShapeDtypeStruct(w_star.shape, F32),
            jax.ShapeDtypeStruct((2, rows, width), F32),
            ends_shape,
            jax.ShapeDtypeStruct(w_rows.shape, F32),
        ),
        grid=(pairs + tiles,),
        in_specs=[SMEM, SMEM, HBM, slab] + [fixed(t) for t in (*x_tables, *to_modes)] + [flat(late)] * 4 + [end_late],
        out_specs=(
            HBM,
            pl.BlockSpec((2, tile, width), lambda i: (0, *late(i))),
            fixed(ends_shape),
            HBM,
        ),
        scratch_shapes=[
            pltpu.VMEM(w_star.shape, F32),
            pltpu.VMEM(w_rows.shape, F32),
            pltpu.VMEM((rows, width), F32),
            pltpu.VMEM((rows, width), F32),
            pltpu.VMEM((levels, 8, width), F32),
            pltpu.VMEM((levels, 8, width), F32),
            pltpu.SemaphoreType.DMA((2,)),
            pltpu.SemaphoreType.DMA((CHUNKS,)),
        ],
        compiler_params=PARAMS,
        name="forward",
    )(places, w_near, w_rows, horiz_div, *x_tables, *to_modes, root, inv, start, top, end)

    all_ends = lax.all_gather(ends, "px")
    packed = jax.ShapeDtypeStruct((group, 2, own_kx, rows), F32)
    working = [pltpu.VMEM((levels, 8, width), F32)] * 2
    edges = pl.pallas_call(
        lambda *refs: edge_kernel(levels, *refs),
        out_shape=packed,
        in_specs=[VMEM] * 11,
        out_specs=VMEM,
        scratch_shapes=working + [pltpu.VMEM((2, rows, width), F32)],
        compiler_params=PARAMS,
        name="edges",
    )(edges, all_ends, weights, vectors, root, inv, start, top, end, *to_modes)
    w_cell, edges = lax.optimization_barrier((w_cell, edges))
    places_late, edges = lax.optimization_barrier((places, edges))
    temp_near, new_temp = warm_air(
        temp_rows,
        ids,
        places_late,
        returned,
        w_cell,
        facet_temp[0],
        net_radiation[0],
        heat_capacity[0],
        heat_coef[0],
    )
    edges = lax.all_to_all(edges, ("px", "py_low"), split_axis=0, concat_axis=0, tiled=True)
    edges, temp_near, new_temp = lax.optimization_barrier((edges, temp_near, new_temp))
    half_id = half.astype(jnp.int32).reshape(1)
    modes, alpha = pl.pallas_call(
        lambda *refs: gather_modes_kernel(levels, px_count, *refs),
        out_shape=(
            jax.ShapeDtypeStruct((blocks, 2, own_kx, y_cells), F32),
            jax.ShapeDtypeStruct((own_kx, y_cells), F32),
        ),
        in_specs=[SMEM] + [VMEM] * 8,
        out_specs=(VMEM, VMEM),
        compiler_params=PARAMS,
        name="gather_modes",
    )(half_id, edges, *y_tables, join_root)
    alpha = lax.ppermute(alpha, "py_half", [(0, 1), (1, 0)])
    joined = pl.pallas_call(
        lambda *refs: join_kernel(levels, px_count, *refs),
        out_shape=packed,
        in_specs=[SMEM] + [VMEM] * 9,
        out_specs=VMEM,
        scratch_shapes=[pltpu.VMEM((blocks, 2, own_kx, y_cells), F32)],
        compiler_params=PARAMS,
        name="join",
    )(half_id, modes, alpha, *y_tables, join_root)
    joined, temp_near = lax.optimization_barrier((joined, temp_near))
    theta_new = pl.pallas_call(
        theta_kernel,
        out_shape=jax.ShapeDtypeStruct(temp_rows.shape, BF16),
        in_specs=[SMEM, SMEM, VMEM],
        out_specs=VMEM,
        scratch_shapes=[pltpu.VMEM(temp_rows.shape, F32)],
        compiler_params=PARAMS,
        cost_estimate=pl.CostEstimate(flops=temp_rows.size, bytes_accessed=8 * temp_rows.size, transcendentals=0),
        name="theta",
    )(places, temp_near, temp_rows).reshape(air_temp.shape)
    joined = lax.all_to_all(joined, ("px", "py_low"), split_axis=0, concat_axis=0, tiled=True)
    sides, more = pl.pallas_call(
        lambda *refs: spread_kernel(levels, *refs),
        out_shape=(jax.ShapeDtypeStruct((2, rows, width), F32), ends_shape),
        in_specs=[VMEM] * 8,
        out_specs=(VMEM, VMEM),
        scratch_shapes=working,
        compiler_params=PARAMS,
        name="spread",
    )(joined, *to_modes, root, start, from_below, top, end)
    more = lax.all_gather(more, "px")

    early = lambda i: (jnp.minimum(i, tiles - 1), 0)
    up = lambda i: (jnp.maximum(i - tiles, 0), 0, 0)
    slab = pl.BlockSpec((2, rows, width), up)
    w_new = pl.pallas_call(
        lambda *refs: inverse_kernel(levels, tile, *refs),
        out_shape=jax.ShapeDtypeStruct(w_star.shape, F32),
        grid=(tiles + pairs,),
        in_specs=[
            SMEM,
            pl.BlockSpec((levels, tile, width), lambda i: (0, *early(i))),
            pl.BlockSpec((2, tile, width), lambda i: (0, *early(i))),
        ]
        + [fixed(a) for a in (all_ends, more, weights, vectors)]
        + [flat(early)] * 4
        + [pl.BlockSpec((tile, 128), early)]
        + [fixed(t) for t in (*x_tables, *to_rows)]
        + [slab, fixed(roof_level)],
        out_specs=slab,
        scratch_shapes=[pltpu.VMEM(w_star.shape, F32)] + working,
        compiler_params=PARAMS,
        name="inverse",
    )(
        place_y.astype(jnp.int32).reshape(1),
        field,
        sides,
        all_ends,
        more,
        weights,
        vectors,
        root,
        start,
        from_below,
        top,
        end,
        *x_tables,
        *to_rows,
        w_corr.reshape(w_star.shape),
        roof_level,
    )
    return (w_new, theta_new, new_temp[None])


def solution(mesh):
    px_count, py_count = mesh.devices.shape
    split_mesh = jax.sharding.Mesh(
        mesh.devices.reshape(px_count, 2, py_count // 2), ("px", "py_half", "py_low")
    )
    py, every = ("py_half", "py_low"), ("px", "py_half", "py_low")
    placed = (P(py, "px", None),) * 3 + (P("px", None),) + (P(every, None),) * 6
    return jax.shard_map(
        body,
        mesh=split_mesh,
        in_specs=placed,
        out_specs=(P(py, "px", None), P(py, "px", None), P(every, None)),
        check_vma=False,
    )
```

```python
import math

import jax
import jax.numpy as jnp
import ml_dtypes
import numpy as np
from jax import lax
from jax.experimental import pallas as pl
from jax.experimental.pallas import tpu as pltpu
from jax.sharding import PartitionSpec as P

F32 = jnp.float32
BF16 = jnp.bfloat16
HBM = pl.BlockSpec(memory_space=pl.ANY)
VMEM = pl.BlockSpec(memory_space=pltpu.VMEM)
SMEM = pl.BlockSpec(memory_space=pltpu.SMEM)
PARAMS = pltpu.CompilerParams(vmem_limit_bytes=58 * 2**20)


def two_halves(table):
    high = table.astype(ml_dtypes.bfloat16)
    low = (table - high.astype(np.float64)).astype(ml_dtypes.bfloat16)
    return (jnp.asarray(high), jnp.asarray(low))


def periodic_tables(size):
    half, quarter = size // 2, size // 4
    groups = (
        (np.arange(0, half + 1, 4), np.arange(4, half, 4), quarter),
        (np.arange(2, half, 4), np.arange(2, half, 4), quarter),
        (np.arange(1, half, 2), np.arange(1, half, 2), half),
    )
    tables, waves = [], []
    for cosines, sines, rows in groups:
        x = np.arange(rows)[:, None]
        norms = np.where((cosines == 0) | (cosines == half), np.sqrt(1.0 / size), np.sqrt(2.0 / size))
        tables.append(
            np.concatenate(
                [
                    norms * np.cos(2.0 * np.pi / size * (x * cosines % size)),
                    np.sqrt(2.0 / size) * np.sin(2.0 * np.pi / size * (x * sines % size)),
                ],
                axis=1,
            )
        )
        waves += [cosines, sines]
    waves = np.concatenate(waves)
    return (tables, 4.0 * np.sin(np.pi * waves / size) ** 2)


def cosine_table(size):
    modes = np.arange(size)[:, None]
    table = np.sqrt(2.0 / size) * np.cos(np.pi * modes * (2 * np.arange(size)[None, :] + 1) / (2 * size))
    table[0] = np.sqrt(1.0 / size)
    return (table, 4.0 * np.sin(np.pi * modes[:, 0] / (2 * size)) ** 2)


def level_tables(size):
    modes, levels = np.arange(size)[None, :], np.arange(size)[:, None]
    omegas = (
        np.pi * (2 * modes + 1) / (2 * size + 1),
        np.pi * (modes + 1) / (size + 1),
        np.pi * (modes + 1) / (size + 0.5),
    )
    vectors = (
        np.cos(omegas[0] * (levels + 0.5)),
        np.sin(omegas[1] * (levels + 1)),
        np.sin(omegas[2] * (levels + 1)),
    )
    vectors = [v / np.sqrt(np.sum(v * v, axis=0, keepdims=True)) for v in vectors]
    return (vectors, [4.0 * np.sin(o[0] / 2) ** 2 for o in omegas])


def split(value):
    high = value.astype(BF16)
    return (high, (value - high.astype(F32)).astype(BF16))


def dot3(left, right, dims=((1,), (0,))):
    one = lambda a, b: lax.dot_general(a, b, (dims, ((), ())), preferred_element_type=F32)
    free = 1 - dims[0][0]
    size = left[0].shape[free]
    both = one(jnp.concatenate(left, axis=free), right[0])
    return both[:size] + (both[size:] + one(left[0], right[1]))


def read_pair(refs):
    return (refs[0][...], refs[1][...])


def periodic_forward(value, tables):
    half, quarter = value.shape[1] // 2, value.shape[1] // 4
    even, odd = value[:, :half] + value[:, half:], value[:, :half] - value[:, half:]
    parts = (even[:, :quarter] + even[:, quarter:], even[:, :quarter] - even[:, quarter:], odd)
    return jnp.concatenate([dot3(split(p), read_pair(t)) for p, t in zip(parts, tables)], axis=1)


def periodic_inverse(value, tables):
    half, quarter = value.shape[1] // 2, value.shape[1] // 4
    parts = (value[:, :quarter], value[:, quarter:half], value[:, half:])
    four, two, odd = [dot3(split(p), read_pair(t), ((1,), (1,))) for p, t in zip(parts, tables)]
    even = jnp.concatenate([four + two, four - two], axis=1)
    return jnp.concatenate([even + odd, even - odd], axis=1)


def power(base, exponent):
    result = None
    while exponent:
        if exponent & 1:
            result = base if result is None else result * base
        base = base * base
        exponent >>= 1
    return result


def recurrence_root(sine):
    half = 0.5 * jnp.sqrt(sine)
    root = jnp.sqrt(1.0 + half * half) - half
    return root * root


def first_sweeps(load, root, top, above, store, levels):
    value = None
    for level in range(levels):
        value = load(level) if value is None else load(level) + root * value
        store[level] = value
    last = value
    value = top * value if above is None else top * value + above
    for level in range(levels - 1, -1, -1):
        value = root * (value - store[level])
    return (value, last)


def second_sweeps(load, start, root, top, above, store, levels, emit):
    value = start
    for level in range(levels):
        value = root * value if load is None else load(level) + root * value
        store[level] = value
    value = top * value if above is None else top * value + above
    for level in range(levels - 1, -1, -1):
        value = root * (value - store[level])
        emit(level, value)


def block_fluxes(ends, weights_ref, vectors_ref, levels, out_ref):
    blocks = len(ends)
    one = lambda dims, b: lax.dot_general(
        vectors_ref[...], b, (dims, ((), ())), precision=lax.Precision.HIGHEST, preferred_element_type=F32
    )
    upper = lower = None
    for block in range(blocks):
        even_next, odd_next = ends[(block + 1) % blocks]
        even, odd = ends[block]
        jump = one(((0,), (0,)), (even_next + odd_next) - (even - odd))
        up, low = weights_ref[0, block] * jump, weights_ref[1, block] * jump
        upper = up if upper is None else upper + up
        lower = low if lower is None else lower + low
    upper, lower = one(((1,), (0,)), upper), one(((1,), (0,)), lower)
    width = upper.shape[1]
    is_even = lax.broadcasted_iota(jnp.int32, (8, width), 0) % 2 == 0
    for level in range(levels):
        up, low = upper[level : level + 1], lower[level : level + 1]
        out_ref[level] = jnp.where(is_even, up - low, -up - low)


def fold_ends(total, out_ref, levels):
    is_even = lax.broadcasted_iota(jnp.int32, total.shape[1:], 0) % 2 == 0
    for level in range(levels):
        value = total[level]
        out_ref[0, level : level + 1] = jnp.sum(jnp.where(is_even, value, 0.0), axis=0, keepdims=True)
        out_ref[1, level : level + 1] = jnp.sum(jnp.where(is_even, 0.0, value), axis=0, keepdims=True)


def forward_kernel(
    levels, tile, ids_ref, w_new_ref, w_hbm, div_ref, t0h, t0l, t1h, t1l, t2h, t2l, ch, cl, root_ref, inv_ref,
    start_ref, top_ref, end_ref, field_hbm, edge_ref, ends_ref, corr_hbm, field, w_rows, above, lowest, store, total,
    sems, w_sems,
):
    step = pl.program_id(0)
    tables = ((t0h, t0l), (t1h, t1l), (t2h, t2l))

    pairs = levels // 2

    @pl.when(step == 0)
    def _():
        loads = chunk_copies(w_hbm, w_rows, w_sems)
        for load in loads:
            load.start()
        above[...] = jnp.zeros_like(above)
        total[...] = jnp.zeros_like(total)
        for load in loads:
            load.wait()
        put_cells(ids_ref, w_new_ref, w_rows)
        pltpu.make_async_copy(w_rows, corr_hbm, sems.at[1]).start()

    row_count = above.shape[0]

    @pl.when(step < pairs)
    def _():
        low = pl.multiple_of((pairs - 1 - step) * 2 * row_count, 2 * row_count)
        value = w_rows[pl.ds(low, 2 * row_count)]
        lower, upper = value[:row_count], value[row_count:]
        source = jnp.concatenate([div_ref[0] + (upper - lower), div_ref[1] + (above[...] - upper)], axis=0)
        modes = periodic_forward(source, tables)
        for k in range(2):
            part = modes[k * row_count : (k + 1) * row_count]
            field[(pairs - 1 - step) * 2 + k] = dot3(read_pair((ch, cl)), split(part))
        above[...] = lower

    @pl.when(step == pairs - 1)
    def _():
        pltpu.make_async_copy(field, field_hbm, sems.at[0]).start()
        lowest[...] = dot3(read_pair((ch, cl)), split(periodic_forward(w_rows[:row_count], tables)))

    @pl.when(step >= pairs)
    def _():
        def rows_of(sub, _):
            here = pl.multiple_of(sub * 8, 8)
            rows = pl.ds(here, 8)
            full = pl.ds(pl.multiple_of((step - pairs) * tile + here, 8), 8)
            root, top = root_ref[rows], top_ref[rows]
            load = lambda level: field[level, full]
            first, _ = first_sweeps(load, root, top, None, store, levels)
            edge_ref[0, rows] = first * inv_ref[rows] - lowest[full]
            weight = end_ref[rows, :1]

            def emit(level, value):
                total[level] += weight * value
                if level == levels - 1:
                    edge_ref[1, rows] = value

            second_sweeps(load, first * start_ref[rows], root, top, None, store, levels, emit)
            return 0

        lax.fori_loop(0, tile // 8, rows_of, 0)

    @pl.when(step == pl.num_programs(0) - 1)
    def _():
        fold_ends(total, ends_ref, levels)
        pltpu.make_async_copy(w_rows, corr_hbm, sems.at[1]).wait()
        pltpu.make_async_copy(field, field_hbm, sems.at[0]).wait()


def edge_kernel(
    levels, edge_ref, ends_ref, weights_ref, vectors_ref, root_ref, inv_ref, start_ref, top_ref, end_ref, ch, cl,
    out_ref, pattern, store, fixed,
):
    step = pl.program_id(0)
    tile = edge_ref.shape[1]

    @pl.when(step == 0)
    def _():
        ends = [(ends_ref[b, 0], ends_ref[b, 1]) for b in range(ends_ref.shape[0])]
        block_fluxes(ends, weights_ref, vectors_ref, levels, pattern)

    def rows_of(sub, _):
        here = pl.multiple_of(sub * 8, 8)
        rows, full = pl.ds(here, 8), pl.ds(pl.multiple_of(step * tile + here, 8), 8)
        root, top = root_ref[rows], top_ref[rows]
        first, last = first_sweeps(lambda level: pattern[level], root, top, None, store, levels)
        weight = end_ref[rows, :1]
        fixed[0, full] = edge_ref[0, rows] - weight * (first * inv_ref[rows])
        last = last + power(root, levels) * (first * start_ref[rows])
        fixed[1, full] = edge_ref[1, rows] - weight * (root * (top - 1.0) * last)
        return 0

    lax.fori_loop(0, tile // 8, rows_of, 0)

    @pl.when(step == pl.num_programs(0) - 1)
    def _():
        for side in range(2):
            value = dot3(split(fixed[side].T), read_pair((ch, cl)))
            out_ref[:, side] = value.reshape(out_ref.shape[0], out_ref.shape[2], out_ref.shape[3])


def join_start(levels, near_top, root):
    square = root * root
    sums = jnp.ones_like(root)
    for _ in range(1, levels):
        sums = 1.0 + square * sums
    whole = power(root, 2 * levels)
    one = 1.0 / (sums + whole)
    near = -root * sums * one
    far = -power(root, levels) * one
    part = power(root, 2 * levels - 1)
    bottom = -root * (1.0 + part) / (1.0 + whole * root)
    pairs = (1.0 + root) * sums
    top = -root * (pairs - part) / (pairs + whole)
    return (near, far, jnp.where(near_top, top, bottom), jnp.where(near_top, bottom, top))


def join_chain(load, blocks, near, far, beta):
    alpha = load(0, 1)
    alphas, betas, heads, slopes = [alpha], [beta], [None], [None]
    for block in range(1, blocks):
        scale = 1.0 / (1.0 - near * beta)
        head = (load(block, 0) - near * alpha) * scale
        slope = far * scale
        alpha = load(block, 1) - far * alpha + far * beta * head
        beta = near + far * beta * slope
        alphas.append(alpha)
        betas.append(beta)
        heads.append(head)
        slopes.append(slope)
    return (alphas, betas, heads, slopes)


def chain_place(block, blocks, half):
    return block + half * (blocks - 1 - 2 * block)


def gather_modes_kernel(levels, px_count, half_ref, edge_ref, t0h, t0l, t1h, t1l, t2h, t2l, root_ref, out_ref, alpha_ref):
    blocks, _, rows, _ = out_ref.shape
    half = half_ref[0]
    for block in range(blocks):
        for side in range(2):
            whole = jnp.concatenate([edge_ref[i * blocks + block, side] for i in range(px_count)], axis=1)
            out_ref[block, side] = whole
    flat = out_ref[...].reshape(blocks * 2 * rows, out_ref.shape[3])
    out_ref[...] = periodic_forward(flat, ((t0h, t0l), (t1h, t1l), (t2h, t2l))).reshape(out_ref.shape)

    def rows_of(sub, _):
        here = pl.ds(pl.multiple_of(sub * 8, 8), 8)
        near, far, own, _ = join_start(levels, half == 1, root_ref[here])
        load = lambda block, outer: out_ref[chain_place(block, blocks, half), jnp.abs(outer - half), here]
        alpha_ref[here] = join_chain(load, blocks, near, far, own)[0][-1]
        return 0

    lax.fori_loop(0, rows // 8, rows_of, 0)


def join_kernel(
    levels, px_count, half_ref, modes_ref, alpha_ref, t0h, t0l, t1h, t1l, t2h, t2l, root_ref, out_ref, modes
):
    blocks, _, rows, _ = modes_ref.shape
    half = half_ref[0]
    width = out_ref.shape[3]

    def rows_of(sub, _):
        here = pl.ds(pl.multiple_of(sub * 8, 8), 8)
        near, far, own, other = join_start(levels, half == 1, root_ref[here])
        load = lambda block, outer: modes_ref[chain_place(block, blocks, half), jnp.abs(outer - half), here]
        alphas, betas, heads, slopes = join_chain(load, blocks, near, far, own)
        for _ in range(1, blocks):
            other = near + far * other * (far / (1.0 - near * other))
        met = alpha_ref[here]
        outer = (met - other * alphas[-1]) / (1.0 - other * betas[-1])
        for block in range(blocks - 1, -1, -1):
            place = chain_place(block, blocks, half)
            modes[place, 1 - half, here] = outer
            if block:
                outer = heads[block] - slopes[block] * outer
                modes[place, half, here] = alphas[block - 1] - betas[block - 1] * outer
            else:
                modes[place, half, here] = jnp.zeros_like(outer)
        return 0

    lax.fori_loop(0, rows // 8, rows_of, 0)
    flat = modes[...].reshape(blocks * 2 * rows, modes.shape[3])
    whole = periodic_inverse(flat, ((t0h, t0l), (t1h, t1l), (t2h, t2l))).reshape(modes.shape)
    for block in range(blocks):
        for side in range(2):
            for i in range(px_count):
                out_ref[i * blocks + block, side] = whole[block, side, :, i * width : (i + 1) * width]


def spread_kernel(
    levels, joined_ref, ch, cl, root_ref, start_ref, below_ref, top_ref, end_ref, out_ref, ends_ref, store, total, sides
):
    step = pl.program_id(0)
    tile = out_ref.shape[1]

    @pl.when(step == 0)
    def _():
        kx_width = joined_ref.shape[0] * joined_ref.shape[2]
        for side in range(2):
            value = joined_ref[:, side].reshape(kx_width, joined_ref.shape[3])
            sides[side] = dot3(read_pair((ch, cl)), split(value), ((1,), (1,)))
        total[...] = jnp.zeros_like(total)

    def rows_of(sub, _):
        here = pl.multiple_of(sub * 8, 8)
        rows, full = pl.ds(here, 8), pl.ds(pl.multiple_of(step * tile + here, 8), 8)
        root, top = root_ref[rows], top_ref[rows]
        below, above = sides[0, full], sides[1, full]
        out_ref[0, rows] = below
        out_ref[1, rows] = above
        start = start_ref[rows] * (power(root, levels) * above) - below_ref[rows] * below
        weight = end_ref[rows, :1]

        def emit(level, value):
            total[level] += weight * value

        second_sweeps(None, start, root, top, above, store, levels, emit)
        return 0

    lax.fori_loop(0, tile // 8, rows_of, 0)

    @pl.when(step == pl.num_programs(0) - 1)
    def _():
        fold_ends(total, ends_ref, levels)


def inverse_kernel(
    levels, tile, place_ref, field_ref, sides_ref, ends_ref, more_ref, weights_ref, vectors_ref, root_ref, start_ref,
    below_ref, top_ref, end_ref, t0h, t0l, t1h, t1l, t2h, t2l, ch, cl, w_ref, roof_ref, out_ref, field, pattern, store,
):
    step = pl.program_id(0)
    tiles = pl.num_programs(0) - levels // 2
    tables = ((t0h, t0l), (t1h, t1l), (t2h, t2l))

    @pl.when(step == 0)
    def _():
        ends = [
            (ends_ref[b, 0] + more_ref[b, 0], ends_ref[b, 1] + more_ref[b, 1]) for b in range(ends_ref.shape[0])
        ]
        block_fluxes(ends, weights_ref, vectors_ref, levels, pattern)

    @pl.when(step < tiles)
    def _():
        def rows_of(sub, _):
            here = pl.multiple_of(sub * 8, 8)
            rows = pl.ds(here, 8)
            full = pl.ds(pl.multiple_of(step * tile + here, 8), 8)
            root, top = root_ref[rows], top_ref[rows]
            below, above = sides_ref[0, rows], sides_ref[1, rows]
            weight = end_ref[rows, :1]
            load = lambda level: field_ref[level, rows] - weight * pattern[level]
            first, _ = first_sweeps(load, root, top, above, store, levels)
            start = start_ref[rows] * first - below_ref[rows] * below
            held = []

            def emit(level, value):
                if held:
                    field[level + 1, full] = held.pop() - value
                held.append(value)

            second_sweeps(load, start, root, top, above, store, levels, emit)
            field[0, full] = jnp.where(place_ref[0] == 0, 0.0, held[0] - below)
            return 0

        lax.fori_loop(0, tile // 8, rows_of, 0)

    @pl.when(step >= tiles)
    def _():
        level = (step - tiles) * 2
        rows_y = [dot3(read_pair((ch, cl)), split(field[level + k])) for k in range(2)]
        slope = periodic_inverse(jnp.concatenate(rows_y, axis=0), tables)
        count = roof_ref.shape[0]
        for k in range(2):
            solid = place_ref[0] * levels + level + k < roof_ref[...]
            out_ref[k] = jnp.where(solid, 0.0, w_ref[k] - slope[k * count : (k + 1) * count])


def facet_places(ids, width):
    safe = jnp.maximum(ids, 0)
    row, column = safe // width, safe % width
    return jnp.stack([row // 8, column // 128, jnp.where(ids < 0, -1, row % 8 * 128 + column % 128)])


def tile_at(places_ref, facet):
    return (
        pl.ds(pl.multiple_of(places_ref[0, facet] * 8, 8), 8),
        pl.ds(pl.multiple_of(places_ref[1, facet] * 128, 128), 128),
    )


def pair_at(places_ref, facet):
    return (
        pl.ds(pl.multiple_of(lax.shift_right_logical(places_ref[0, facet], 1) * 16, 16), 16),
        pl.ds(pl.multiple_of(places_ref[1, facet] * 128, 128), 128),
    )


def pick_cells(ids_ref, ref, rows_ref, flat_ref):
    sublane = lax.broadcasted_iota(jnp.int32, (8, 128), 0)
    position = sublane * 128 + lax.broadcasted_iota(jnp.int32, (8, 128), 1)

    def pick(i, _):
        rows = None
        for lane in range(8):
            facet = i * 8 + lane
            mark = ids_ref[2, facet]
            if ref.dtype == F32:
                tile = ref[tile_at(ids_ref, facet)]
            else:
                both = ref[pair_at(ids_ref, facet)].astype(F32)
                tile = jnp.where(ids_ref[0, facet] & 1 == 0, both[:8], both[8:])
            tile = jnp.where(position == mark, tile, 0.0)
            tile = pltpu.roll(tile, (lane - lax.shift_right_arithmetic(mark, 7)) & 7, 0)
            rows = tile if rows is None else jnp.where(sublane == lane, tile, rows)
        rows_ref[pl.ds(pl.multiple_of(i * 8, 8), 8)] = rows

    group_count = rows_ref.shape[0] // 8
    per_trip = math.gcd(group_count, 8)

    def trip(i, _):
        for k in range(per_trip):
            pick(i * per_trip + k, None)
        return 0

    lax.fori_loop(0, group_count // per_trip, trip, 0)
    ones = jnp.ones((8, 128), F32)
    for group in range(flat_ref.shape[0]):
        rows = rows_ref[group * 128 : (group + 1) * 128]
        flat = lax.dot_general(
            ones, rows, (((1,), (1,)), ((), ())), precision=lax.Precision.HIGHEST, preferred_element_type=F32
        )
        flat_ref[group : group + 1] = flat[:1]


def level_solve_tables(sine, levels, is_first, is_last):
    root = recurrence_root(sine)
    top = jnp.where(is_last, root / (1.0 + root), 0.0)
    square = root * root
    kappa = jnp.zeros_like(root)
    for _ in range(levels):
        kappa = square * (1.0 + kappa)
    decay = power(root, levels)
    inverse = 1.0 / root
    bottom = jnp.where(is_first, 1.0 - inverse, 1.0)
    inv = 1.0 / (1.0 + bottom * (kappa - top * decay * decay))
    return (root, inv, bottom * inv, inv * inverse, top)


CHUNKS = 8


def chunk_copies(source, target, sems):
    rows = source.shape[0] // CHUNKS
    parts = [pl.ds(i * rows, rows) for i in range(CHUNKS)]
    return [pltpu.make_async_copy(source.at[p], target.at[p], sems.at[i]) for i, p in enumerate(parts)]


def gather_kernel(
    levels, ids_ref, ends_ref, w_hbm, sin_x_ref, sin_y_ref, out_ref, o0, o1, o2, o3, o4, rows_ref, w_ref, tables, sems,
    w_sems,
):
    w_parts = chunk_copies(w_hbm, w_ref, w_sems)
    for copy in w_parts:
        copy.start()

    def fill(i, _):
        rows = pl.ds(pl.multiple_of(i * 8, 8), 8)
        sine = sin_y_ref[rows, :1] + sin_x_ref[...]
        for k, value in enumerate(level_solve_tables(sine, levels, ends_ref[0] == 1, ends_ref[1] == 1)):
            tables[k, rows] = value
        return 0

    lax.fori_loop(0, sin_y_ref.shape[0] // 8, fill, 0)
    leaving = [pltpu.make_async_copy(tables.at[k], o, sems.at[k]) for k, o in enumerate((o0, o1, o2, o3, o4))]
    for copy in w_parts:
        copy.wait()
    for copy in leaving:
        copy.start()
    pick_cells(ids_ref, w_ref, rows_ref, out_ref)
    for copy in leaving:
        copy.wait()


def gather_temp_kernel(ids_ref, temp_ref, out_ref, rows_ref):
    pick_cells(ids_ref, temp_ref, rows_ref, out_ref)


def put_cells(ids_ref, new_ref, out):
    sublane = lax.broadcasted_iota(jnp.int32, (8, 128), 0)
    position = sublane * 128 + lax.broadcasted_iota(jnp.int32, (8, 128), 1)

    per_trip = math.gcd(new_ref.shape[0], 32)

    def put(i, _):
        for k in range(per_trip):
            facet = i * per_trip + k
            hit = position == ids_ref[2, facet]
            pltpu.store(out.at[tile_at(ids_ref, facet)], jnp.full((8, 128), new_ref[facet]), mask=hit)
        return 0

    lax.fori_loop(0, new_ref.shape[0] // per_trip, put, 0)


def theta_kernel(ids_ref, new_ref, temp_ref, out_ref, wide):
    rows = temp_ref.shape[0]
    chunk = math.gcd(rows, 64)

    def widen(i, _):
        here = pl.ds(pl.multiple_of(i * chunk, chunk), chunk)
        wide[here] = temp_ref[here].astype(F32)
        return 0

    def narrow(i, _):
        here = pl.ds(pl.multiple_of(i * chunk, chunk), chunk)
        out_ref[here] = wide[here].astype(BF16)
        return 0

    lax.fori_loop(0, rows // chunk, widen, 0)
    put_cells(ids_ref, new_ref, wide)
    lax.fori_loop(0, rows // chunk, narrow, 0)


def by_owner(flat, slots):
    shares = 128 // slots
    return jnp.stack([pltpu.roll(flat, (128 - k * slots) % 128, 1) if k else flat for k in range(shares)])


class Links:
    def __init__(self, sizes, slots, sent, received):
        names = ("px", "py_half", "py_low")
        self.sizes, self.shares = sizes, 128 // slots
        self.count = sizes[0] * sizes[1] * sizes[2]
        self.places = [lax.axis_index(name) for name in names]
        self.me = (self.places[0] * sizes[1] + self.places[1]) * sizes[2] + self.places[2]
        self.mine = (lax.rem(self.me, self.shares), lax.div(self.me, self.shares))
        self.sent, self.received = sent, received

    def each_peer(self, act):
        sizes, places = self.sizes, self.places

        def one(step, _):
            low = lax.rem(places[2] + step, sizes[2])
            rest = lax.div(step, sizes[2])
            middle = lax.rem(places[1] + rest, sizes[1])
            first = lax.rem(places[0] + lax.div(rest, sizes[1]), sizes[0])
            act((first * sizes[1] + middle) * sizes[2] + low, (first, middle, low))
            return 0

        lax.fori_loop(1, self.count, one, 0)

    def copy(self, phase, source, target, peer, device, landing):
        at = lambda ref, index: ref.at[lax.rem(index, self.shares), lax.div(index, self.shares)]
        return pltpu.make_async_remote_copy(
            at(source, peer),
            at(target, landing),
            self.sent.at[phase, peer],
            self.received.at[phase, landing],
            device_id=device,
            device_id_type=pl.DeviceIdType.MESH,
        )

    def greet(self):
        barrier = pltpu.get_barrier_semaphore()
        self.each_peer(
            lambda peer, device: pl.semaphore_signal(
                barrier, inc=1, device_id=device, device_id_type=pl.DeviceIdType.MESH
            )
        )
        return barrier

    def start(self, phase, source, target):
        self.each_peer(lambda peer, device: self.copy(phase, source, target, peer, device, self.me).start())
        target[self.mine] = source[self.mine]

    def finish(self, phase, source, target):
        self.each_peer(lambda peer, device: self.copy(phase, source, target, peer, device, peer).wait())


def from_owners(parts, slots):
    lane = lax.broadcasted_iota(jnp.int32, parts.shape[1:], 1)
    total = None
    for k in range(parts.shape[0]):
        part = jnp.where(lane < slots, parts[k], 0.0)
        part = pltpu.roll(part, k * slots, 1) if k else part
        total = part if total is None else total + part
    return total


def stress_kernel(
    sizes, slots, own_ref, facet_ref, drag_ref, heat_ref, back_ref, w_ref, sample, got, flux, back, sent, received
):
    links = Links(sizes, slots, sent, received)
    barrier = links.greet()
    sample[:, :, 0] = by_owner(own_ref[...], slots)
    pl.semaphore_wait(barrier, links.count - 1)
    links.start(0, sample, got)
    facet, drag, heat = [by_owner(ref[...], slots) for ref in (facet_ref, drag_ref, heat_ref)]
    links.finish(0, sample, got)
    w_cell = got[:, :, 0]
    speeds = jnp.sqrt(w_cell * w_cell + 0.25)
    flux[:, :, 0] = drag * speeds * w_cell
    flux[:, :, 1] = heat * speeds
    flux[:, :, 2] = facet
    links.start(1, flux, back)
    w_ref[...] = w_cell
    links.finish(1, flux, back)
    for k in range(3):
        back_ref[k] = from_owners(back[:, :, k], slots)


def facet_temp_kernel(
    sizes, slots, own_ref, facet_ref, radiation_ref, capacity_ref, heat_ref, w_ref, new_ref, sample, got, sent, received
):
    links = Links(sizes, slots, sent, received)
    barrier = links.greet()
    sample[:, :, 0] = by_owner(own_ref[...], slots)
    pl.semaphore_wait(barrier, links.count - 1)
    links.start(0, sample, got)
    facet, radiation, capacity, heat = [
        by_owner(ref[...], slots) for ref in (facet_ref, radiation_ref, capacity_ref, heat_ref)
    ]
    w_cell = w_ref[...]
    scale = heat * jnp.sqrt(w_cell * w_cell + 0.25)
    links.finish(0, sample, got)
    flux = scale * (facet - got[:, :, 0])
    new_ref[...] = from_owners(facet + (radiation - flux - 0.5 * facet) / capacity, slots)


def facet_sums(ids, returned):
    same = ids[:, None] == ids[None, :]
    return jnp.sum(jnp.where(same, returned.reshape(1, -1), 0.0), axis=1)


def near_walls(w_rows, sin_x, sin_y, ends, ids, places, facet_temp, drag_coef, heat_coef):
    count = ids.shape[0]
    sizes = tuple(lax.axis_size(name) for name in ("px", "py_half", "py_low"))
    slots = count // (sizes[0] * sizes[1] * sizes[2])
    flat = (count // 128, 128)
    rows, width = sin_y.shape[0], sin_x.shape[1]
    own, *tables = pl.pallas_call(
        lambda *refs: gather_kernel(w_rows.shape[0] // rows, *refs),
        out_shape=[jax.ShapeDtypeStruct(flat, F32)] + [jax.ShapeDtypeStruct((rows, width), F32)] * 5,
        in_specs=[SMEM, SMEM, HBM, VMEM, VMEM],
        out_specs=[VMEM] + [HBM] * 5,
        scratch_shapes=[
            pltpu.VMEM((count, 128), F32),
            pltpu.VMEM(w_rows.shape, F32),
            pltpu.VMEM((5, rows, width), F32),
            pltpu.SemaphoreType.DMA((5,)),
            pltpu.SemaphoreType.DMA((CHUNKS,)),
        ],
        compiler_params=PARAMS,
        name="facet_gather",
    )(places, ends, w_rows, sin_x, sin_y)
    by_rows = (128 // slots, flat[0], 128)
    tall = lambda values: pltpu.VMEM((128 // slots, flat[0], values, 128), F32)
    returned, w_cell = pl.pallas_call(
        lambda *refs: stress_kernel(sizes, slots, *refs),
        out_shape=(jax.ShapeDtypeStruct((3, *flat), F32), jax.ShapeDtypeStruct(by_rows, F32)),
        in_specs=[VMEM] * 4,
        out_specs=(VMEM, VMEM),
        scratch_shapes=[tall(1), tall(1), tall(3), tall(3)]
        + [pltpu.SemaphoreType.DMA((2, sizes[0] * sizes[1] * sizes[2]))] * 2,
        compiler_params=pltpu.CompilerParams(collective_id=1, has_side_effects=True),
        name="stress_exchange",
    )(own, facet_temp.reshape(flat), drag_coef.reshape(flat), heat_coef.reshape(flat))
    return (own.reshape(count) - facet_sums(ids, returned[0]), returned, w_cell, tables)


def warm_air(temp_rows, ids, places, returned):
    count = ids.shape[0]
    flat = (count // 128, 128)
    own = pl.pallas_call(
        gather_temp_kernel,
        out_shape=jax.ShapeDtypeStruct(flat, F32),
        in_specs=[SMEM, VMEM],
        out_specs=VMEM,
        scratch_shapes=[pltpu.VMEM((count, 128), F32)],
        compiler_params=PARAMS,
        cost_estimate=pl.CostEstimate(flops=0, bytes_accessed=4 * temp_rows.size, transcendentals=0),
        name="temp_gather",
    )(places, temp_rows)
    heat_flux = returned[1] * (returned[2] - own)
    return (own, own.reshape(count) + facet_sums(ids, heat_flux))


def warm_facets(own, w_cell, facet_temp, net_radiation, heat_capacity, heat_coef):
    flat = own.shape
    sizes = tuple(lax.axis_size(name) for name in ("px", "py_half", "py_low"))
    slots = own.size // (sizes[0] * sizes[1] * sizes[2])
    tall = pltpu.VMEM((128 // slots, flat[0], 1, 128), F32)
    new_temp = pl.pallas_call(
        lambda *refs: facet_temp_kernel(sizes, slots, *refs),
        out_shape=jax.ShapeDtypeStruct(flat, F32),
        in_specs=[VMEM] * 6,
        out_specs=VMEM,
        scratch_shapes=[tall] * 2 + [pltpu.SemaphoreType.DMA((1, sizes[0] * sizes[1] * sizes[2]))] * 2,
        compiler_params=pltpu.CompilerParams(collective_id=2, has_side_effects=True),
        cost_estimate=pl.CostEstimate(flops=0, bytes_accessed=2**24, transcendentals=0),
        name="facet_temp",
    )(own, *[a.reshape(flat) for a in (facet_temp, net_radiation, heat_capacity, heat_coef)], w_cell)
    return new_temp.reshape(facet_temp.shape)


def body(
    horiz_div,
    w_star,
    air_temp,
    roof_level,
    facet_cells,
    facet_temp,
    net_radiation,
    heat_capacity,
    drag_coef,
    heat_coef,
):
    levels, rows, width = w_star.shape
    px_count, blocks = lax.axis_size("px"), lax.axis_size("py_low")
    py_count = 2 * blocks
    group = px_count * blocks
    place_x, place_y, half = lax.axis_index("px"), lax.axis_index(("py_half", "py_low")), lax.axis_index("py_half")
    own_kx = width // group
    y_cells = rows * px_count

    w_rows = w_star.reshape(levels * rows, width)
    temp_rows = air_temp.reshape(levels * rows, width)
    ids = facet_cells[0]
    places = facet_places(ids, width)
    x_parts, sin_x = periodic_tables(width)
    y_parts, sin_y = periodic_tables(y_cells)
    cosines, sin_block = cosine_table(rows)
    x_tables = [t for part in x_parts for t in two_halves(part)]
    y_tables = [t for part in y_parts for t in two_halves(part)]
    to_modes, to_rows = two_halves(cosines), two_halves(np.ascontiguousarray(cosines.T))
    sin_x = jnp.asarray(sin_x, F32)

    is_first, is_last = place_y == 0, place_y == py_count - 1
    w_near, returned, w_cell, (root, inv, start, from_below, top) = near_walls(
        w_rows,
        sin_x[None, :],
        jnp.asarray(np.repeat(sin_block[:, None], 128, axis=1), F32),
        jnp.stack([is_first, is_last]).astype(jnp.int32),
        ids,
        places,
        facet_temp[0],
        drag_coef[0],
        heat_coef[0],
    )

    end = np.where(np.arange(rows) == 0, np.sqrt(1.0 / rows), cosines[:, 0])
    end = jnp.asarray(np.repeat(end[:, None], 128, axis=1), F32)

    vectors, sin_z = level_tables(levels)
    pick = lambda three: jnp.where(is_first, three[0], jnp.where(is_last, three[2], three[1])).astype(F32)
    vectors, sin_z = pick(vectors), pick(sin_z)
    sine_z = sin_z[:, None] + sin_x[None, :]
    size_z = jnp.sqrt(sine_z)
    half_z = 0.5 * size_z
    cosh_z = jnp.sqrt(1.0 + half_z * half_z)
    half_step = cosh_z - half_z
    across = jnp.exp(2.0 * rows * jnp.log(half_step))
    scale = 1.0 / ((1.0 - across * across) * size_z)
    same_end = -half_step * (1.0 + across * across / (half_step * half_step)) * scale
    far_end = -2.0 * across * cosh_z * scale
    turns = np.arange(px_count)
    circulant = jnp.stack(
        [1.0 / (1.0 - 2.0 * same_end + 2.0 * math.cos(2.0 * math.pi * s / px_count) * far_end) for s in turns]
    )
    circulant = lax.optimization_barrier(circulant)
    phase_of = jnp.asarray(np.cos(2.0 * np.pi * turns[:, None] * turns[None, :] / px_count) / px_count, F32)
    offsets = jnp.stack([(place_x - turns) % px_count, (place_x - 1 - turns) % px_count])
    phases = phase_of[offsets]
    weights = jnp.sum(phases[:, :, :, None, None] * circulant[None, None], axis=2)

    mine = place_x * blocks + lax.axis_index("py_low")
    own_sin = lax.dynamic_slice_in_dim(sin_x, mine * own_kx, own_kx)
    join_root = recurrence_root(own_sin[:, None] + jnp.asarray(sin_y, F32)[None, :])

    tile = math.gcd(rows, 32)
    tiles = rows // tile
    flat = lambda i: pl.BlockSpec((tile, width), i)
    fixed = lambda a: pl.BlockSpec(a.shape, lambda i: (0,) * len(a.shape))
    pairs = levels // 2
    late = lambda i: (jnp.maximum(i - pairs, 0), 0)
    down = lambda i: (jnp.maximum(pairs - 1 - i, 0), 0, 0)
    slab = pl.BlockSpec((2, rows, width), down)
    end_late = pl.BlockSpec((tile, 128), late)
    ends_shape = jax.ShapeDtypeStruct((2, levels, width), F32)
    field, edges, ends, w_corr = pl.pallas_call(
        lambda *refs: forward_kernel(levels, tile, *refs),
        out_shape=(
            jax.ShapeDtypeStruct(w_star.shape, F32),
            jax.ShapeDtypeStruct((2, rows, width), F32),
            ends_shape,
            jax.ShapeDtypeStruct(w_rows.shape, F32),
        ),
        grid=(pairs + tiles,),
        in_specs=[SMEM, SMEM, HBM, slab] + [fixed(t) for t in (*x_tables, *to_modes)] + [flat(late)] * 4 + [end_late],
        out_specs=(
            HBM,
            pl.BlockSpec((2, tile, width), lambda i: (0, *late(i))),
            fixed(ends_shape),
            HBM,
        ),
        scratch_shapes=[
            pltpu.VMEM(w_star.shape, F32),
            pltpu.VMEM(w_rows.shape, F32),
            pltpu.VMEM((rows, width), F32),
            pltpu.VMEM((rows, width), F32),
            pltpu.VMEM((levels, 8, width), F32),
            pltpu.VMEM((levels, 8, width), F32),
            pltpu.SemaphoreType.DMA((2,)),
            pltpu.SemaphoreType.DMA((CHUNKS,)),
        ],
        compiler_params=PARAMS,
        name="forward",
    )(places, w_near, w_rows, horiz_div, *x_tables, *to_modes, root, inv, start, top, end)

    all_ends = lax.all_gather(ends, "px")
    here = lambda i: (i, 0)
    packed = jax.ShapeDtypeStruct((group, 2, own_kx, rows), F32)
    working = [pltpu.VMEM((levels, 8, width), F32)] * 2
    edges = pl.pallas_call(
        lambda *refs: edge_kernel(levels, *refs),
        out_shape=packed,
        grid=(tiles,),
        in_specs=[pl.BlockSpec((2, tile, width), lambda i: (0, i, 0))]
        + [fixed(a) for a in (all_ends, weights, vectors)]
        + [flat(here)] * 4
        + [pl.BlockSpec((tile, 128), here)]
        + [fixed(t) for t in to_modes],
        out_specs=fixed(packed),
        scratch_shapes=working + [pltpu.VMEM((2, rows, width), F32)],
        compiler_params=PARAMS,
        name="edges",
    )(edges, all_ends, weights, vectors, root, inv, start, top, end, *to_modes)
    w_cell, edges = lax.optimization_barrier((w_cell, edges))
    places_late, edges = lax.optimization_barrier((places, edges))
    temp_own, temp_near = warm_air(temp_rows, ids, places_late, returned)
    edges = lax.all_to_all(edges, ("px", "py_low"), split_axis=0, concat_axis=0, tiled=True)
    edges, temp_near = lax.optimization_barrier((edges, temp_near))
    half_id = half.astype(jnp.int32).reshape(1)
    modes, alpha = pl.pallas_call(
        lambda *refs: gather_modes_kernel(levels, px_count, *refs),
        out_shape=(
            jax.ShapeDtypeStruct((blocks, 2, own_kx, y_cells), F32),
            jax.ShapeDtypeStruct((own_kx, y_cells), F32),
        ),
        in_specs=[SMEM] + [VMEM] * 8,
        out_specs=(VMEM, VMEM),
        compiler_params=PARAMS,
        name="gather_modes",
    )(half_id, edges, *y_tables, join_root)
    alpha, temp_near = lax.optimization_barrier((alpha, temp_near))
    theta_new = pl.pallas_call(
        theta_kernel,
        out_shape=jax.ShapeDtypeStruct(temp_rows.shape, BF16),
        in_specs=[SMEM, SMEM, VMEM],
        out_specs=VMEM,
        scratch_shapes=[pltpu.VMEM(temp_rows.shape, F32)],
        compiler_params=PARAMS,
        cost_estimate=pl.CostEstimate(flops=temp_rows.size, bytes_accessed=8 * temp_rows.size, transcendentals=0),
        name="theta",
    )(places, temp_near, temp_rows).reshape(air_temp.shape)
    alpha = lax.ppermute(alpha, "py_half", [(0, 1), (1, 0)])
    alpha, theta_new = lax.optimization_barrier((alpha, theta_new))
    joined = pl.pallas_call(
        lambda *refs: join_kernel(levels, px_count, *refs),
        out_shape=packed,
        in_specs=[SMEM] + [VMEM] * 9,
        out_specs=VMEM,
        scratch_shapes=[pltpu.VMEM((blocks, 2, own_kx, y_cells), F32)],
        compiler_params=PARAMS,
        name="join",
    )(half_id, modes, alpha, *y_tables, join_root)
    joined, temp_own = lax.optimization_barrier((joined, temp_own))
    new_temp = warm_facets(
        temp_own, w_cell, facet_temp[0], net_radiation[0], heat_capacity[0], heat_coef[0]
    )
    joined = lax.all_to_all(joined, ("px", "py_low"), split_axis=0, concat_axis=0, tiled=True)
    sides, more = pl.pallas_call(
        lambda *refs: spread_kernel(levels, *refs),
        out_shape=(jax.ShapeDtypeStruct((2, rows, width), F32), ends_shape),
        grid=(tiles,),
        in_specs=[fixed(packed)]
        + [fixed(t) for t in to_modes]
        + [flat(here)] * 4
        + [pl.BlockSpec((tile, 128), here)],
        out_specs=(pl.BlockSpec((2, tile, width), lambda i: (0, i, 0)), fixed(ends_shape)),
        scratch_shapes=working + [pltpu.VMEM((2, rows, width), F32)],
        compiler_params=PARAMS,
        name="spread",
    )(joined, *to_modes, root, start, from_below, top, end)
    more = lax.all_gather(more, "px")

    early = lambda i: (jnp.minimum(i, tiles - 1), 0)
    up = lambda i: (jnp.maximum(i - tiles, 0), 0, 0)
    slab = pl.BlockSpec((2, rows, width), up)
    w_new = pl.pallas_call(
        lambda *refs: inverse_kernel(levels, tile, *refs),
        out_shape=jax.ShapeDtypeStruct(w_star.shape, F32),
        grid=(tiles + pairs,),
        in_specs=[
            SMEM,
            pl.BlockSpec((levels, tile, width), lambda i: (0, *early(i))),
            pl.BlockSpec((2, tile, width), lambda i: (0, *early(i))),
        ]
        + [fixed(a) for a in (all_ends, more, weights, vectors)]
        + [flat(early)] * 4
        + [pl.BlockSpec((tile, 128), early)]
        + [fixed(t) for t in (*x_tables, *to_rows)]
        + [slab, fixed(roof_level)],
        out_specs=slab,
        scratch_shapes=[pltpu.VMEM(w_star.shape, F32)] + working,
        compiler_params=PARAMS,
        name="inverse",
    )(
        place_y.astype(jnp.int32).reshape(1),
        field,
        sides,
        all_ends,
        more,
        weights,
        vectors,
        root,
        start,
        from_below,
        top,
        end,
        *x_tables,
        *to_rows,
        w_corr.reshape(w_star.shape),
        roof_level,
    )
    return (w_new, theta_new, new_temp[None])


def solution(mesh):
    px_count, py_count = mesh.devices.shape
    split_mesh = jax.sharding.Mesh(
        mesh.devices.reshape(px_count, 2, py_count // 2), ("px", "py_half", "py_low")
    )
    py, every = ("py_half", "py_low"), ("px", "py_half", "py_low")
    placed = (P(py, "px", None),) * 3 + (P("px", None),) + (P(every, None),) * 6
    return jax.shard_map(
        body,
        mesh=split_mesh,
        in_specs=placed,
        out_specs=(P(py, "px", None), P(py, "px", None), P(every, None)),
        check_vma=False,
    )
```

```python
import math

import jax
import jax.numpy as jnp
import ml_dtypes
import numpy as np
from jax import lax
from jax.experimental import pallas as pl
from jax.experimental.pallas import tpu as pltpu
from jax.sharding import PartitionSpec as P

F32 = jnp.float32
BF16 = jnp.bfloat16
HBM = pl.BlockSpec(memory_space=pl.ANY)
VMEM = pl.BlockSpec(memory_space=pltpu.VMEM)
SMEM = pl.BlockSpec(memory_space=pltpu.SMEM)
PARAMS = pltpu.CompilerParams(vmem_limit_bytes=58 * 2**20)
SMALL = pltpu.CompilerParams(vmem_limit_bytes=28 * 2**20)


def two_halves(table):
    high = table.astype(ml_dtypes.bfloat16)
    low = (table - high.astype(np.float64)).astype(ml_dtypes.bfloat16)
    return (jnp.asarray(high), jnp.asarray(low))


def periodic_tables(size):
    half, quarter = size // 2, size // 4
    groups = (
        (np.arange(0, half + 1, 4), np.arange(4, half, 4), quarter),
        (np.arange(2, half, 4), np.arange(2, half, 4), quarter),
        (np.arange(1, half, 2), np.arange(1, half, 2), half),
    )
    tables, waves = [], []
    for cosines, sines, rows in groups:
        x = np.arange(rows)[:, None]
        norms = np.where((cosines == 0) | (cosines == half), np.sqrt(1.0 / size), np.sqrt(2.0 / size))
        tables.append(
            np.concatenate(
                [
                    norms * np.cos(2.0 * np.pi / size * (x * cosines % size)),
                    np.sqrt(2.0 / size) * np.sin(2.0 * np.pi / size * (x * sines % size)),
                ],
                axis=1,
            )
        )
        waves += [cosines, sines]
    waves = np.concatenate(waves)
    return (tables, 4.0 * np.sin(np.pi * waves / size) ** 2)


def cosine_table(size):
    modes = np.arange(size)[:, None]
    table = np.sqrt(2.0 / size) * np.cos(np.pi * modes * (2 * np.arange(size)[None, :] + 1) / (2 * size))
    table[0] = np.sqrt(1.0 / size)
    return (table, 4.0 * np.sin(np.pi * modes[:, 0] / (2 * size)) ** 2)


def level_tables(size):
    modes, levels = np.arange(size)[None, :], np.arange(size)[:, None]
    omegas = (
        np.pi * (2 * modes + 1) / (2 * size + 1),
        np.pi * (modes + 1) / (size + 1),
        np.pi * (modes + 1) / (size + 0.5),
    )
    vectors = (
        np.cos(omegas[0] * (levels + 0.5)),
        np.sin(omegas[1] * (levels + 1)),
        np.sin(omegas[2] * (levels + 1)),
    )
    vectors = [v / np.sqrt(np.sum(v * v, axis=0, keepdims=True)) for v in vectors]
    return (vectors, [4.0 * np.sin(o[0] / 2) ** 2 for o in omegas])


def split(value):
    high = value.astype(BF16)
    return (high, (value - high.astype(F32)).astype(BF16))


def dot3(left, right, dims=((1,), (0,))):
    one = lambda a, b: lax.dot_general(a, b, (dims, ((), ())), preferred_element_type=F32)
    free = 1 - dims[0][0]
    size = left[0].shape[free]
    both = one(jnp.concatenate(left, axis=free), right[0])
    return both[:size] + (both[size:] + one(left[0], right[1]))


def read_pair(refs):
    return (refs[0][...], refs[1][...])


def periodic_forward(value, tables):
    half, quarter = value.shape[1] // 2, value.shape[1] // 4
    even, odd = value[:, :half] + value[:, half:], value[:, :half] - value[:, half:]
    parts = (even[:, :quarter] + even[:, quarter:], even[:, :quarter] - even[:, quarter:], odd)
    return jnp.concatenate([dot3(split(p), read_pair(t)) for p, t in zip(parts, tables)], axis=1)


def periodic_inverse(value, tables):
    half, quarter = value.shape[1] // 2, value.shape[1] // 4
    parts = (value[:, :quarter], value[:, quarter:half], value[:, half:])
    four, two, odd = [dot3(split(p), read_pair(t), ((1,), (1,))) for p, t in zip(parts, tables)]
    even = jnp.concatenate([four + two, four - two], axis=1)
    return jnp.concatenate([even + odd, even - odd], axis=1)


def power(base, exponent):
    result = None
    while exponent:
        if exponent & 1:
            result = base if result is None else result * base
        base = base * base
        exponent >>= 1
    return result


def recurrence_root(sine):
    half = 0.5 * jnp.sqrt(sine)
    root = jnp.sqrt(1.0 + half * half) - half
    return root * root


def first_sweeps(load, root, top, above, store, levels):
    value = None
    for level in range(levels):
        value = load(level) if value is None else load(level) + root * value
        store[level] = value
    last = value
    value = top * value if above is None else top * value + above
    for level in range(levels - 1, -1, -1):
        value = root * (value - store[level])
    return (value, last)


def second_sweeps(load, start, root, top, above, store, levels, emit):
    value = start
    for level in range(levels):
        value = root * value if load is None else load(level) + root * value
        store[level] = value
    value = top * value if above is None else top * value + above
    for level in range(levels - 1, -1, -1):
        value = root * (value - store[level])
        emit(level, value)


def block_fluxes(ends, weights_ref, vectors_ref, levels, out_ref):
    blocks = len(ends)
    one = lambda dims, b: lax.dot_general(
        vectors_ref[...], b, (dims, ((), ())), precision=lax.Precision.HIGHEST, preferred_element_type=F32
    )
    upper = lower = None
    for block in range(blocks):
        even_next, odd_next = ends[(block + 1) % blocks]
        even, odd = ends[block]
        jump = one(((0,), (0,)), (even_next + odd_next) - (even - odd))
        up, low = weights_ref[0, block] * jump, weights_ref[1, block] * jump
        upper = up if upper is None else upper + up
        lower = low if lower is None else lower + low
    upper, lower = one(((1,), (0,)), upper), one(((1,), (0,)), lower)
    width = upper.shape[1]
    is_even = lax.broadcasted_iota(jnp.int32, (8, width), 0) % 2 == 0
    for level in range(levels):
        up, low = upper[level : level + 1], lower[level : level + 1]
        out_ref[level] = jnp.where(is_even, up - low, -up - low)


def fold_ends(total, out_ref, levels):
    is_even = lax.broadcasted_iota(jnp.int32, total.shape[1:], 0) % 2 == 0
    for level in range(levels):
        value = total[level]
        out_ref[0, level : level + 1] = jnp.sum(jnp.where(is_even, value, 0.0), axis=0, keepdims=True)
        out_ref[1, level : level + 1] = jnp.sum(jnp.where(is_even, 0.0, value), axis=0, keepdims=True)


def forward_kernel(
    levels, tile, ids_ref, w_new_ref, w_hbm, div_ref, t0h, t0l, t1h, t1l, t2h, t2l, ch, cl, root_ref, inv_ref,
    start_ref, top_ref, end_ref, field_hbm, edge_ref, ends_ref, corr_hbm, field, w_rows, above, lowest, store, total,
    sems, w_sems,
):
    step = pl.program_id(0)
    tables = ((t0h, t0l), (t1h, t1l), (t2h, t2l))

    pairs = levels // 2

    @pl.when(step == 0)
    def _():
        loads = chunk_copies(w_hbm, w_rows, w_sems)
        for load in loads:
            load.start()
        above[...] = jnp.zeros_like(above)
        total[...] = jnp.zeros_like(total)
        for load in loads:
            load.wait()
        put_cells(ids_ref, w_new_ref, w_rows)
        pltpu.make_async_copy(w_rows, corr_hbm, sems.at[1]).start()

    row_count = above.shape[0]

    @pl.when(step < pairs)
    def _():
        low = pl.multiple_of((pairs - 1 - step) * 2 * row_count, 2 * row_count)
        value = w_rows[pl.ds(low, 2 * row_count)]
        lower, upper = value[:row_count], value[row_count:]
        source = jnp.concatenate([div_ref[0] + (upper - lower), div_ref[1] + (above[...] - upper)], axis=0)
        modes = periodic_forward(source, tables)
        for k in range(2):
            part = modes[k * row_count : (k + 1) * row_count]
            field[(pairs - 1 - step) * 2 + k] = dot3(read_pair((ch, cl)), split(part))
        above[...] = lower

    @pl.when(step == pairs - 1)
    def _():
        pltpu.make_async_copy(field, field_hbm, sems.at[0]).start()
        lowest[...] = dot3(read_pair((ch, cl)), split(periodic_forward(w_rows[:row_count], tables)))

    @pl.when(step >= pairs)
    def _():
        def rows_of(sub, _):
            here = pl.multiple_of(sub * 8, 8)
            rows = pl.ds(here, 8)
            full = pl.ds(pl.multiple_of((step - pairs) * tile + here, 8), 8)
            root, top = root_ref[rows], top_ref[rows]
            load = lambda level: field[level, full]
            first, _ = first_sweeps(load, root, top, None, store, levels)
            edge_ref[0, rows] = first * inv_ref[rows] - lowest[full]
            weight = end_ref[rows, :1]

            def emit(level, value):
                total[level] += weight * value
                if level == levels - 1:
                    edge_ref[1, rows] = value

            second_sweeps(load, first * start_ref[rows], root, top, None, store, levels, emit)
            return 0

        lax.fori_loop(0, tile // 8, rows_of, 0)

    @pl.when(step == pl.num_programs(0) - 1)
    def _():
        fold_ends(total, ends_ref, levels)
        pltpu.make_async_copy(w_rows, corr_hbm, sems.at[1]).wait()
        pltpu.make_async_copy(field, field_hbm, sems.at[0]).wait()


def edge_kernel(
    levels, edge_ref, ends_ref, weights_ref, vectors_ref, root_ref, inv_ref, start_ref, top_ref, end_ref, ch, cl,
    out_ref, pattern, store, fixed,
):
    block_fluxes(
        [(ends_ref[b, 0], ends_ref[b, 1]) for b in range(ends_ref.shape[0])], weights_ref, vectors_ref, levels, pattern
    )

    def rows_of(sub, _):
        rows = pl.ds(pl.multiple_of(sub * 8, 8), 8)
        root, top = root_ref[rows], top_ref[rows]
        first, last = first_sweeps(lambda level: pattern[level], root, top, None, store, levels)
        weight = end_ref[rows, :1]
        fixed[0, rows] = edge_ref[0, rows] - weight * (first * inv_ref[rows])
        last = last + power(root, levels) * (first * start_ref[rows])
        fixed[1, rows] = edge_ref[1, rows] - weight * (root * (top - 1.0) * last)
        return 0

    lax.fori_loop(0, edge_ref.shape[1] // 8, rows_of, 0)
    for side in range(2):
        value = dot3(split(fixed[side].T), read_pair((ch, cl)))
        out_ref[:, side] = value.reshape(out_ref.shape[0], out_ref.shape[2], out_ref.shape[3])


def join_start(levels, near_top, root):
    square = root * root
    sums = jnp.ones_like(root)
    for _ in range(1, levels):
        sums = 1.0 + square * sums
    whole = power(root, 2 * levels)
    one = 1.0 / (sums + whole)
    near = -root * sums * one
    far = -power(root, levels) * one
    part = power(root, 2 * levels - 1)
    bottom = -root * (1.0 + part) / (1.0 + whole * root)
    pairs = (1.0 + root) * sums
    top = -root * (pairs - part) / (pairs + whole)
    return (near, far, jnp.where(near_top, top, bottom), jnp.where(near_top, bottom, top))


def join_chain(load, blocks, near, far, beta):
    alpha = load(0, 1)
    alphas, betas, heads, slopes = [alpha], [beta], [None], [None]
    for block in range(1, blocks):
        scale = 1.0 / (1.0 - near * beta)
        head = (load(block, 0) - near * alpha) * scale
        slope = far * scale
        alpha = load(block, 1) - far * alpha + far * beta * head
        beta = near + far * beta * slope
        alphas.append(alpha)
        betas.append(beta)
        heads.append(head)
        slopes.append(slope)
    return (alphas, betas, heads, slopes)


def chain_place(block, blocks, half):
    return block + half * (blocks - 1 - 2 * block)


def gather_modes_kernel(levels, px_count, half_ref, edge_ref, t0h, t0l, t1h, t1l, t2h, t2l, root_ref, out_ref, alpha_ref):
    blocks, _, rows, _ = out_ref.shape
    half = half_ref[0]
    for block in range(blocks):
        for side in range(2):
            whole = jnp.concatenate([edge_ref[i * blocks + block, side] for i in range(px_count)], axis=1)
            out_ref[block, side] = whole
    flat = out_ref[...].reshape(blocks * 2 * rows, out_ref.shape[3])
    out_ref[...] = periodic_forward(flat, ((t0h, t0l), (t1h, t1l), (t2h, t2l))).reshape(out_ref.shape)

    def rows_of(sub, _):
        here = pl.ds(pl.multiple_of(sub * 8, 8), 8)
        near, far, own, _ = join_start(levels, half == 1, root_ref[here])
        load = lambda block, outer: out_ref[chain_place(block, blocks, half), jnp.abs(outer - half), here]
        alpha_ref[here] = join_chain(load, blocks, near, far, own)[0][-1]
        return 0

    lax.fori_loop(0, rows // 8, rows_of, 0)


def join_kernel(
    levels, px_count, half_ref, modes_ref, alpha_ref, t0h, t0l, t1h, t1l, t2h, t2l, root_ref, out_ref, modes
):
    blocks, _, rows, _ = modes_ref.shape
    half = half_ref[0]
    width = out_ref.shape[3]

    def rows_of(sub, _):
        here = pl.ds(pl.multiple_of(sub * 8, 8), 8)
        near, far, own, other = join_start(levels, half == 1, root_ref[here])
        load = lambda block, outer: modes_ref[chain_place(block, blocks, half), jnp.abs(outer - half), here]
        alphas, betas, heads, slopes = join_chain(load, blocks, near, far, own)
        for _ in range(1, blocks):
            other = near + far * other * (far / (1.0 - near * other))
        met = alpha_ref[here]
        outer = (met - other * alphas[-1]) / (1.0 - other * betas[-1])
        for block in range(blocks - 1, -1, -1):
            place = chain_place(block, blocks, half)
            modes[place, 1 - half, here] = outer
            if block:
                outer = heads[block] - slopes[block] * outer
                modes[place, half, here] = alphas[block - 1] - betas[block - 1] * outer
            else:
                modes[place, half, here] = jnp.zeros_like(outer)
        return 0

    lax.fori_loop(0, rows // 8, rows_of, 0)
    flat = modes[...].reshape(blocks * 2 * rows, modes.shape[3])
    whole = periodic_inverse(flat, ((t0h, t0l), (t1h, t1l), (t2h, t2l))).reshape(modes.shape)
    for block in range(blocks):
        for side in range(2):
            for i in range(px_count):
                out_ref[i * blocks + block, side] = whole[block, side, :, i * width : (i + 1) * width]


def spread_kernel(levels, joined_ref, ch, cl, root_ref, start_ref, below_ref, top_ref, end_ref, out_ref, ends_ref, store, total):
    kx_width = joined_ref.shape[0] * joined_ref.shape[2]
    for side in range(2):
        value = joined_ref[:, side].reshape(kx_width, joined_ref.shape[3])
        out_ref[side] = dot3(read_pair((ch, cl)), split(value), ((1,), (1,)))
    total[...] = jnp.zeros_like(total)

    def rows_of(sub, _):
        rows = pl.ds(pl.multiple_of(sub * 8, 8), 8)
        root, top = root_ref[rows], top_ref[rows]
        below, above = out_ref[0, rows], out_ref[1, rows]
        start = start_ref[rows] * (power(root, levels) * above) - below_ref[rows] * below
        weight = end_ref[rows, :1]

        def emit(level, value):
            total[level] += weight * value

        second_sweeps(None, start, root, top, above, store, levels, emit)
        return 0

    lax.fori_loop(0, out_ref.shape[1] // 8, rows_of, 0)
    fold_ends(total, ends_ref, levels)


def inverse_kernel(
    levels, tile, place_ref, field_ref, sides_ref, ends_ref, more_ref, weights_ref, vectors_ref, root_ref, start_ref,
    below_ref, top_ref, end_ref, t0h, t0l, t1h, t1l, t2h, t2l, ch, cl, w_ref, roof_ref, out_ref, field, pattern, store,
):
    step = pl.program_id(0)
    tiles = pl.num_programs(0) - levels // 2
    tables = ((t0h, t0l), (t1h, t1l), (t2h, t2l))

    @pl.when(step == 0)
    def _():
        ends = [
            (ends_ref[b, 0] + more_ref[b, 0], ends_ref[b, 1] + more_ref[b, 1]) for b in range(ends_ref.shape[0])
        ]
        block_fluxes(ends, weights_ref, vectors_ref, levels, pattern)

    @pl.when(step < tiles)
    def _():
        def rows_of(sub, _):
            here = pl.multiple_of(sub * 8, 8)
            rows = pl.ds(here, 8)
            full = pl.ds(pl.multiple_of(step * tile + here, 8), 8)
            root, top = root_ref[rows], top_ref[rows]
            below, above = sides_ref[0, rows], sides_ref[1, rows]
            weight = end_ref[rows, :1]
            load = lambda level: field_ref[level, rows] - weight * pattern[level]
            first, _ = first_sweeps(load, root, top, above, store, levels)
            start = start_ref[rows] * first - below_ref[rows] * below
            held = []

            def emit(level, value):
                if held:
                    field[level + 1, full] = held.pop() - value
                held.append(value)

            second_sweeps(load, start, root, top, above, store, levels, emit)
            field[0, full] = jnp.where(place_ref[0] == 0, 0.0, held[0] - below)
            return 0

        lax.fori_loop(0, tile // 8, rows_of, 0)

    @pl.when(step >= tiles)
    def _():
        level = (step - tiles) * 2
        rows_y = [dot3(read_pair((ch, cl)), split(field[level + k])) for k in range(2)]
        slope = periodic_inverse(jnp.concatenate(rows_y, axis=0), tables)
        count = roof_ref.shape[0]
        for k in range(2):
            solid = place_ref[0] * levels + level + k < roof_ref[...]
            out_ref[k] = jnp.where(solid, 0.0, w_ref[k] - slope[k * count : (k + 1) * count])


def facet_places(ids, width):
    safe = jnp.maximum(ids, 0)
    row, column = safe // width, safe % width
    return jnp.stack([row // 8, column // 128, jnp.where(ids < 0, -1, row % 8 * 128 + column % 128)])


def tile_at(places_ref, facet):
    return (
        pl.ds(pl.multiple_of(places_ref[0, facet] * 8, 8), 8),
        pl.ds(pl.multiple_of(places_ref[1, facet] * 128, 128), 128),
    )


def pair_at(places_ref, facet):
    return (
        pl.ds(pl.multiple_of(lax.shift_right_logical(places_ref[0, facet], 1) * 16, 16), 16),
        pl.ds(pl.multiple_of(places_ref[1, facet] * 128, 128), 128),
    )


def pick_cells(ids_ref, ref, rows_ref, flat_ref):
    sublane = lax.broadcasted_iota(jnp.int32, (8, 128), 0)
    position = sublane * 128 + lax.broadcasted_iota(jnp.int32, (8, 128), 1)

    def pick(i, _):
        rows = None
        for lane in range(8):
            facet = i * 8 + lane
            mark = ids_ref[2, facet]
            if ref.dtype == F32:
                tile = ref[tile_at(ids_ref, facet)]
            else:
                both = ref[pair_at(ids_ref, facet)].astype(F32)
                tile = jnp.where(ids_ref[0, facet] & 1 == 0, both[:8], both[8:])
            tile = jnp.where(position == mark, tile, 0.0)
            tile = pltpu.roll(tile, (lane - lax.shift_right_arithmetic(mark, 7)) & 7, 0)
            rows = tile if rows is None else jnp.where(sublane == lane, tile, rows)
        rows_ref[pl.ds(pl.multiple_of(i * 8, 8), 8)] = rows

    group_count = rows_ref.shape[0] // 8
    per_trip = math.gcd(group_count, 8)

    def trip(i, _):
        for k in range(per_trip):
            pick(i * per_trip + k, None)
        return 0

    lax.fori_loop(0, group_count // per_trip, trip, 0)
    ones = jnp.ones((8, 128), F32)
    for group in range(flat_ref.shape[0]):
        rows = rows_ref[group * 128 : (group + 1) * 128]
        flat = lax.dot_general(
            ones, rows, (((1,), (1,)), ((), ())), precision=lax.Precision.HIGHEST, preferred_element_type=F32
        )
        flat_ref[group : group + 1] = flat[:1]


def level_solve_tables(sine, levels, is_first, is_last):
    root = recurrence_root(sine)
    top = jnp.where(is_last, root / (1.0 + root), 0.0)
    square = root * root
    kappa = jnp.zeros_like(root)
    for _ in range(levels):
        kappa = square * (1.0 + kappa)
    decay = power(root, levels)
    inverse = 1.0 / root
    bottom = jnp.where(is_first, 1.0 - inverse, 1.0)
    inv = 1.0 / (1.0 + bottom * (kappa - top * decay * decay))
    return (root, inv, bottom * inv, inv * inverse, top)


CHUNKS = 8


def chunk_copies(source, target, sems):
    rows = source.shape[0] // CHUNKS
    parts = [pl.ds(i * rows, rows) for i in range(CHUNKS)]
    return [pltpu.make_async_copy(source.at[p], target.at[p], sems.at[i]) for i, p in enumerate(parts)]


def gather_kernel(
    levels, ids_ref, ends_ref, w_hbm, sin_x_ref, sin_y_ref, out_ref, o0, o1, o2, o3, o4, rows_ref, w_ref, tables, sems,
    w_sems,
):
    w_parts = chunk_copies(w_hbm, w_ref, w_sems)
    for copy in w_parts:
        copy.start()

    def fill(i, _):
        rows = pl.ds(pl.multiple_of(i * 8, 8), 8)
        sine = sin_y_ref[rows, :1] + sin_x_ref[...]
        for k, value in enumerate(level_solve_tables(sine, levels, ends_ref[0] == 1, ends_ref[1] == 1)):
            tables[k, rows] = value
        return 0

    lax.fori_loop(0, sin_y_ref.shape[0] // 8, fill, 0)
    leaving = [pltpu.make_async_copy(tables.at[k], o, sems.at[k]) for k, o in enumerate((o0, o1, o2, o3, o4))]
    for copy in w_parts:
        copy.wait()
    for copy in leaving:
        copy.start()
    pick_cells(ids_ref, w_ref, rows_ref, out_ref)
    for copy in leaving:
        copy.wait()


def gather_temp_kernel(ids_ref, temp_ref, out_ref, rows_ref):
    pick_cells(ids_ref, temp_ref, rows_ref, out_ref)


def put_cells(ids_ref, new_ref, out):
    sublane = lax.broadcasted_iota(jnp.int32, (8, 128), 0)
    position = sublane * 128 + lax.broadcasted_iota(jnp.int32, (8, 128), 1)

    per_trip = math.gcd(new_ref.shape[0], 32)

    def put(i, _):
        for k in range(per_trip):
            facet = i * per_trip + k
            hit = position == ids_ref[2, facet]
            pltpu.store(out.at[tile_at(ids_ref, facet)], jnp.full((8, 128), new_ref[facet]), mask=hit)
        return 0

    lax.fori_loop(0, new_ref.shape[0] // per_trip, put, 0)


def theta_kernel(ids_ref, new_ref, temp_ref, out_ref, wide):
    rows = temp_ref.shape[0]
    chunk = math.gcd(rows, 64)

    def widen(i, _):
        here = pl.ds(pl.multiple_of(i * chunk, chunk), chunk)
        wide[here] = temp_ref[here].astype(F32)
        return 0

    def narrow(i, _):
        here = pl.ds(pl.multiple_of(i * chunk, chunk), chunk)
        out_ref[here] = wide[here].astype(BF16)
        return 0

    lax.fori_loop(0, rows // chunk, widen, 0)
    put_cells(ids_ref, new_ref, wide)
    lax.fori_loop(0, rows // chunk, narrow, 0)


def by_owner(flat, slots):
    shares = 128 // slots
    return jnp.stack([pltpu.roll(flat, (128 - k * slots) % 128, 1) if k else flat for k in range(shares)])


class Links:
    def __init__(self, sizes, slots, sent, received):
        names = ("px", "py_half", "py_low")
        self.sizes, self.shares = sizes, 128 // slots
        self.count = sizes[0] * sizes[1] * sizes[2]
        self.places = [lax.axis_index(name) for name in names]
        self.me = (self.places[0] * sizes[1] + self.places[1]) * sizes[2] + self.places[2]
        self.mine = (lax.rem(self.me, self.shares), lax.div(self.me, self.shares))
        self.sent, self.received = sent, received

    def each_peer(self, act):
        sizes, places = self.sizes, self.places

        def one(step, _):
            low = lax.rem(places[2] + step, sizes[2])
            rest = lax.div(step, sizes[2])
            middle = lax.rem(places[1] + rest, sizes[1])
            first = lax.rem(places[0] + lax.div(rest, sizes[1]), sizes[0])
            act((first * sizes[1] + middle) * sizes[2] + low, (first, middle, low))
            return 0

        lax.fori_loop(1, self.count, one, 0)

    def copy(self, phase, source, target, peer, device, landing):
        at = lambda ref, index: ref.at[lax.rem(index, self.shares), lax.div(index, self.shares)]
        return pltpu.make_async_remote_copy(
            at(source, peer),
            at(target, landing),
            self.sent.at[phase, peer],
            self.received.at[phase, landing],
            device_id=device,
            device_id_type=pl.DeviceIdType.MESH,
        )

    def greet(self):
        barrier = pltpu.get_barrier_semaphore()
        self.each_peer(
            lambda peer, device: pl.semaphore_signal(
                barrier, inc=1, device_id=device, device_id_type=pl.DeviceIdType.MESH
            )
        )
        return barrier

    def start(self, phase, source, target):
        self.each_peer(lambda peer, device: self.copy(phase, source, target, peer, device, self.me).start())
        target[self.mine] = source[self.mine]

    def finish(self, phase, source, target):
        self.each_peer(lambda peer, device: self.copy(phase, source, target, peer, device, peer).wait())


def from_owners(parts, slots):
    lane = lax.broadcasted_iota(jnp.int32, parts.shape[1:], 1)
    total = None
    for k in range(parts.shape[0]):
        part = jnp.where(lane < slots, parts[k], 0.0)
        part = pltpu.roll(part, k * slots, 1) if k else part
        total = part if total is None else total + part
    return total


def stress_kernel(
    sizes, slots, own_ref, facet_ref, drag_ref, heat_ref, back_ref, w_ref, sample, got, flux, back, sent, received
):
    links = Links(sizes, slots, sent, received)
    barrier = links.greet()
    sample[:, :, 0] = by_owner(own_ref[...], slots)
    pl.semaphore_wait(barrier, links.count - 1)
    links.start(0, sample, got)
    facet, drag, heat = [by_owner(ref[...], slots) for ref in (facet_ref, drag_ref, heat_ref)]
    links.finish(0, sample, got)
    w_cell = got[:, :, 0]
    speeds = jnp.sqrt(w_cell * w_cell + 0.25)
    flux[:, :, 0] = drag * speeds * w_cell
    flux[:, :, 1] = heat * speeds
    flux[:, :, 2] = facet
    links.start(1, flux, back)
    w_ref[...] = w_cell
    links.finish(1, flux, back)
    for k in range(3):
        back_ref[k] = from_owners(back[:, :, k], slots)


def facet_temp_kernel(
    sizes, slots, own_ref, facet_ref, radiation_ref, capacity_ref, heat_ref, w_ref, new_ref, sample, got, sent, received
):
    links = Links(sizes, slots, sent, received)
    barrier = links.greet()
    sample[:, :, 0] = by_owner(own_ref[...], slots)
    pl.semaphore_wait(barrier, links.count - 1)
    links.start(0, sample, got)
    facet, radiation, capacity, heat = [
        by_owner(ref[...], slots) for ref in (facet_ref, radiation_ref, capacity_ref, heat_ref)
    ]
    w_cell = w_ref[...]
    scale = heat * jnp.sqrt(w_cell * w_cell + 0.25)
    links.finish(0, sample, got)
    flux = scale * (facet - got[:, :, 0])
    new_ref[...] = from_owners(facet + (radiation - flux - 0.5 * facet) / capacity, slots)


def facet_sums(ids, returned):
    same = ids[:, None] == ids[None, :]
    return jnp.sum(jnp.where(same, returned.reshape(1, -1), 0.0), axis=1)


def near_walls(w_rows, sin_x, sin_y, ends, ids, places, facet_temp, drag_coef, heat_coef):
    count = ids.shape[0]
    sizes = tuple(lax.axis_size(name) for name in ("px", "py_half", "py_low"))
    slots = count // (sizes[0] * sizes[1] * sizes[2])
    flat = (count // 128, 128)
    rows, width = sin_y.shape[0], sin_x.shape[1]
    own, *tables = pl.pallas_call(
        lambda *refs: gather_kernel(w_rows.shape[0] // rows, *refs),
        out_shape=[jax.ShapeDtypeStruct(flat, F32)] + [jax.ShapeDtypeStruct((rows, width), F32)] * 5,
        in_specs=[SMEM, SMEM, HBM, VMEM, VMEM],
        out_specs=[VMEM] + [HBM] * 5,
        scratch_shapes=[
            pltpu.VMEM((count, 128), F32),
            pltpu.VMEM(w_rows.shape, F32),
            pltpu.VMEM((5, rows, width), F32),
            pltpu.SemaphoreType.DMA((5,)),
            pltpu.SemaphoreType.DMA((CHUNKS,)),
        ],
        compiler_params=PARAMS,
        name="facet_gather",
    )(places, ends, w_rows, sin_x, sin_y)
    by_rows = (128 // slots, flat[0], 128)
    tall = lambda values: pltpu.VMEM((128 // slots, flat[0], values, 128), F32)
    returned, w_cell = pl.pallas_call(
        lambda *refs: stress_kernel(sizes, slots, *refs),
        out_shape=(jax.ShapeDtypeStruct((3, *flat), F32), jax.ShapeDtypeStruct(by_rows, F32)),
        in_specs=[VMEM] * 4,
        out_specs=(VMEM, VMEM),
        scratch_shapes=[tall(1), tall(1), tall(3), tall(3)]
        + [pltpu.SemaphoreType.DMA((2, sizes[0] * sizes[1] * sizes[2]))] * 2,
        compiler_params=pltpu.CompilerParams(collective_id=1, has_side_effects=True),
        name="stress_exchange",
    )(own, facet_temp.reshape(flat), drag_coef.reshape(flat), heat_coef.reshape(flat))
    return (own.reshape(count) - facet_sums(ids, returned[0]), returned, w_cell, tables)


def warm_air(temp_rows, ids, places, returned):
    count = ids.shape[0]
    flat = (count // 128, 128)
    own = pl.pallas_call(
        gather_temp_kernel,
        out_shape=jax.ShapeDtypeStruct(flat, F32),
        in_specs=[SMEM, VMEM],
        out_specs=VMEM,
        scratch_shapes=[pltpu.VMEM((count, 128), F32)],
        compiler_params=PARAMS,
        cost_estimate=pl.CostEstimate(flops=0, bytes_accessed=4 * temp_rows.size, transcendentals=0),
        name="temp_gather",
    )(places, temp_rows)
    heat_flux = returned[1] * (returned[2] - own)
    return (own, own.reshape(count) + facet_sums(ids, heat_flux))


def warm_facets(own, w_cell, facet_temp, net_radiation, heat_capacity, heat_coef):
    flat = own.shape
    sizes = tuple(lax.axis_size(name) for name in ("px", "py_half", "py_low"))
    slots = own.size // (sizes[0] * sizes[1] * sizes[2])
    tall = pltpu.VMEM((128 // slots, flat[0], 1, 128), F32)
    new_temp = pl.pallas_call(
        lambda *refs: facet_temp_kernel(sizes, slots, *refs),
        out_shape=jax.ShapeDtypeStruct(flat, F32),
        in_specs=[VMEM] * 6,
        out_specs=VMEM,
        scratch_shapes=[tall] * 2 + [pltpu.SemaphoreType.DMA((1, sizes[0] * sizes[1] * sizes[2]))] * 2,
        compiler_params=pltpu.CompilerParams(collective_id=2, has_side_effects=True),
        cost_estimate=pl.CostEstimate(flops=0, bytes_accessed=2**24, transcendentals=0),
        name="facet_temp",
    )(own, *[a.reshape(flat) for a in (facet_temp, net_radiation, heat_capacity, heat_coef)], w_cell)
    return new_temp.reshape(facet_temp.shape)


def body(
    horiz_div,
    w_star,
    air_temp,
    roof_level,
    facet_cells,
    facet_temp,
    net_radiation,
    heat_capacity,
    drag_coef,
    heat_coef,
):
    levels, rows, width = w_star.shape
    px_count, blocks = lax.axis_size("px"), lax.axis_size("py_low")
    py_count = 2 * blocks
    group = px_count * blocks
    place_x, place_y, half = lax.axis_index("px"), lax.axis_index(("py_half", "py_low")), lax.axis_index("py_half")
    own_kx = width // group
    y_cells = rows * px_count

    w_rows = w_star.reshape(levels * rows, width)
    temp_rows = air_temp.reshape(levels * rows, width)
    ids = facet_cells[0]
    places = facet_places(ids, width)
    x_parts, sin_x = periodic_tables(width)
    y_parts, sin_y = periodic_tables(y_cells)
    cosines, sin_block = cosine_table(rows)
    x_tables = [t for part in x_parts for t in two_halves(part)]
    y_tables = [t for part in y_parts for t in two_halves(part)]
    to_modes, to_rows = two_halves(cosines), two_halves(np.ascontiguousarray(cosines.T))
    sin_x = jnp.asarray(sin_x, F32)

    is_first, is_last = place_y == 0, place_y == py_count - 1
    w_near, returned, w_cell, (root, inv, start, from_below, top) = near_walls(
        w_rows,
        sin_x[None, :],
        jnp.asarray(np.repeat(sin_block[:, None], 128, axis=1), F32),
        jnp.stack([is_first, is_last]).astype(jnp.int32),
        ids,
        places,
        facet_temp[0],
        drag_coef[0],
        heat_coef[0],
    )

    end = np.where(np.arange(rows) == 0, np.sqrt(1.0 / rows), cosines[:, 0])
    end = jnp.asarray(np.repeat(end[:, None], 128, axis=1), F32)

    vectors, sin_z = level_tables(levels)
    pick = lambda three: jnp.where(is_first, three[0], jnp.where(is_last, three[2], three[1])).astype(F32)
    vectors, sin_z = pick(vectors), pick(sin_z)
    sine_z = sin_z[:, None] + sin_x[None, :]
    size_z = jnp.sqrt(sine_z)
    half_z = 0.5 * size_z
    cosh_z = jnp.sqrt(1.0 + half_z * half_z)
    half_step = cosh_z - half_z
    across = jnp.exp(2.0 * rows * jnp.log(half_step))
    scale = 1.0 / ((1.0 - across * across) * size_z)
    same_end = -half_step * (1.0 + across * across / (half_step * half_step)) * scale
    far_end = -2.0 * across * cosh_z * scale
    turns = np.arange(px_count)
    circulant = jnp.stack(
        [1.0 / (1.0 - 2.0 * same_end + 2.0 * math.cos(2.0 * math.pi * s / px_count) * far_end) for s in turns]
    )
    circulant = lax.optimization_barrier(circulant)
    phase_of = jnp.asarray(np.cos(2.0 * np.pi * turns[:, None] * turns[None, :] / px_count) / px_count, F32)
    offsets = jnp.stack([(place_x - turns) % px_count, (place_x - 1 - turns) % px_count])
    phases = phase_of[offsets]
    weights = jnp.sum(phases[:, :, :, None, None] * circulant[None, None], axis=2)

    mine = place_x * blocks + lax.axis_index("py_low")
    own_sin = lax.dynamic_slice_in_dim(sin_x, mine * own_kx, own_kx)
    join_root = recurrence_root(own_sin[:, None] + jnp.asarray(sin_y, F32)[None, :])

    tile = math.gcd(rows, 32)
    tiles = rows // tile
    flat = lambda i: pl.BlockSpec((tile, width), i)
    fixed = lambda a: pl.BlockSpec(a.shape, lambda i: (0,) * len(a.shape))
    pairs = levels // 2
    late = lambda i: (jnp.maximum(i - pairs, 0), 0)
    down = lambda i: (jnp.maximum(pairs - 1 - i, 0), 0, 0)
    slab = pl.BlockSpec((2, rows, width), down)
    end_late = pl.BlockSpec((tile, 128), late)
    ends_shape = jax.ShapeDtypeStruct((2, levels, width), F32)
    field, edges, ends, w_corr = pl.pallas_call(
        lambda *refs: forward_kernel(levels, tile, *refs),
        out_shape=(
            jax.ShapeDtypeStruct(w_star.shape, F32),
            jax.ShapeDtypeStruct((2, rows, width), F32),
            ends_shape,
            jax.ShapeDtypeStruct(w_rows.shape, F32),
        ),
        grid=(pairs + tiles,),
        in_specs=[SMEM, SMEM, HBM, slab] + [fixed(t) for t in (*x_tables, *to_modes)] + [flat(late)] * 4 + [end_late],
        out_specs=(
            HBM,
            pl.BlockSpec((2, tile, width), lambda i: (0, *late(i))),
            fixed(ends_shape),
            HBM,
        ),
        scratch_shapes=[
            pltpu.VMEM(w_star.shape, F32),
            pltpu.VMEM(w_rows.shape, F32),
            pltpu.VMEM((rows, width), F32),
            pltpu.VMEM((rows, width), F32),
            pltpu.VMEM((levels, 8, width), F32),
            pltpu.VMEM((levels, 8, width), F32),
            pltpu.SemaphoreType.DMA((2,)),
            pltpu.SemaphoreType.DMA((CHUNKS,)),
        ],
        compiler_params=PARAMS,
        name="forward",
    )(places, w_near, w_rows, horiz_div, *x_tables, *to_modes, root, inv, start, top, end)

    all_ends = lax.all_gather(ends, "px")
    packed = jax.ShapeDtypeStruct((group, 2, own_kx, rows), F32)
    working = [pltpu.VMEM((levels, 8, width), F32)] * 2
    edges = pl.pallas_call(
        lambda *refs: edge_kernel(levels, *refs),
        out_shape=packed,
        in_specs=[VMEM] * 11,
        out_specs=VMEM,
        scratch_shapes=working + [pltpu.VMEM((2, rows, width), F32)],
        compiler_params=SMALL,
        name="edges",
    )(edges, all_ends, weights, vectors, root, inv, start, top, end, *to_modes)
    w_cell, edges = lax.optimization_barrier((w_cell, edges))
    places_late, edges = lax.optimization_barrier((places, edges))
    temp_own, temp_near = warm_air(temp_rows, ids, places_late, returned)
    edges = lax.all_to_all(edges, ("px", "py_low"), split_axis=0, concat_axis=0, tiled=True)
    edges, temp_near = lax.optimization_barrier((edges, temp_near))
    half_id = half.astype(jnp.int32).reshape(1)
    modes, alpha = pl.pallas_call(
        lambda *refs: gather_modes_kernel(levels, px_count, *refs),
        out_shape=(
            jax.ShapeDtypeStruct((blocks, 2, own_kx, y_cells), F32),
            jax.ShapeDtypeStruct((own_kx, y_cells), F32),
        ),
        in_specs=[SMEM] + [VMEM] * 8,
        out_specs=(VMEM, VMEM),
        compiler_params=SMALL,
        name="gather_modes",
    )(half_id, edges, *y_tables, join_root)
    alpha, temp_own = lax.optimization_barrier((alpha, temp_own))
    new_temp = warm_facets(
        temp_own, w_cell, facet_temp[0], net_radiation[0], heat_capacity[0], heat_coef[0]
    )
    alpha = lax.ppermute(alpha, "py_half", [(0, 1), (1, 0)])
    alpha, new_temp = lax.optimization_barrier((alpha, new_temp))
    joined = pl.pallas_call(
        lambda *refs: join_kernel(levels, px_count, *refs),
        out_shape=packed,
        in_specs=[SMEM] + [VMEM] * 9,
        out_specs=VMEM,
        scratch_shapes=[pltpu.VMEM((blocks, 2, own_kx, y_cells), F32)],
        compiler_params=SMALL,
        name="join",
    )(half_id, modes, alpha, *y_tables, join_root)
    joined, temp_near = lax.optimization_barrier((joined, temp_near))
    theta_new = pl.pallas_call(
        theta_kernel,
        out_shape=jax.ShapeDtypeStruct(temp_rows.shape, BF16),
        in_specs=[SMEM, SMEM, VMEM],
        out_specs=VMEM,
        scratch_shapes=[pltpu.VMEM(temp_rows.shape, F32)],
        compiler_params=PARAMS,
        cost_estimate=pl.CostEstimate(flops=temp_rows.size, bytes_accessed=8 * temp_rows.size, transcendentals=0),
        name="theta",
    )(places, temp_near, temp_rows).reshape(air_temp.shape)
    joined = lax.all_to_all(joined, ("px", "py_low"), split_axis=0, concat_axis=0, tiled=True)
    sides, more = pl.pallas_call(
        lambda *refs: spread_kernel(levels, *refs),
        out_shape=(jax.ShapeDtypeStruct((2, rows, width), F32), ends_shape),
        in_specs=[VMEM] * 8,
        out_specs=(VMEM, VMEM),
        scratch_shapes=working,
        compiler_params=SMALL,
        name="spread",
    )(joined, *to_modes, root, start, from_below, top, end)
    more = lax.all_gather(more, "px")

    early = lambda i: (jnp.minimum(i, tiles - 1), 0)
    up = lambda i: (jnp.maximum(i - tiles, 0), 0, 0)
    slab = pl.BlockSpec((2, rows, width), up)
    w_new = pl.pallas_call(
        lambda *refs: inverse_kernel(levels, tile, *refs),
        out_shape=jax.ShapeDtypeStruct(w_star.shape, F32),
        grid=(tiles + pairs,),
        in_specs=[
            SMEM,
            pl.BlockSpec((levels, tile, width), lambda i: (0, *early(i))),
            pl.BlockSpec((2, tile, width), lambda i: (0, *early(i))),
        ]
        + [fixed(a) for a in (all_ends, more, weights, vectors)]
        + [flat(early)] * 4
        + [pl.BlockSpec((tile, 128), early)]
        + [fixed(t) for t in (*x_tables, *to_rows)]
        + [slab, fixed(roof_level)],
        out_specs=slab,
        scratch_shapes=[pltpu.VMEM(w_star.shape, F32)] + working,
        compiler_params=PARAMS,
        name="inverse",
    )(
        place_y.astype(jnp.int32).reshape(1),
        field,
        sides,
        all_ends,
        more,
        weights,
        vectors,
        root,
        start,
        from_below,
        top,
        end,
        *x_tables,
        *to_rows,
        w_corr.reshape(w_star.shape),
        roof_level,
    )
    return (w_new, theta_new, new_temp[None])


def solution(mesh):
    px_count, py_count = mesh.devices.shape
    split_mesh = jax.sharding.Mesh(
        mesh.devices.reshape(px_count, 2, py_count // 2), ("px", "py_half", "py_low")
    )
    py, every = ("py_half", "py_low"), ("px", "py_half", "py_low")
    placed = (P(py, "px", None),) * 3 + (P("px", None),) + (P(every, None),) * 6
    return jax.shard_map(
        body,
        mesh=split_mesh,
        in_specs=placed,
        out_specs=(P(py, "px", None), P(py, "px", None), P(every, None)),
        check_vma=False,
    )
```

```python
import math

import jax
import jax.numpy as jnp
import ml_dtypes
import numpy as np
from jax import lax
from jax.experimental import pallas as pl
from jax.experimental.pallas import tpu as pltpu
from jax.sharding import PartitionSpec as P

F32 = jnp.float32
BF16 = jnp.bfloat16
HBM = pl.BlockSpec(memory_space=pl.ANY)
VMEM = pl.BlockSpec(memory_space=pltpu.VMEM)
SMEM = pl.BlockSpec(memory_space=pltpu.SMEM)
PARAMS = pltpu.CompilerParams(vmem_limit_bytes=58 * 2**20)
SMALL = pltpu.CompilerParams(vmem_limit_bytes=28 * 2**20)


def two_halves(table):
    high = table.astype(ml_dtypes.bfloat16)
    low = (table - high.astype(np.float64)).astype(ml_dtypes.bfloat16)
    return (jnp.asarray(high), jnp.asarray(low))


def periodic_tables(size):
    half, quarter = size // 2, size // 4
    groups = (
        (np.arange(0, half + 1, 4), np.arange(4, half, 4), quarter),
        (np.arange(2, half, 4), np.arange(2, half, 4), quarter),
        (np.arange(1, half, 2), np.arange(1, half, 2), half),
    )
    tables, waves = [], []
    for cosines, sines, rows in groups:
        x = np.arange(rows)[:, None]
        norms = np.where((cosines == 0) | (cosines == half), np.sqrt(1.0 / size), np.sqrt(2.0 / size))
        tables.append(
            np.concatenate(
                [
                    norms * np.cos(2.0 * np.pi / size * (x * cosines % size)),
                    np.sqrt(2.0 / size) * np.sin(2.0 * np.pi / size * (x * sines % size)),
                ],
                axis=1,
            )
        )
        waves += [cosines, sines]
    waves = np.concatenate(waves)
    return (tables, 4.0 * np.sin(np.pi * waves / size) ** 2)


def cosine_table(size):
    modes = np.arange(size)[:, None]
    table = np.sqrt(2.0 / size) * np.cos(np.pi * modes * (2 * np.arange(size)[None, :] + 1) / (2 * size))
    table[0] = np.sqrt(1.0 / size)
    return (table, 4.0 * np.sin(np.pi * modes[:, 0] / (2 * size)) ** 2)


def level_tables(size):
    modes, levels = np.arange(size)[None, :], np.arange(size)[:, None]
    omegas = (
        np.pi * (2 * modes + 1) / (2 * size + 1),
        np.pi * (modes + 1) / (size + 1),
        np.pi * (modes + 1) / (size + 0.5),
    )
    vectors = (
        np.cos(omegas[0] * (levels + 0.5)),
        np.sin(omegas[1] * (levels + 1)),
        np.sin(omegas[2] * (levels + 1)),
    )
    vectors = [v / np.sqrt(np.sum(v * v, axis=0, keepdims=True)) for v in vectors]
    return (vectors, [4.0 * np.sin(o[0] / 2) ** 2 for o in omegas])


def split(value):
    high = value.astype(BF16)
    return (high, (value - high.astype(F32)).astype(BF16))


def dot3(left, right, dims=((1,), (0,))):
    one = lambda a, b: lax.dot_general(a, b, (dims, ((), ())), preferred_element_type=F32)
    free = 1 - dims[0][0]
    size = left[0].shape[free]
    both = one(jnp.concatenate(left, axis=free), right[0])
    return both[:size] + (both[size:] + one(left[0], right[1]))


def read_pair(refs):
    return (refs[0][...], refs[1][...])


def periodic_forward(value, tables):
    half, quarter = value.shape[1] // 2, value.shape[1] // 4
    even, odd = value[:, :half] + value[:, half:], value[:, :half] - value[:, half:]
    parts = (even[:, :quarter] + even[:, quarter:], even[:, :quarter] - even[:, quarter:], odd)
    return jnp.concatenate([dot3(split(p), read_pair(t)) for p, t in zip(parts, tables)], axis=1)


def periodic_inverse(value, tables):
    half, quarter = value.shape[1] // 2, value.shape[1] // 4
    parts = (value[:, :quarter], value[:, quarter:half], value[:, half:])
    four, two, odd = [dot3(split(p), read_pair(t), ((1,), (1,))) for p, t in zip(parts, tables)]
    even = jnp.concatenate([four + two, four - two], axis=1)
    return jnp.concatenate([even + odd, even - odd], axis=1)


def power(base, exponent):
    result = None
    while exponent:
        if exponent & 1:
            result = base if result is None else result * base
        base = base * base
        exponent >>= 1
    return result


def recurrence_root(sine):
    half = 0.5 * jnp.sqrt(sine)
    root = jnp.sqrt(1.0 + half * half) - half
    return root * root


def first_sweeps(load, root, top, above, store, levels):
    value = None
    for level in range(levels):
        value = load(level) if value is None else load(level) + root * value
        store[level] = value
    last = value
    value = top * value if above is None else top * value + above
    for level in range(levels - 1, -1, -1):
        value = root * (value - store[level])
    return (value, last)


def second_sweeps(load, start, root, top, above, store, levels, emit):
    value = start
    for level in range(levels):
        value = root * value if load is None else load(level) + root * value
        store[level] = value
    value = top * value if above is None else top * value + above
    for level in range(levels - 1, -1, -1):
        value = root * (value - store[level])
        emit(level, value)


def block_fluxes(ends, weights_ref, vectors_ref, levels, out_ref):
    blocks = len(ends)
    one = lambda dims, b: lax.dot_general(
        vectors_ref[...], b, (dims, ((), ())), precision=lax.Precision.HIGHEST, preferred_element_type=F32
    )
    upper = lower = None
    for block in range(blocks):
        even_next, odd_next = ends[(block + 1) % blocks]
        even, odd = ends[block]
        jump = one(((0,), (0,)), (even_next + odd_next) - (even - odd))
        up, low = weights_ref[0, block] * jump, weights_ref[1, block] * jump
        upper = up if upper is None else upper + up
        lower = low if lower is None else lower + low
    upper, lower = one(((1,), (0,)), upper), one(((1,), (0,)), lower)
    width = upper.shape[1]
    is_even = lax.broadcasted_iota(jnp.int32, (8, width), 0) % 2 == 0
    for level in range(levels):
        up, low = upper[level : level + 1], lower[level : level + 1]
        out_ref[level] = jnp.where(is_even, up - low, -up - low)


def fold_ends(total, out_ref, levels):
    is_even = lax.broadcasted_iota(jnp.int32, total.shape[1:], 0) % 2 == 0
    for level in range(levels):
        value = total[level]
        out_ref[0, level : level + 1] = jnp.sum(jnp.where(is_even, value, 0.0), axis=0, keepdims=True)
        out_ref[1, level : level + 1] = jnp.sum(jnp.where(is_even, 0.0, value), axis=0, keepdims=True)


def forward_kernel(
    levels, tile, ids_ref, w_new_ref, w_hbm, div_ref, t0h, t0l, t1h, t1l, t2h, t2l, ch, cl, root_ref, inv_ref,
    start_ref, top_ref, end_ref, field_hbm, edge_ref, ends_ref, corr_hbm, field, w_rows, above, lowest, store, total,
    sems, w_sems,
):
    step = pl.program_id(0)
    tables = ((t0h, t0l), (t1h, t1l), (t2h, t2l))

    pairs = levels // 2

    @pl.when(step == 0)
    def _():
        loads = chunk_copies(w_hbm, w_rows, w_sems)
        for load in loads:
            load.start()
        above[...] = jnp.zeros_like(above)
        total[...] = jnp.zeros_like(total)
        for load in loads:
            load.wait()
        put_cells(ids_ref, w_new_ref, w_rows)
        pltpu.make_async_copy(w_rows, corr_hbm, sems.at[1]).start()

    row_count = above.shape[0]

    @pl.when(step < pairs)
    def _():
        low = pl.multiple_of((pairs - 1 - step) * 2 * row_count, 2 * row_count)
        value = w_rows[pl.ds(low, 2 * row_count)]
        lower, upper = value[:row_count], value[row_count:]
        source = jnp.concatenate([div_ref[0] + (upper - lower), div_ref[1] + (above[...] - upper)], axis=0)
        modes = periodic_forward(source, tables)
        for k in range(2):
            part = modes[k * row_count : (k + 1) * row_count]
            field[(pairs - 1 - step) * 2 + k] = dot3(read_pair((ch, cl)), split(part))
        above[...] = lower

    @pl.when(step == pairs - 1)
    def _():
        pltpu.make_async_copy(field, field_hbm, sems.at[0]).start()
        lowest[...] = dot3(read_pair((ch, cl)), split(periodic_forward(w_rows[:row_count], tables)))

    @pl.when(step >= pairs)
    def _():
        def rows_of(sub, _):
            here = pl.multiple_of(sub * 8, 8)
            rows = pl.ds(here, 8)
            full = pl.ds(pl.multiple_of((step - pairs) * tile + here, 8), 8)
            root, top = root_ref[rows], top_ref[rows]
            load = lambda level: field[level, full]
            first, _ = first_sweeps(load, root, top, None, store, levels)
            edge_ref[0, rows] = first * inv_ref[rows] - lowest[full]
            weight = end_ref[rows, :1]

            def emit(level, value):
                total[level] += weight * value
                if level == levels - 1:
                    edge_ref[1, rows] = value

            second_sweeps(load, first * start_ref[rows], root, top, None, store, levels, emit)
            return 0

        lax.fori_loop(0, tile // 8, rows_of, 0)

    @pl.when(step == pl.num_programs(0) - 1)
    def _():
        fold_ends(total, ends_ref, levels)
        pltpu.make_async_copy(w_rows, corr_hbm, sems.at[1]).wait()
        pltpu.make_async_copy(field, field_hbm, sems.at[0]).wait()


def edge_kernel(
    levels, edge_ref, ends_ref, weights_ref, vectors_ref, root_ref, inv_ref, start_ref, top_ref, end_ref, ch, cl,
    out_ref, pattern, store, fixed,
):
    block_fluxes(
        [(ends_ref[b, 0], ends_ref[b, 1]) for b in range(ends_ref.shape[0])], weights_ref, vectors_ref, levels, pattern
    )

    def rows_of(sub, _):
        rows = pl.ds(pl.multiple_of(sub * 8, 8), 8)
        root, top = root_ref[rows], top_ref[rows]
        first, last = first_sweeps(lambda level: pattern[level], root, top, None, store, levels)
        weight = end_ref[rows, :1]
        fixed[0, rows] = edge_ref[0, rows] - weight * (first * inv_ref[rows])
        last = last + power(root, levels) * (first * start_ref[rows])
        fixed[1, rows] = edge_ref[1, rows] - weight * (root * (top - 1.0) * last)
        return 0

    lax.fori_loop(0, edge_ref.shape[1] // 8, rows_of, 0)
    for side in range(2):
        value = dot3(split(fixed[side].T), read_pair((ch, cl)))
        out_ref[:, side] = value.reshape(out_ref.shape[0], out_ref.shape[2], out_ref.shape[3])


def join_start(levels, near_top, root):
    square = root * root
    sums = jnp.ones_like(root)
    for _ in range(1, levels):
        sums = 1.0 + square * sums
    whole = power(root, 2 * levels)
    one = 1.0 / (sums + whole)
    near = -root * sums * one
    far = -power(root, levels) * one
    part = power(root, 2 * levels - 1)
    bottom = -root * (1.0 + part) / (1.0 + whole * root)
    pairs = (1.0 + root) * sums
    top = -root * (pairs - part) / (pairs + whole)
    return (near, far, jnp.where(near_top, top, bottom), jnp.where(near_top, bottom, top))


def join_chain(load, blocks, near, far, beta):
    alpha = load(0, 1)
    alphas, betas, heads, slopes = [alpha], [beta], [None], [None]
    for block in range(1, blocks):
        scale = 1.0 / (1.0 - near * beta)
        head = (load(block, 0) - near * alpha) * scale
        slope = far * scale
        alpha = load(block, 1) - far * alpha + far * beta * head
        beta = near + far * beta * slope
        alphas.append(alpha)
        betas.append(beta)
        heads.append(head)
        slopes.append(slope)
    return (alphas, betas, heads, slopes)


def chain_place(block, blocks, half):
    return block + half * (blocks - 1 - 2 * block)


def gather_modes_kernel(levels, px_count, half_ref, edge_ref, t0h, t0l, t1h, t1l, t2h, t2l, root_ref, out_ref, alpha_ref):
    blocks, _, rows, _ = out_ref.shape
    half = half_ref[0]
    for block in range(blocks):
        for side in range(2):
            whole = jnp.concatenate([edge_ref[i * blocks + block, side] for i in range(px_count)], axis=1)
            out_ref[block, side] = whole
    flat = out_ref[...].reshape(blocks * 2 * rows, out_ref.shape[3])
    out_ref[...] = periodic_forward(flat, ((t0h, t0l), (t1h, t1l), (t2h, t2l))).reshape(out_ref.shape)

    def rows_of(sub, _):
        here = pl.ds(pl.multiple_of(sub * 8, 8), 8)
        near, far, own, _ = join_start(levels, half == 1, root_ref[here])
        load = lambda block, outer: out_ref[chain_place(block, blocks, half), jnp.abs(outer - half), here]
        alpha_ref[here] = join_chain(load, blocks, near, far, own)[0][-1]
        return 0

    lax.fori_loop(0, rows // 8, rows_of, 0)


def join_kernel(
    levels, px_count, half_ref, modes_ref, alpha_ref, t0h, t0l, t1h, t1l, t2h, t2l, root_ref, out_ref, modes
):
    blocks, _, rows, _ = modes_ref.shape
    half = half_ref[0]
    width = out_ref.shape[3]

    def rows_of(sub, _):
        here = pl.ds(pl.multiple_of(sub * 8, 8), 8)
        near, far, own, other = join_start(levels, half == 1, root_ref[here])
        load = lambda block, outer: modes_ref[chain_place(block, blocks, half), jnp.abs(outer - half), here]
        alphas, betas, heads, slopes = join_chain(load, blocks, near, far, own)
        for _ in range(1, blocks):
            other = near + far * other * (far / (1.0 - near * other))
        met = alpha_ref[here]
        outer = (met - other * alphas[-1]) / (1.0 - other * betas[-1])
        for block in range(blocks - 1, -1, -1):
            place = chain_place(block, blocks, half)
            modes[place, 1 - half, here] = outer
            if block:
                outer = heads[block] - slopes[block] * outer
                modes[place, half, here] = alphas[block - 1] - betas[block - 1] * outer
            else:
                modes[place, half, here] = jnp.zeros_like(outer)
        return 0

    lax.fori_loop(0, rows // 8, rows_of, 0)
    flat = modes[...].reshape(blocks * 2 * rows, modes.shape[3])
    whole = periodic_inverse(flat, ((t0h, t0l), (t1h, t1l), (t2h, t2l))).reshape(modes.shape)
    for block in range(blocks):
        for side in range(2):
            for i in range(px_count):
                out_ref[i * blocks + block, side] = whole[block, side, :, i * width : (i + 1) * width]


def spread_kernel(levels, joined_ref, ch, cl, root_ref, start_ref, below_ref, top_ref, end_ref, out_ref, ends_ref, store, total):
    kx_width = joined_ref.shape[0] * joined_ref.shape[2]
    for side in range(2):
        value = joined_ref[:, side].reshape(kx_width, joined_ref.shape[3])
        out_ref[side] = dot3(read_pair((ch, cl)), split(value), ((1,), (1,)))
    total[...] = jnp.zeros_like(total)

    def rows_of(sub, _):
        rows = pl.ds(pl.multiple_of(sub * 8, 8), 8)
        root, top = root_ref[rows], top_ref[rows]
        below, above = out_ref[0, rows], out_ref[1, rows]
        start = start_ref[rows] * (power(root, levels) * above) - below_ref[rows] * below
        weight = end_ref[rows, :1]

        def emit(level, value):
            total[level] += weight * value

        second_sweeps(None, start, root, top, above, store, levels, emit)
        return 0

    lax.fori_loop(0, out_ref.shape[1] // 8, rows_of, 0)
    fold_ends(total, ends_ref, levels)


def inverse_kernel(
    levels, tile, place_ref, field_ref, sides_ref, ends_ref, more_ref, weights_ref, vectors_ref, root_ref, start_ref,
    below_ref, top_ref, end_ref, t0h, t0l, t1h, t1l, t2h, t2l, ch, cl, w_ref, roof_ref, out_ref, field, pattern, store,
):
    step = pl.program_id(0)
    tiles = pl.num_programs(0) - levels // 2
    tables = ((t0h, t0l), (t1h, t1l), (t2h, t2l))

    @pl.when(step == 0)
    def _():
        ends = [
            (ends_ref[b, 0] + more_ref[b, 0], ends_ref[b, 1] + more_ref[b, 1]) for b in range(ends_ref.shape[0])
        ]
        block_fluxes(ends, weights_ref, vectors_ref, levels, pattern)

    @pl.when(step < tiles)
    def _():
        def rows_of(sub, _):
            here = pl.multiple_of(sub * 8, 8)
            rows = pl.ds(here, 8)
            full = pl.ds(pl.multiple_of(step * tile + here, 8), 8)
            root, top = root_ref[rows], top_ref[rows]
            below, above = sides_ref[0, rows], sides_ref[1, rows]
            weight = end_ref[rows, :1]
            load = lambda level: field_ref[level, rows] - weight * pattern[level]
            first, _ = first_sweeps(load, root, top, above, store, levels)
            start = start_ref[rows] * first - below_ref[rows] * below
            held = []

            def emit(level, value):
                if held:
                    field[level + 1, full] = held.pop() - value
                held.append(value)

            second_sweeps(load, start, root, top, above, store, levels, emit)
            field[0, full] = jnp.where(place_ref[0] == 0, 0.0, held[0] - below)
            return 0

        lax.fori_loop(0, tile // 8, rows_of, 0)

    @pl.when(step >= tiles)
    def _():
        level = (step - tiles) * 2
        rows_y = [dot3(read_pair((ch, cl)), split(field[level + k])) for k in range(2)]
        slope = periodic_inverse(jnp.concatenate(rows_y, axis=0), tables)
        count = roof_ref.shape[0]
        for k in range(2):
            solid = place_ref[0] * levels + level + k < roof_ref[...]
            out_ref[k] = jnp.where(solid, 0.0, w_ref[k] - slope[k * count : (k + 1) * count])


def facet_places(ids, width):
    safe = jnp.maximum(ids, 0)
    row, column = safe // width, safe % width
    return jnp.stack([row // 8, column // 128, jnp.where(ids < 0, -1, row % 8 * 128 + column % 128)])


def tile_at(places_ref, facet):
    return (
        pl.ds(pl.multiple_of(places_ref[0, facet] * 8, 8), 8),
        pl.ds(pl.multiple_of(places_ref[1, facet] * 128, 128), 128),
    )


def pair_at(places_ref, facet):
    return (
        pl.ds(pl.multiple_of(lax.shift_right_logical(places_ref[0, facet], 1) * 16, 16), 16),
        pl.ds(pl.multiple_of(places_ref[1, facet] * 128, 128), 128),
    )


def pick_cells(ids_ref, ref, rows_ref, flat_ref):
    sublane = lax.broadcasted_iota(jnp.int32, (8, 128), 0)
    position = sublane * 128 + lax.broadcasted_iota(jnp.int32, (8, 128), 1)

    def pick(i, _):
        rows = None
        for lane in range(8):
            facet = i * 8 + lane
            mark = ids_ref[2, facet]
            if ref.dtype == F32:
                tile = ref[tile_at(ids_ref, facet)]
            else:
                both = ref[pair_at(ids_ref, facet)].astype(F32)
                tile = jnp.where(ids_ref[0, facet] & 1 == 0, both[:8], both[8:])
            tile = jnp.where(position == mark, tile, 0.0)
            tile = pltpu.roll(tile, (lane - lax.shift_right_arithmetic(mark, 7)) & 7, 0)
            rows = tile if rows is None else jnp.where(sublane == lane, tile, rows)
        rows_ref[pl.ds(pl.multiple_of(i * 8, 8), 8)] = rows

    group_count = rows_ref.shape[0] // 8
    per_trip = math.gcd(group_count, 8)

    def trip(i, _):
        for k in range(per_trip):
            pick(i * per_trip + k, None)
        return 0

    lax.fori_loop(0, group_count // per_trip, trip, 0)
    ones = jnp.ones((8, 128), F32)
    for group in range(flat_ref.shape[0]):
        rows = rows_ref[group * 128 : (group + 1) * 128]
        flat = lax.dot_general(
            ones, rows, (((1,), (1,)), ((), ())), precision=lax.Precision.HIGHEST, preferred_element_type=F32
        )
        flat_ref[group : group + 1] = flat[:1]


def level_solve_tables(sine, levels, is_first, is_last):
    root = recurrence_root(sine)
    top = jnp.where(is_last, root / (1.0 + root), 0.0)
    square = root * root
    kappa = jnp.zeros_like(root)
    for _ in range(levels):
        kappa = square * (1.0 + kappa)
    decay = power(root, levels)
    inverse = 1.0 / root
    bottom = jnp.where(is_first, 1.0 - inverse, 1.0)
    inv = 1.0 / (1.0 + bottom * (kappa - top * decay * decay))
    return (root, inv, bottom * inv, inv * inverse, top)


CHUNKS = 8


def chunk_copies(source, target, sems):
    rows = source.shape[0] // CHUNKS
    parts = [pl.ds(i * rows, rows) for i in range(CHUNKS)]
    return [pltpu.make_async_copy(source.at[p], target.at[p], sems.at[i]) for i, p in enumerate(parts)]


def gather_kernel(
    levels, ids_ref, ends_ref, w_hbm, sin_x_ref, sin_y_ref, out_ref, o0, o1, o2, o3, o4, rows_ref, w_ref, tables, sems,
    w_sems,
):
    w_parts = chunk_copies(w_hbm, w_ref, w_sems)
    for copy in w_parts:
        copy.start()

    def fill(i, _):
        rows = pl.ds(pl.multiple_of(i * 8, 8), 8)
        sine = sin_y_ref[rows, :1] + sin_x_ref[...]
        for k, value in enumerate(level_solve_tables(sine, levels, ends_ref[0] == 1, ends_ref[1] == 1)):
            tables[k, rows] = value
        return 0

    lax.fori_loop(0, sin_y_ref.shape[0] // 8, fill, 0)
    leaving = [pltpu.make_async_copy(tables.at[k], o, sems.at[k]) for k, o in enumerate((o0, o1, o2, o3, o4))]
    for copy in w_parts:
        copy.wait()
    for copy in leaving:
        copy.start()
    pick_cells(ids_ref, w_ref, rows_ref, out_ref)
    for copy in leaving:
        copy.wait()


def gather_temp_kernel(ids_ref, temp_ref, out_ref, rows_ref):
    pick_cells(ids_ref, temp_ref, rows_ref, out_ref)


def put_cells(ids_ref, new_ref, out):
    sublane = lax.broadcasted_iota(jnp.int32, (8, 128), 0)
    position = sublane * 128 + lax.broadcasted_iota(jnp.int32, (8, 128), 1)

    per_trip = math.gcd(new_ref.shape[0], 32)

    def put(i, _):
        for k in range(per_trip):
            facet = i * per_trip + k
            hit = position == ids_ref[2, facet]
            pltpu.store(out.at[tile_at(ids_ref, facet)], jnp.full((8, 128), new_ref[facet]), mask=hit)
        return 0

    lax.fori_loop(0, new_ref.shape[0] // per_trip, put, 0)


def theta_kernel(ids_ref, new_ref, temp_ref, out_ref, wide):
    rows = temp_ref.shape[0]
    chunk = math.gcd(rows, 64)

    def widen(i, _):
        here = pl.ds(pl.multiple_of(i * chunk, chunk), chunk)
        wide[here] = temp_ref[here].astype(F32)
        return 0

    def narrow(i, _):
        here = pl.ds(pl.multiple_of(i * chunk, chunk), chunk)
        out_ref[here] = wide[here].astype(BF16)
        return 0

    lax.fori_loop(0, rows // chunk, widen, 0)
    put_cells(ids_ref, new_ref, wide)
    lax.fori_loop(0, rows // chunk, narrow, 0)


def by_owner(flat, slots):
    shares = 128 // slots
    return jnp.stack([pltpu.roll(flat, (128 - k * slots) % 128, 1) if k else flat for k in range(shares)])


class Links:
    def __init__(self, sizes, slots, sent, received):
        names = ("px", "py_half", "py_low")
        self.sizes, self.shares = sizes, 128 // slots
        self.count = sizes[0] * sizes[1] * sizes[2]
        self.places = [lax.axis_index(name) for name in names]
        self.me = (self.places[0] * sizes[1] + self.places[1]) * sizes[2] + self.places[2]
        self.mine = (lax.rem(self.me, self.shares), lax.div(self.me, self.shares))
        self.sent, self.received = sent, received

    def each_peer(self, act):
        sizes, places = self.sizes, self.places

        def one(step, _):
            low = lax.rem(places[2] + step, sizes[2])
            rest = lax.div(step, sizes[2])
            middle = lax.rem(places[1] + rest, sizes[1])
            first = lax.rem(places[0] + lax.div(rest, sizes[1]), sizes[0])
            act((first * sizes[1] + middle) * sizes[2] + low, (first, middle, low))
            return 0

        lax.fori_loop(1, self.count, one, 0)

    def copy(self, phase, source, target, peer, device, landing):
        at = lambda ref, index: ref.at[lax.rem(index, self.shares), lax.div(index, self.shares)]
        return pltpu.make_async_remote_copy(
            at(source, peer),
            at(target, landing),
            self.sent.at[phase, peer],
            self.received.at[phase, landing],
            device_id=device,
            device_id_type=pl.DeviceIdType.MESH,
        )

    def greet(self):
        barrier = pltpu.get_barrier_semaphore()
        self.each_peer(
            lambda peer, device: pl.semaphore_signal(
                barrier, inc=1, device_id=device, device_id_type=pl.DeviceIdType.MESH
            )
        )
        return barrier

    def start(self, phase, source, target):
        self.each_peer(lambda peer, device: self.copy(phase, source, target, peer, device, self.me).start())
        target[self.mine] = source[self.mine]

    def finish(self, phase, source, target):
        self.each_peer(lambda peer, device: self.copy(phase, source, target, peer, device, peer).wait())


def from_owners(parts, slots):
    lane = lax.broadcasted_iota(jnp.int32, parts.shape[1:], 1)
    total = None
    for k in range(parts.shape[0]):
        part = jnp.where(lane < slots, parts[k], 0.0)
        part = pltpu.roll(part, k * slots, 1) if k else part
        total = part if total is None else total + part
    return total


def stress_kernel(
    sizes, slots, own_ref, facet_ref, drag_ref, heat_ref, back_ref, w_ref, sample, got, flux, back, sent, received
):
    links = Links(sizes, slots, sent, received)
    barrier = links.greet()
    sample[:, :, 0] = by_owner(own_ref[...], slots)
    pl.semaphore_wait(barrier, links.count - 1)
    links.start(0, sample, got)
    facet, drag, heat = [by_owner(ref[...], slots) for ref in (facet_ref, drag_ref, heat_ref)]
    links.finish(0, sample, got)
    w_cell = got[:, :, 0]
    speeds = jnp.sqrt(w_cell * w_cell + 0.25)
    flux[:, :, 0] = drag * speeds * w_cell
    flux[:, :, 1] = heat * speeds
    flux[:, :, 2] = facet
    links.start(1, flux, back)
    w_ref[...] = w_cell
    links.finish(1, flux, back)
    for k in range(3):
        back_ref[k] = from_owners(back[:, :, k], slots)


def facet_temp_kernel(
    sizes, slots, own_ref, facet_ref, radiation_ref, capacity_ref, heat_ref, w_ref, new_ref, sample, got, sent, received
):
    links = Links(sizes, slots, sent, received)
    barrier = links.greet()
    sample[:, :, 0] = by_owner(own_ref[...], slots)
    pl.semaphore_wait(barrier, links.count - 1)
    links.start(0, sample, got)
    facet, radiation, capacity, heat = [
        by_owner(ref[...], slots) for ref in (facet_ref, radiation_ref, capacity_ref, heat_ref)
    ]
    w_cell = w_ref[...]
    scale = heat * jnp.sqrt(w_cell * w_cell + 0.25)
    links.finish(0, sample, got)
    flux = scale * (facet - got[:, :, 0])
    new_ref[...] = from_owners(facet + (radiation - flux - 0.5 * facet) / capacity, slots)


def facet_sums(ids, returned):
    same = ids[:, None] == ids[None, :]
    return jnp.sum(jnp.where(same, returned.reshape(1, -1), 0.0), axis=1)


def near_walls(w_rows, sin_x, sin_y, ends, ids, places, facet_temp, drag_coef, heat_coef):
    count = ids.shape[0]
    sizes = tuple(lax.axis_size(name) for name in ("px", "py_half", "py_low"))
    slots = count // (sizes[0] * sizes[1] * sizes[2])
    flat = (count // 128, 128)
    rows, width = sin_y.shape[0], sin_x.shape[1]
    own, *tables = pl.pallas_call(
        lambda *refs: gather_kernel(w_rows.shape[0] // rows, *refs),
        out_shape=[jax.ShapeDtypeStruct(flat, F32)] + [jax.ShapeDtypeStruct((rows, width), F32)] * 5,
        in_specs=[SMEM, SMEM, HBM, VMEM, VMEM],
        out_specs=[VMEM] + [HBM] * 5,
        scratch_shapes=[
            pltpu.VMEM((count, 128), F32),
            pltpu.VMEM(w_rows.shape, F32),
            pltpu.VMEM((5, rows, width), F32),
            pltpu.SemaphoreType.DMA((5,)),
            pltpu.SemaphoreType.DMA((CHUNKS,)),
        ],
        compiler_params=PARAMS,
        name="facet_gather",
    )(places, ends, w_rows, sin_x, sin_y)
    by_rows = (128 // slots, flat[0], 128)
    tall = lambda values: pltpu.VMEM((128 // slots, flat[0], values, 128), F32)
    returned, w_cell = pl.pallas_call(
        lambda *refs: stress_kernel(sizes, slots, *refs),
        out_shape=(jax.ShapeDtypeStruct((3, *flat), F32), jax.ShapeDtypeStruct(by_rows, F32)),
        in_specs=[VMEM] * 4,
        out_specs=(VMEM, VMEM),
        scratch_shapes=[tall(1), tall(1), tall(3), tall(3)]
        + [pltpu.SemaphoreType.DMA((2, sizes[0] * sizes[1] * sizes[2]))] * 2,
        compiler_params=pltpu.CompilerParams(collective_id=1, has_side_effects=True),
        name="stress_exchange",
    )(own, facet_temp.reshape(flat), drag_coef.reshape(flat), heat_coef.reshape(flat))
    return (own.reshape(count) - facet_sums(ids, returned[0]), returned, w_cell, tables)


def warm_air(temp_rows, ids, places, returned):
    count = ids.shape[0]
    flat = (count // 128, 128)
    own = pl.pallas_call(
        gather_temp_kernel,
        out_shape=jax.ShapeDtypeStruct(flat, F32),
        in_specs=[SMEM, VMEM],
        out_specs=VMEM,
        scratch_shapes=[pltpu.VMEM((count, 128), F32)],
        compiler_params=PARAMS,
        cost_estimate=pl.CostEstimate(flops=0, bytes_accessed=4 * temp_rows.size, transcendentals=0),
        name="temp_gather",
    )(places, temp_rows)
    heat_flux = returned[1] * (returned[2] - own)
    return (own, own.reshape(count) + facet_sums(ids, heat_flux))


def warm_facets(own, w_cell, facet_temp, net_radiation, heat_capacity, heat_coef):
    flat = own.shape
    sizes = tuple(lax.axis_size(name) for name in ("px", "py_half", "py_low"))
    slots = own.size // (sizes[0] * sizes[1] * sizes[2])
    tall = pltpu.VMEM((128 // slots, flat[0], 1, 128), F32)
    new_temp = pl.pallas_call(
        lambda *refs: facet_temp_kernel(sizes, slots, *refs),
        out_shape=jax.ShapeDtypeStruct(flat, F32),
        in_specs=[VMEM] * 6,
        out_specs=VMEM,
        scratch_shapes=[tall] * 2 + [pltpu.SemaphoreType.DMA((1, sizes[0] * sizes[1] * sizes[2]))] * 2,
        compiler_params=pltpu.CompilerParams(collective_id=2, has_side_effects=True),
        cost_estimate=pl.CostEstimate(flops=0, bytes_accessed=2**24, transcendentals=0),
        name="facet_temp",
    )(own, *[a.reshape(flat) for a in (facet_temp, net_radiation, heat_capacity, heat_coef)], w_cell)
    return new_temp.reshape(facet_temp.shape)


def body(
    horiz_div,
    w_star,
    air_temp,
    roof_level,
    facet_cells,
    facet_temp,
    net_radiation,
    heat_capacity,
    drag_coef,
    heat_coef,
):
    levels, rows, width = w_star.shape
    px_count, blocks = lax.axis_size("px"), lax.axis_size("py_low")
    py_count = 2 * blocks
    group = px_count * blocks
    place_x, place_y, half = lax.axis_index("px"), lax.axis_index(("py_half", "py_low")), lax.axis_index("py_half")
    own_kx = width // group
    y_cells = rows * px_count

    w_rows = w_star.reshape(levels * rows, width)
    temp_rows = air_temp.reshape(levels * rows, width)
    ids = facet_cells[0]
    places = facet_places(ids, width)
    x_parts, sin_x = periodic_tables(width)
    y_parts, sin_y = periodic_tables(y_cells)
    cosines, sin_block = cosine_table(rows)
    x_tables = [t for part in x_parts for t in two_halves(part)]
    y_tables = [t for part in y_parts for t in two_halves(part)]
    to_modes, to_rows = two_halves(cosines), two_halves(np.ascontiguousarray(cosines.T))
    sin_x = jnp.asarray(sin_x, F32)

    is_first, is_last = place_y == 0, place_y == py_count - 1
    w_near, returned, w_cell, (root, inv, start, from_below, top) = near_walls(
        w_rows,
        sin_x[None, :],
        jnp.asarray(np.repeat(sin_block[:, None], 128, axis=1), F32),
        jnp.stack([is_first, is_last]).astype(jnp.int32),
        ids,
        places,
        facet_temp[0],
        drag_coef[0],
        heat_coef[0],
    )

    end = np.where(np.arange(rows) == 0, np.sqrt(1.0 / rows), cosines[:, 0])
    end = jnp.asarray(np.repeat(end[:, None], 128, axis=1), F32)

    vectors, sin_z = level_tables(levels)
    pick = lambda three: jnp.where(is_first, three[0], jnp.where(is_last, three[2], three[1])).astype(F32)
    vectors, sin_z = pick(vectors), pick(sin_z)
    sine_z = sin_z[:, None] + sin_x[None, :]
    size_z = jnp.sqrt(sine_z)
    half_z = 0.5 * size_z
    cosh_z = jnp.sqrt(1.0 + half_z * half_z)
    half_step = cosh_z - half_z
    across = jnp.exp(2.0 * rows * jnp.log(half_step))
    scale = 1.0 / ((1.0 - across * across) * size_z)
    same_end = -half_step * (1.0 + across * across / (half_step * half_step)) * scale
    far_end = -2.0 * across * cosh_z * scale
    turns = np.arange(px_count)
    circulant = jnp.stack(
        [1.0 / (1.0 - 2.0 * same_end + 2.0 * math.cos(2.0 * math.pi * s / px_count) * far_end) for s in turns]
    )
    circulant = lax.optimization_barrier(circulant)
    phase_of = jnp.asarray(np.cos(2.0 * np.pi * turns[:, None] * turns[None, :] / px_count) / px_count, F32)
    offsets = jnp.stack([(place_x - turns) % px_count, (place_x - 1 - turns) % px_count])
    phases = phase_of[offsets]
    weights = jnp.sum(phases[:, :, :, None, None] * circulant[None, None], axis=2)

    mine = place_x * blocks + lax.axis_index("py_low")
    own_sin = lax.dynamic_slice_in_dim(sin_x, mine * own_kx, own_kx)
    join_root = recurrence_root(own_sin[:, None] + jnp.asarray(sin_y, F32)[None, :])

    tile = math.gcd(rows, 32)
    tiles = rows // tile
    flat = lambda i: pl.BlockSpec((tile, width), i)
    fixed = lambda a: pl.BlockSpec(a.shape, lambda i: (0,) * len(a.shape))
    pairs = levels // 2
    late = lambda i: (jnp.maximum(i - pairs, 0), 0)
    down = lambda i: (jnp.maximum(pairs - 1 - i, 0), 0, 0)
    slab = pl.BlockSpec((2, rows, width), down)
    end_late = pl.BlockSpec((tile, 128), late)
    ends_shape = jax.ShapeDtypeStruct((2, levels, width), F32)
    field, edges, ends, w_corr = pl.pallas_call(
        lambda *refs: forward_kernel(levels, tile, *refs),
        out_shape=(
            jax.ShapeDtypeStruct(w_star.shape, F32),
            jax.ShapeDtypeStruct((2, rows, width), F32),
            ends_shape,
            jax.ShapeDtypeStruct(w_rows.shape, F32),
        ),
        grid=(pairs + tiles,),
        in_specs=[SMEM, SMEM, HBM, slab] + [fixed(t) for t in (*x_tables, *to_modes)] + [flat(late)] * 4 + [end_late],
        out_specs=(
            HBM,
            pl.BlockSpec((2, tile, width), lambda i: (0, *late(i))),
            fixed(ends_shape),
            HBM,
        ),
        scratch_shapes=[
            pltpu.VMEM(w_star.shape, F32),
            pltpu.VMEM(w_rows.shape, F32),
            pltpu.VMEM((rows, width), F32),
            pltpu.VMEM((rows, width), F32),
            pltpu.VMEM((levels, 8, width), F32),
            pltpu.VMEM((levels, 8, width), F32),
            pltpu.SemaphoreType.DMA((2,)),
            pltpu.SemaphoreType.DMA((CHUNKS,)),
        ],
        compiler_params=PARAMS,
        name="forward",
    )(places, w_near, w_rows, horiz_div, *x_tables, *to_modes, root, inv, start, top, end)

    all_ends = lax.all_gather(ends, "px")
    packed = jax.ShapeDtypeStruct((group, 2, own_kx, rows), F32)
    working = [pltpu.VMEM((levels, 8, width), F32)] * 2
    edges = pl.pallas_call(
        lambda *refs: edge_kernel(levels, *refs),
        out_shape=packed,
        in_specs=[VMEM] * 11,
        out_specs=VMEM,
        scratch_shapes=working + [pltpu.VMEM((2, rows, width), F32)],
        compiler_params=SMALL,
        name="edges",
    )(edges, all_ends, weights, vectors, root, inv, start, top, end, *to_modes)
    w_cell, edges = lax.optimization_barrier((w_cell, edges))
    places_late, edges = lax.optimization_barrier((places, edges))
    temp_own, temp_near = warm_air(temp_rows, ids, places_late, returned)
    edges = lax.all_to_all(edges, ("px", "py_low"), split_axis=0, concat_axis=0, tiled=True)
    edges, temp_near = lax.optimization_barrier((edges, temp_near))
    half_id = half.astype(jnp.int32).reshape(1)
    modes, alpha = pl.pallas_call(
        lambda *refs: gather_modes_kernel(levels, px_count, *refs),
        out_shape=(
            jax.ShapeDtypeStruct((blocks, 2, own_kx, y_cells), F32),
            jax.ShapeDtypeStruct((own_kx, y_cells), F32),
        ),
        in_specs=[SMEM] + [VMEM] * 8,
        out_specs=(VMEM, VMEM),
        compiler_params=PARAMS,
        name="gather_modes",
    )(half_id, edges, *y_tables, join_root)
    alpha, temp_own = lax.optimization_barrier((alpha, temp_own))
    new_temp = warm_facets(
        temp_own, w_cell, facet_temp[0], net_radiation[0], heat_capacity[0], heat_coef[0]
    )
    alpha = lax.ppermute(alpha, "py_half", [(0, 1), (1, 0)])
    alpha, new_temp = lax.optimization_barrier((alpha, new_temp))
    joined = pl.pallas_call(
        lambda *refs: join_kernel(levels, px_count, *refs),
        out_shape=packed,
        in_specs=[SMEM] + [VMEM] * 9,
        out_specs=VMEM,
        scratch_shapes=[pltpu.VMEM((blocks, 2, own_kx, y_cells), F32)],
        compiler_params=PARAMS,
        name="join",
    )(half_id, modes, alpha, *y_tables, join_root)
    joined, temp_near = lax.optimization_barrier((joined, temp_near))
    theta_new = pl.pallas_call(
        theta_kernel,
        out_shape=jax.ShapeDtypeStruct(temp_rows.shape, BF16),
        in_specs=[SMEM, SMEM, VMEM],
        out_specs=VMEM,
        scratch_shapes=[pltpu.VMEM(temp_rows.shape, F32)],
        compiler_params=PARAMS,
        cost_estimate=pl.CostEstimate(flops=temp_rows.size, bytes_accessed=8 * temp_rows.size, transcendentals=0),
        name="theta",
    )(places, temp_near, temp_rows).reshape(air_temp.shape)
    joined = lax.all_to_all(joined, ("px", "py_low"), split_axis=0, concat_axis=0, tiled=True)
    sides, more = pl.pallas_call(
        lambda *refs: spread_kernel(levels, *refs),
        out_shape=(jax.ShapeDtypeStruct((2, rows, width), F32), ends_shape),
        in_specs=[VMEM] * 8,
        out_specs=(VMEM, VMEM),
        scratch_shapes=working,
        compiler_params=SMALL,
        name="spread",
    )(joined, *to_modes, root, start, from_below, top, end)
    more = lax.all_gather(more, "px")

    early = lambda i: (jnp.minimum(i, tiles - 1), 0)
    up = lambda i: (jnp.maximum(i - tiles, 0), 0, 0)
    slab = pl.BlockSpec((2, rows, width), up)
    w_new = pl.pallas_call(
        lambda *refs: inverse_kernel(levels, tile, *refs),
        out_shape=jax.ShapeDtypeStruct(w_star.shape, F32),
        grid=(tiles + pairs,),
        in_specs=[
            SMEM,
            pl.BlockSpec((levels, tile, width), lambda i: (0, *early(i))),
            pl.BlockSpec((2, tile, width), lambda i: (0, *early(i))),
        ]
        + [fixed(a) for a in (all_ends, more, weights, vectors)]
        + [flat(early)] * 4
        + [pl.BlockSpec((tile, 128), early)]
        + [fixed(t) for t in (*x_tables, *to_rows)]
        + [slab, fixed(roof_level)],
        out_specs=slab,
        scratch_shapes=[pltpu.VMEM(w_star.shape, F32)] + working,
        compiler_params=PARAMS,
        name="inverse",
    )(
        place_y.astype(jnp.int32).reshape(1),
        field,
        sides,
        all_ends,
        more,
        weights,
        vectors,
        root,
        start,
        from_below,
        top,
        end,
        *x_tables,
        *to_rows,
        w_corr.reshape(w_star.shape),
        roof_level,
    )
    return (w_new, theta_new, new_temp[None])


def solution(mesh):
    px_count, py_count = mesh.devices.shape
    split_mesh = jax.sharding.Mesh(
        mesh.devices.reshape(px_count, 2, py_count // 2), ("px", "py_half", "py_low")
    )
    py, every = ("py_half", "py_low"), ("px", "py_half", "py_low")
    placed = (P(py, "px", None),) * 3 + (P("px", None),) + (P(every, None),) * 6
    return jax.shard_map(
        body,
        mesh=split_mesh,
        in_specs=placed,
        out_specs=(P(py, "px", None), P(py, "px", None), P(every, None)),
        check_vma=False,
    )
```

```python
import math

import jax
import jax.numpy as jnp
import ml_dtypes
import numpy as np
from jax import lax
from jax.experimental import pallas as pl
from jax.experimental.pallas import tpu as pltpu
from jax.sharding import PartitionSpec as P

F32 = jnp.float32
BF16 = jnp.bfloat16
HBM = pl.BlockSpec(memory_space=pl.ANY)
VMEM = pl.BlockSpec(memory_space=pltpu.VMEM)
SMEM = pl.BlockSpec(memory_space=pltpu.SMEM)
PARAMS = pltpu.CompilerParams(vmem_limit_bytes=58 * 2**20)
SMALL = pltpu.CompilerParams(vmem_limit_bytes=28 * 2**20)


def two_halves(table):
    high = table.astype(ml_dtypes.bfloat16)
    low = (table - high.astype(np.float64)).astype(ml_dtypes.bfloat16)
    return (jnp.asarray(high), jnp.asarray(low))


def periodic_tables(size):
    half, quarter = size // 2, size // 4
    groups = (
        (np.arange(0, half + 1, 4), np.arange(4, half, 4), quarter),
        (np.arange(2, half, 4), np.arange(2, half, 4), quarter),
        (np.arange(1, half, 2), np.arange(1, half, 2), half),
    )
    tables, waves = [], []
    for cosines, sines, rows in groups:
        x = np.arange(rows)[:, None]
        norms = np.where((cosines == 0) | (cosines == half), np.sqrt(1.0 / size), np.sqrt(2.0 / size))
        tables.append(
            np.concatenate(
                [
                    norms * np.cos(2.0 * np.pi / size * (x * cosines % size)),
                    np.sqrt(2.0 / size) * np.sin(2.0 * np.pi / size * (x * sines % size)),
                ],
                axis=1,
            )
        )
        waves += [cosines, sines]
    waves = np.concatenate(waves)
    return (tables, 4.0 * np.sin(np.pi * waves / size) ** 2)


def cosine_table(size):
    modes = np.arange(size)[:, None]
    table = np.sqrt(2.0 / size) * np.cos(np.pi * modes * (2 * np.arange(size)[None, :] + 1) / (2 * size))
    table[0] = np.sqrt(1.0 / size)
    return (table, 4.0 * np.sin(np.pi * modes[:, 0] / (2 * size)) ** 2)


def level_tables(size):
    modes, levels = np.arange(size)[None, :], np.arange(size)[:, None]
    omegas = (
        np.pi * (2 * modes + 1) / (2 * size + 1),
        np.pi * (modes + 1) / (size + 1),
        np.pi * (modes + 1) / (size + 0.5),
    )
    vectors = (
        np.cos(omegas[0] * (levels + 0.5)),
        np.sin(omegas[1] * (levels + 1)),
        np.sin(omegas[2] * (levels + 1)),
    )
    vectors = [v / np.sqrt(np.sum(v * v, axis=0, keepdims=True)) for v in vectors]
    return (vectors, [4.0 * np.sin(o[0] / 2) ** 2 for o in omegas])


def split(value):
    high = value.astype(BF16)
    return (high, (value - high.astype(F32)).astype(BF16))


def dot3(left, right, dims=((1,), (0,))):
    one = lambda a, b: lax.dot_general(a, b, (dims, ((), ())), preferred_element_type=F32)
    free = 1 - dims[0][0]
    size = left[0].shape[free]
    both = one(jnp.concatenate(left, axis=free), right[0])
    return both[:size] + (both[size:] + one(left[0], right[1]))


def read_pair(refs):
    return (refs[0][...], refs[1][...])


def periodic_forward(value, tables):
    half, quarter = value.shape[1] // 2, value.shape[1] // 4
    even, odd = value[:, :half] + value[:, half:], value[:, :half] - value[:, half:]
    parts = (even[:, :quarter] + even[:, quarter:], even[:, :quarter] - even[:, quarter:], odd)
    return jnp.concatenate([dot3(split(p), read_pair(t)) for p, t in zip(parts, tables)], axis=1)


def periodic_inverse(value, tables):
    half, quarter = value.shape[1] // 2, value.shape[1] // 4
    parts = (value[:, :quarter], value[:, quarter:half], value[:, half:])
    four, two, odd = [dot3(split(p), read_pair(t), ((1,), (1,))) for p, t in zip(parts, tables)]
    even = jnp.concatenate([four + two, four - two], axis=1)
    return jnp.concatenate([even + odd, even - odd], axis=1)


def power(base, exponent):
    result = None
    while exponent:
        if exponent & 1:
            result = base if result is None else result * base
        base = base * base
        exponent >>= 1
    return result


def recurrence_root(sine):
    half = 0.5 * jnp.sqrt(sine)
    root = jnp.sqrt(1.0 + half * half) - half
    return root * root


def first_sweeps(load, root, top, above, store, levels):
    value = None
    for level in range(levels):
        value = load(level) if value is None else load(level) + root * value
        store[level] = value
    last = value
    value = top * value if above is None else top * value + above
    for level in range(levels - 1, -1, -1):
        value = root * (value - store[level])
    return (value, last)


def second_sweeps(load, start, root, top, above, store, levels, emit):
    value = start
    for level in range(levels):
        value = root * value if load is None else load(level) + root * value
        store[level] = value
    value = top * value if above is None else top * value + above
    for level in range(levels - 1, -1, -1):
        value = root * (value - store[level])
        emit(level, value)


def block_fluxes(ends, weights_ref, vectors_ref, levels, out_ref):
    blocks = len(ends)
    one = lambda dims, b: lax.dot_general(
        vectors_ref[...], b, (dims, ((), ())), precision=lax.Precision.HIGHEST, preferred_element_type=F32
    )
    upper = lower = None
    for block in range(blocks):
        even_next, odd_next = ends[(block + 1) % blocks]
        even, odd = ends[block]
        jump = one(((0,), (0,)), (even_next + odd_next) - (even - odd))
        up, low = weights_ref[0, block] * jump, weights_ref[1, block] * jump
        upper = up if upper is None else upper + up
        lower = low if lower is None else lower + low
    upper, lower = one(((1,), (0,)), upper), one(((1,), (0,)), lower)
    width = upper.shape[1]
    is_even = lax.broadcasted_iota(jnp.int32, (8, width), 0) % 2 == 0
    for level in range(levels):
        up, low = upper[level : level + 1], lower[level : level + 1]
        out_ref[level] = jnp.where(is_even, up - low, -up - low)


def fold_ends(total, out_ref, levels):
    is_even = lax.broadcasted_iota(jnp.int32, total.shape[1:], 0) % 2 == 0
    for level in range(levels):
        value = total[level]
        out_ref[0, level : level + 1] = jnp.sum(jnp.where(is_even, value, 0.0), axis=0, keepdims=True)
        out_ref[1, level : level + 1] = jnp.sum(jnp.where(is_even, 0.0, value), axis=0, keepdims=True)


def forward_kernel(
    levels, tile, ids_ref, w_new_ref, w_hbm, div_ref, t0h, t0l, t1h, t1l, t2h, t2l, ch, cl, root_ref, inv_ref,
    start_ref, top_ref, end_ref, field_hbm, edge_ref, ends_ref, corr_hbm, field, w_rows, above, lowest, store, total,
    sems, w_sems,
):
    step = pl.program_id(0)
    tables = ((t0h, t0l), (t1h, t1l), (t2h, t2l))

    pairs = levels // 2

    @pl.when(step == 0)
    def _():
        loads = chunk_copies(w_hbm, w_rows, w_sems)
        for load in loads:
            load.start()
        above[...] = jnp.zeros_like(above)
        total[...] = jnp.zeros_like(total)
        for load in loads:
            load.wait()
        put_cells(ids_ref, w_new_ref, w_rows)
        pltpu.make_async_copy(w_rows, corr_hbm, sems.at[1]).start()

    row_count = above.shape[0]

    @pl.when(step < pairs)
    def _():
        low = pl.multiple_of((pairs - 1 - step) * 2 * row_count, 2 * row_count)
        value = w_rows[pl.ds(low, 2 * row_count)]
        lower, upper = value[:row_count], value[row_count:]
        source = jnp.concatenate([div_ref[0] + (upper - lower), div_ref[1] + (above[...] - upper)], axis=0)
        modes = periodic_forward(source, tables)
        for k in range(2):
            part = modes[k * row_count : (k + 1) * row_count]
            field[(pairs - 1 - step) * 2 + k] = dot3(read_pair((ch, cl)), split(part))
        above[...] = lower

    @pl.when(step == pairs - 1)
    def _():
        pltpu.make_async_copy(field, field_hbm, sems.at[0]).start()
        lowest[...] = dot3(read_pair((ch, cl)), split(periodic_forward(w_rows[:row_count], tables)))

    @pl.when(step >= pairs)
    def _():
        def rows_of(sub, _):
            here = pl.multiple_of(sub * 8, 8)
            rows = pl.ds(here, 8)
            full = pl.ds(pl.multiple_of((step - pairs) * tile + here, 8), 8)
            root, top = root_ref[rows], top_ref[rows]
            load = lambda level: field[level, full]
            first, _ = first_sweeps(load, root, top, None, store, levels)
            edge_ref[0, rows] = first * inv_ref[rows] - lowest[full]
            weight = end_ref[rows, :1]

            def emit(level, value):
                total[level] += weight * value
                if level == levels - 1:
                    edge_ref[1, rows] = value

            second_sweeps(load, first * start_ref[rows], root, top, None, store, levels, emit)
            return 0

        lax.fori_loop(0, tile // 8, rows_of, 0)

    @pl.when(step == pl.num_programs(0) - 1)
    def _():
        fold_ends(total, ends_ref, levels)
        pltpu.make_async_copy(w_rows, corr_hbm, sems.at[1]).wait()
        pltpu.make_async_copy(field, field_hbm, sems.at[0]).wait()


def edge_kernel(
    levels, edge_ref, ends_ref, weights_ref, vectors_ref, root_ref, inv_ref, start_ref, top_ref, end_ref, ch, cl,
    out_ref, pattern, store, fixed,
):
    block_fluxes(
        [(ends_ref[b, 0], ends_ref[b, 1]) for b in range(ends_ref.shape[0])], weights_ref, vectors_ref, levels, pattern
    )

    def rows_of(sub, _):
        rows = pl.ds(pl.multiple_of(sub * 8, 8), 8)
        root, top = root_ref[rows], top_ref[rows]
        first, last = first_sweeps(lambda level: pattern[level], root, top, None, store, levels)
        weight = end_ref[rows, :1]
        fixed[0, rows] = edge_ref[0, rows] - weight * (first * inv_ref[rows])
        last = last + power(root, levels) * (first * start_ref[rows])
        fixed[1, rows] = edge_ref[1, rows] - weight * (root * (top - 1.0) * last)
        return 0

    lax.fori_loop(0, edge_ref.shape[1] // 8, rows_of, 0)
    for side in range(2):
        value = dot3(split(fixed[side].T), read_pair((ch, cl)))
        out_ref[:, side] = value.reshape(out_ref.shape[0], out_ref.shape[2], out_ref.shape[3])


def join_start(levels, near_top, root):
    square = root * root
    sums = jnp.ones_like(root)
    for _ in range(1, levels):
        sums = 1.0 + square * sums
    whole = power(root, 2 * levels)
    one = 1.0 / (sums + whole)
    near = -root * sums * one
    far = -power(root, levels) * one
    part = power(root, 2 * levels - 1)
    bottom = -root * (1.0 + part) / (1.0 + whole * root)
    pairs = (1.0 + root) * sums
    top = -root * (pairs - part) / (pairs + whole)
    return (near, far, jnp.where(near_top, top, bottom), jnp.where(near_top, bottom, top))


def join_chain(load, blocks, near, far, beta):
    alpha = load(0, 1)
    alphas, betas, heads, slopes = [alpha], [beta], [None], [None]
    for block in range(1, blocks):
        scale = 1.0 / (1.0 - near * beta)
        head = (load(block, 0) - near * alpha) * scale
        slope = far * scale
        alpha = load(block, 1) - far * alpha + far * beta * head
        beta = near + far * beta * slope
        alphas.append(alpha)
        betas.append(beta)
        heads.append(head)
        slopes.append(slope)
    return (alphas, betas, heads, slopes)


def chain_place(block, blocks, half):
    return block + half * (blocks - 1 - 2 * block)


def gather_modes_kernel(levels, px_count, half_ref, edge_ref, t0h, t0l, t1h, t1l, t2h, t2l, root_ref, out_ref, alpha_ref):
    blocks, _, rows, _ = out_ref.shape
    half = half_ref[0]
    for block in range(blocks):
        for side in range(2):
            whole = jnp.concatenate([edge_ref[i * blocks + block, side] for i in range(px_count)], axis=1)
            out_ref[block, side] = whole
    flat = out_ref[...].reshape(blocks * 2 * rows, out_ref.shape[3])
    out_ref[...] = periodic_forward(flat, ((t0h, t0l), (t1h, t1l), (t2h, t2l))).reshape(out_ref.shape)

    def rows_of(sub, _):
        here = pl.ds(pl.multiple_of(sub * 8, 8), 8)
        near, far, own, _ = join_start(levels, half == 1, root_ref[here])
        load = lambda block, outer: out_ref[chain_place(block, blocks, half), jnp.abs(outer - half), here]
        alpha_ref[here] = join_chain(load, blocks, near, far, own)[0][-1]
        return 0

    lax.fori_loop(0, rows // 8, rows_of, 0)


def join_kernel(
    levels, px_count, half_ref, modes_ref, alpha_ref, t0h, t0l, t1h, t1l, t2h, t2l, root_ref, out_ref, modes
):
    blocks, _, rows, _ = modes_ref.shape
    half = half_ref[0]
    width = out_ref.shape[3]

    def rows_of(sub, _):
        here = pl.ds(pl.multiple_of(sub * 8, 8), 8)
        near, far, own, other = join_start(levels, half == 1, root_ref[here])
        load = lambda block, outer: modes_ref[chain_place(block, blocks, half), jnp.abs(outer - half), here]
        alphas, betas, heads, slopes = join_chain(load, blocks, near, far, own)
        for _ in range(1, blocks):
            other = near + far * other * (far / (1.0 - near * other))
        met = alpha_ref[here]
        outer = (met - other * alphas[-1]) / (1.0 - other * betas[-1])
        for block in range(blocks - 1, -1, -1):
            place = chain_place(block, blocks, half)
            modes[place, 1 - half, here] = outer
            if block:
                outer = heads[block] - slopes[block] * outer
                modes[place, half, here] = alphas[block - 1] - betas[block - 1] * outer
            else:
                modes[place, half, here] = jnp.zeros_like(outer)
        return 0

    lax.fori_loop(0, rows // 8, rows_of, 0)
    flat = modes[...].reshape(blocks * 2 * rows, modes.shape[3])
    whole = periodic_inverse(flat, ((t0h, t0l), (t1h, t1l), (t2h, t2l))).reshape(modes.shape)
    for block in range(blocks):
        for side in range(2):
            for i in range(px_count):
                out_ref[i * blocks + block, side] = whole[block, side, :, i * width : (i + 1) * width]


def spread_kernel(levels, joined_ref, ch, cl, root_ref, start_ref, below_ref, top_ref, end_ref, out_ref, ends_ref, store, total):
    kx_width = joined_ref.shape[0] * joined_ref.shape[2]
    for side in range(2):
        value = joined_ref[:, side].reshape(kx_width, joined_ref.shape[3])
        out_ref[side] = dot3(read_pair((ch, cl)), split(value), ((1,), (1,)))
    total[...] = jnp.zeros_like(total)

    def rows_of(sub, _):
        rows = pl.ds(pl.multiple_of(sub * 8, 8), 8)
        root, top = root_ref[rows], top_ref[rows]
        below, above = out_ref[0, rows], out_ref[1, rows]
        start = start_ref[rows] * (power(root, levels) * above) - below_ref[rows] * below
        weight = end_ref[rows, :1]

        def emit(level, value):
            total[level] += weight * value

        second_sweeps(None, start, root, top, above, store, levels, emit)
        return 0

    lax.fori_loop(0, out_ref.shape[1] // 8, rows_of, 0)
    fold_ends(total, ends_ref, levels)


def inverse_kernel(
    levels, tile, place_ref, field_ref, sides_ref, ends_ref, more_ref, weights_ref, vectors_ref, root_ref, start_ref,
    below_ref, top_ref, end_ref, t0h, t0l, t1h, t1l, t2h, t2l, ch, cl, w_ref, roof_ref, out_ref, field, pattern, store,
):
    step = pl.program_id(0)
    tiles = pl.num_programs(0) - levels // 2
    tables = ((t0h, t0l), (t1h, t1l), (t2h, t2l))

    @pl.when(step == 0)
    def _():
        ends = [
            (ends_ref[b, 0] + more_ref[b, 0], ends_ref[b, 1] + more_ref[b, 1]) for b in range(ends_ref.shape[0])
        ]
        block_fluxes(ends, weights_ref, vectors_ref, levels, pattern)

    @pl.when(step < tiles)
    def _():
        def rows_of(sub, _):
            here = pl.multiple_of(sub * 8, 8)
            rows = pl.ds(here, 8)
            full = pl.ds(pl.multiple_of(step * tile + here, 8), 8)
            root, top = root_ref[rows], top_ref[rows]
            below, above = sides_ref[0, rows], sides_ref[1, rows]
            weight = end_ref[rows, :1]
            load = lambda level: field_ref[level, rows] - weight * pattern[level]
            first, _ = first_sweeps(load, root, top, above, store, levels)
            start = start_ref[rows] * first - below_ref[rows] * below
            held = []

            def emit(level, value):
                if held:
                    field[level + 1, full] = held.pop() - value
                held.append(value)

            second_sweeps(load, start, root, top, above, store, levels, emit)
            field[0, full] = jnp.where(place_ref[0] == 0, 0.0, held[0] - below)
            return 0

        lax.fori_loop(0, tile // 8, rows_of, 0)

    @pl.when(step >= tiles)
    def _():
        level = (step - tiles) * 2
        rows_y = [dot3(read_pair((ch, cl)), split(field[level + k])) for k in range(2)]
        slope = periodic_inverse(jnp.concatenate(rows_y, axis=0), tables)
        count = roof_ref.shape[0]
        for k in range(2):
            solid = place_ref[0] * levels + level + k < roof_ref[...]
            out_ref[k] = jnp.where(solid, 0.0, w_ref[k] - slope[k * count : (k + 1) * count])


def facet_places(ids, width):
    safe = jnp.maximum(ids, 0)
    row, column = safe // width, safe % width
    return jnp.stack([row // 8, column // 128, jnp.where(ids < 0, -1, row % 8 * 128 + column % 128)])


def tile_at(places_ref, facet):
    return (
        pl.ds(pl.multiple_of(places_ref[0, facet] * 8, 8), 8),
        pl.ds(pl.multiple_of(places_ref[1, facet] * 128, 128), 128),
    )


def pair_at(places_ref, facet):
    return (
        pl.ds(pl.multiple_of(lax.shift_right_logical(places_ref[0, facet], 1) * 16, 16), 16),
        pl.ds(pl.multiple_of(places_ref[1, facet] * 128, 128), 128),
    )


def pick_cells(ids_ref, ref, rows_ref, flat_ref):
    sublane = lax.broadcasted_iota(jnp.int32, (8, 128), 0)
    position = sublane * 128 + lax.broadcasted_iota(jnp.int32, (8, 128), 1)

    def pick(i, _):
        rows = None
        for lane in range(8):
            facet = i * 8 + lane
            mark = ids_ref[2, facet]
            if ref.dtype == F32:
                tile = ref[tile_at(ids_ref, facet)]
            else:
                both = ref[pair_at(ids_ref, facet)].astype(F32)
                tile = jnp.where(ids_ref[0, facet] & 1 == 0, both[:8], both[8:])
            tile = jnp.where(position == mark, tile, 0.0)
            tile = pltpu.roll(tile, (lane - lax.shift_right_arithmetic(mark, 7)) & 7, 0)
            rows = tile if rows is None else jnp.where(sublane == lane, tile, rows)
        rows_ref[pl.ds(pl.multiple_of(i * 8, 8), 8)] = rows

    group_count = rows_ref.shape[0] // 8
    per_trip = math.gcd(group_count, 8)

    def trip(i, _):
        for k in range(per_trip):
            pick(i * per_trip + k, None)
        return 0

    lax.fori_loop(0, group_count // per_trip, trip, 0)
    ones = jnp.ones((8, 128), F32)
    for group in range(flat_ref.shape[0]):
        rows = rows_ref[group * 128 : (group + 1) * 128]
        flat = lax.dot_general(
            ones, rows, (((1,), (1,)), ((), ())), precision=lax.Precision.HIGHEST, preferred_element_type=F32
        )
        flat_ref[group : group + 1] = flat[:1]


def level_solve_tables(sine, levels, is_first, is_last):
    root = recurrence_root(sine)
    top = jnp.where(is_last, root / (1.0 + root), 0.0)
    square = root * root
    kappa = jnp.zeros_like(root)
    for _ in range(levels):
        kappa = square * (1.0 + kappa)
    decay = power(root, levels)
    inverse = 1.0 / root
    bottom = jnp.where(is_first, 1.0 - inverse, 1.0)
    inv = 1.0 / (1.0 + bottom * (kappa - top * decay * decay))
    return (root, inv, bottom * inv, inv * inverse, top)


CHUNKS = 8


def chunk_copies(source, target, sems):
    rows = source.shape[0] // CHUNKS
    parts = [pl.ds(i * rows, rows) for i in range(CHUNKS)]
    return [pltpu.make_async_copy(source.at[p], target.at[p], sems.at[i]) for i, p in enumerate(parts)]


def gather_kernel(
    levels, ids_ref, ends_ref, w_hbm, sin_x_ref, sin_y_ref, out_ref, o0, o1, o2, o3, o4, rows_ref, w_ref, tables, sems,
    w_sems,
):
    w_parts = chunk_copies(w_hbm, w_ref, w_sems)
    for copy in w_parts:
        copy.start()

    def fill(i, _):
        rows = pl.ds(pl.multiple_of(i * 8, 8), 8)
        sine = sin_y_ref[rows, :1] + sin_x_ref[...]
        for k, value in enumerate(level_solve_tables(sine, levels, ends_ref[0] == 1, ends_ref[1] == 1)):
            tables[k, rows] = value
        return 0

    lax.fori_loop(0, sin_y_ref.shape[0] // 8, fill, 0)
    leaving = [pltpu.make_async_copy(tables.at[k], o, sems.at[k]) for k, o in enumerate((o0, o1, o2, o3, o4))]
    for copy in w_parts:
        copy.wait()
    for copy in leaving:
        copy.start()
    pick_cells(ids_ref, w_ref, rows_ref, out_ref)
    for copy in leaving:
        copy.wait()


def gather_temp_kernel(ids_ref, temp_ref, out_ref, rows_ref):
    pick_cells(ids_ref, temp_ref, rows_ref, out_ref)


def put_cells(ids_ref, new_ref, out):
    sublane = lax.broadcasted_iota(jnp.int32, (8, 128), 0)
    position = sublane * 128 + lax.broadcasted_iota(jnp.int32, (8, 128), 1)

    per_trip = math.gcd(new_ref.shape[0], 32)

    def put(i, _):
        for k in range(per_trip):
            facet = i * per_trip + k
            hit = position == ids_ref[2, facet]
            pltpu.store(out.at[tile_at(ids_ref, facet)], jnp.full((8, 128), new_ref[facet]), mask=hit)
        return 0

    lax.fori_loop(0, new_ref.shape[0] // per_trip, put, 0)


def theta_kernel(ids_ref, new_ref, temp_ref, out_ref, wide):
    rows = temp_ref.shape[0]
    chunk = math.gcd(rows, 64)

    def widen(i, _):
        here = pl.ds(pl.multiple_of(i * chunk, chunk), chunk)
        wide[here] = temp_ref[here].astype(F32)
        return 0

    def narrow(i, _):
        here = pl.ds(pl.multiple_of(i * chunk, chunk), chunk)
        out_ref[here] = wide[here].astype(BF16)
        return 0

    lax.fori_loop(0, rows // chunk, widen, 0)
    put_cells(ids_ref, new_ref, wide)
    lax.fori_loop(0, rows // chunk, narrow, 0)


def by_owner(flat, slots):
    shares = 128 // slots
    return jnp.stack([pltpu.roll(flat, (128 - k * slots) % 128, 1) if k else flat for k in range(shares)])


class Links:
    def __init__(self, sizes, slots, sent, received):
        names = ("px", "py_half", "py_low")
        self.sizes, self.shares = sizes, 128 // slots
        self.count = sizes[0] * sizes[1] * sizes[2]
        self.places = [lax.axis_index(name) for name in names]
        self.me = (self.places[0] * sizes[1] + self.places[1]) * sizes[2] + self.places[2]
        self.mine = (lax.rem(self.me, self.shares), lax.div(self.me, self.shares))
        self.sent, self.received = sent, received

    def each_peer(self, act):
        sizes, places = self.sizes, self.places

        def one(step, _):
            low = lax.rem(places[2] + step, sizes[2])
            rest = lax.div(step, sizes[2])
            middle = lax.rem(places[1] + rest, sizes[1])
            first = lax.rem(places[0] + lax.div(rest, sizes[1]), sizes[0])
            act((first * sizes[1] + middle) * sizes[2] + low, (first, middle, low))
            return 0

        lax.fori_loop(1, self.count, one, 0)

    def copy(self, phase, source, target, peer, device, landing):
        at = lambda ref, index: ref.at[lax.rem(index, self.shares), lax.div(index, self.shares)]
        return pltpu.make_async_remote_copy(
            at(source, peer),
            at(target, landing),
            self.sent.at[phase, peer],
            self.received.at[phase, landing],
            device_id=device,
            device_id_type=pl.DeviceIdType.MESH,
        )

    def greet(self):
        barrier = pltpu.get_barrier_semaphore()
        self.each_peer(
            lambda peer, device: pl.semaphore_signal(
                barrier, inc=1, device_id=device, device_id_type=pl.DeviceIdType.MESH
            )
        )
        return barrier

    def start(self, phase, source, target):
        self.each_peer(lambda peer, device: self.copy(phase, source, target, peer, device, self.me).start())
        target[self.mine] = source[self.mine]

    def finish(self, phase, source, target):
        self.each_peer(lambda peer, device: self.copy(phase, source, target, peer, device, peer).wait())


def from_owners(parts, slots):
    lane = lax.broadcasted_iota(jnp.int32, parts.shape[1:], 1)
    total = None
    for k in range(parts.shape[0]):
        part = jnp.where(lane < slots, parts[k], 0.0)
        part = pltpu.roll(part, k * slots, 1) if k else part
        total = part if total is None else total + part
    return total


def stress_kernel(
    sizes, slots, own_ref, facet_ref, drag_ref, heat_ref, back_ref, w_ref, sample, got, flux, back, sent, received
):
    links = Links(sizes, slots, sent, received)
    barrier = links.greet()
    sample[:, :, 0] = by_owner(own_ref[...], slots)
    pl.semaphore_wait(barrier, links.count - 1)
    links.start(0, sample, got)
    facet, drag, heat = [by_owner(ref[...], slots) for ref in (facet_ref, drag_ref, heat_ref)]
    links.finish(0, sample, got)
    w_cell = got[:, :, 0]
    speeds = jnp.sqrt(w_cell * w_cell + 0.25)
    flux[:, :, 0] = drag * speeds * w_cell
    flux[:, :, 1] = heat * speeds
    flux[:, :, 2] = facet
    links.start(1, flux, back)
    w_ref[...] = w_cell
    links.finish(1, flux, back)
    for k in range(3):
        back_ref[k] = from_owners(back[:, :, k], slots)


def facet_temp_kernel(
    sizes, slots, own_ref, facet_ref, radiation_ref, capacity_ref, heat_ref, w_ref, new_ref, sample, got, sent, received
):
    links = Links(sizes, slots, sent, received)
    barrier = links.greet()
    sample[:, :, 0] = by_owner(own_ref[...], slots)
    pl.semaphore_wait(barrier, links.count - 1)
    links.start(0, sample, got)
    facet, radiation, capacity, heat = [
        by_owner(ref[...], slots) for ref in (facet_ref, radiation_ref, capacity_ref, heat_ref)
    ]
    w_cell = w_ref[...]
    scale = heat * jnp.sqrt(w_cell * w_cell + 0.25)
    links.finish(0, sample, got)
    flux = scale * (facet - got[:, :, 0])
    new_ref[...] = from_owners(facet + (radiation - flux - 0.5 * facet) / capacity, slots)


def facet_sums(ids, returned):
    same = ids[:, None] == ids[None, :]
    return jnp.sum(jnp.where(same, returned.reshape(1, -1), 0.0), axis=1)


def near_walls(w_rows, sin_x, sin_y, ends, ids, places, facet_temp, drag_coef, heat_coef):
    count = ids.shape[0]
    sizes = tuple(lax.axis_size(name) for name in ("px", "py_half", "py_low"))
    slots = count // (sizes[0] * sizes[1] * sizes[2])
    flat = (count // 128, 128)
    rows, width = sin_y.shape[0], sin_x.shape[1]
    own, *tables = pl.pallas_call(
        lambda *refs: gather_kernel(w_rows.shape[0] // rows, *refs),
        out_shape=[jax.ShapeDtypeStruct(flat, F32)] + [jax.ShapeDtypeStruct((rows, width), F32)] * 5,
        in_specs=[SMEM, SMEM, HBM, VMEM, VMEM],
        out_specs=[VMEM] + [HBM] * 5,
        scratch_shapes=[
            pltpu.VMEM((count, 128), F32),
            pltpu.VMEM(w_rows.shape, F32),
            pltpu.VMEM((5, rows, width), F32),
            pltpu.SemaphoreType.DMA((5,)),
            pltpu.SemaphoreType.DMA((CHUNKS,)),
        ],
        compiler_params=PARAMS,
        name="facet_gather",
    )(places, ends, w_rows, sin_x, sin_y)
    by_rows = (128 // slots, flat[0], 128)
    tall = lambda values: pltpu.VMEM((128 // slots, flat[0], values, 128), F32)
    returned, w_cell = pl.pallas_call(
        lambda *refs: stress_kernel(sizes, slots, *refs),
        out_shape=(jax.ShapeDtypeStruct((3, *flat), F32), jax.ShapeDtypeStruct(by_rows, F32)),
        in_specs=[VMEM] * 4,
        out_specs=(VMEM, VMEM),
        scratch_shapes=[tall(1), tall(1), tall(3), tall(3)]
        + [pltpu.SemaphoreType.DMA((2, sizes[0] * sizes[1] * sizes[2]))] * 2,
        compiler_params=pltpu.CompilerParams(collective_id=1, has_side_effects=True),
        name="stress_exchange",
    )(own, facet_temp.reshape(flat), drag_coef.reshape(flat), heat_coef.reshape(flat))
    return (own.reshape(count) - facet_sums(ids, returned[0]), returned, w_cell, tables)


def warm_air(temp_rows, ids, places, returned):
    count = ids.shape[0]
    flat = (count // 128, 128)
    own = pl.pallas_call(
        gather_temp_kernel,
        out_shape=jax.ShapeDtypeStruct(flat, F32),
        in_specs=[SMEM, VMEM],
        out_specs=VMEM,
        scratch_shapes=[pltpu.VMEM((count, 128), F32)],
        compiler_params=PARAMS,
        cost_estimate=pl.CostEstimate(flops=0, bytes_accessed=4 * temp_rows.size, transcendentals=0),
        name="temp_gather",
    )(places, temp_rows)
    heat_flux = returned[1] * (returned[2] - own)
    return (own, own.reshape(count) + facet_sums(ids, heat_flux))


def warm_facets(own, w_cell, facet_temp, net_radiation, heat_capacity, heat_coef):
    flat = own.shape
    sizes = tuple(lax.axis_size(name) for name in ("px", "py_half", "py_low"))
    slots = own.size // (sizes[0] * sizes[1] * sizes[2])
    tall = pltpu.VMEM((128 // slots, flat[0], 1, 128), F32)
    new_temp = pl.pallas_call(
        lambda *refs: facet_temp_kernel(sizes, slots, *refs),
        out_shape=jax.ShapeDtypeStruct(flat, F32),
        in_specs=[VMEM] * 6,
        out_specs=VMEM,
        scratch_shapes=[tall] * 2 + [pltpu.SemaphoreType.DMA((1, sizes[0] * sizes[1] * sizes[2]))] * 2,
        compiler_params=pltpu.CompilerParams(collective_id=2, has_side_effects=True),
        cost_estimate=pl.CostEstimate(flops=0, bytes_accessed=2**24, transcendentals=0),
        name="facet_temp",
    )(own, *[a.reshape(flat) for a in (facet_temp, net_radiation, heat_capacity, heat_coef)], w_cell)
    return new_temp.reshape(facet_temp.shape)


def body(
    horiz_div,
    w_star,
    air_temp,
    roof_level,
    facet_cells,
    facet_temp,
    net_radiation,
    heat_capacity,
    drag_coef,
    heat_coef,
):
    levels, rows, width = w_star.shape
    px_count, blocks = lax.axis_size("px"), lax.axis_size("py_low")
    py_count = 2 * blocks
    group = px_count * blocks
    place_x, place_y, half = lax.axis_index("px"), lax.axis_index(("py_half", "py_low")), lax.axis_index("py_half")
    own_kx = width // group
    y_cells = rows * px_count

    w_rows = w_star.reshape(levels * rows, width)
    temp_rows = air_temp.reshape(levels * rows, width)
    ids = facet_cells[0]
    places = facet_places(ids, width)
    x_parts, sin_x = periodic_tables(width)
    y_parts, sin_y = periodic_tables(y_cells)
    cosines, sin_block = cosine_table(rows)
    x_tables = [t for part in x_parts for t in two_halves(part)]
    y_tables = [t for part in y_parts for t in two_halves(part)]
    to_modes, to_rows = two_halves(cosines), two_halves(np.ascontiguousarray(cosines.T))
    sin_x = jnp.asarray(sin_x, F32)

    is_first, is_last = place_y == 0, place_y == py_count - 1
    w_near, returned, w_cell, (root, inv, start, from_below, top) = near_walls(
        w_rows,
        sin_x[None, :],
        jnp.asarray(np.repeat(sin_block[:, None], 128, axis=1), F32),
        jnp.stack([is_first, is_last]).astype(jnp.int32),
        ids,
        places,
        facet_temp[0],
        drag_coef[0],
        heat_coef[0],
    )

    end = np.where(np.arange(rows) == 0, np.sqrt(1.0 / rows), cosines[:, 0])
    end = jnp.asarray(np.repeat(end[:, None], 128, axis=1), F32)

    vectors, sin_z = level_tables(levels)
    pick = lambda three: jnp.where(is_first, three[0], jnp.where(is_last, three[2], three[1])).astype(F32)
    vectors, sin_z = pick(vectors), pick(sin_z)
    sine_z = sin_z[:, None] + sin_x[None, :]
    size_z = jnp.sqrt(sine_z)
    half_z = 0.5 * size_z
    cosh_z = jnp.sqrt(1.0 + half_z * half_z)
    half_step = cosh_z - half_z
    across = jnp.exp(2.0 * rows * jnp.log(half_step))
    scale = 1.0 / ((1.0 - across * across) * size_z)
    same_end = -half_step * (1.0 + across * across / (half_step * half_step)) * scale
    far_end = -2.0 * across * cosh_z * scale
    turns = np.arange(px_count)
    circulant = jnp.stack(
        [1.0 / (1.0 - 2.0 * same_end + 2.0 * math.cos(2.0 * math.pi * s / px_count) * far_end) for s in turns]
    )
    circulant = lax.optimization_barrier(circulant)
    phase_of = jnp.asarray(np.cos(2.0 * np.pi * turns[:, None] * turns[None, :] / px_count) / px_count, F32)
    offsets = jnp.stack([(place_x - turns) % px_count, (place_x - 1 - turns) % px_count])
    phases = phase_of[offsets]
    weights = jnp.sum(phases[:, :, :, None, None] * circulant[None, None], axis=2)

    mine = place_x * blocks + lax.axis_index("py_low")
    own_sin = lax.dynamic_slice_in_dim(sin_x, mine * own_kx, own_kx)
    join_root = recurrence_root(own_sin[:, None] + jnp.asarray(sin_y, F32)[None, :])

    tile = math.gcd(rows, 32)
    tiles = rows // tile
    flat = lambda i: pl.BlockSpec((tile, width), i)
    fixed = lambda a: pl.BlockSpec(a.shape, lambda i: (0,) * len(a.shape))
    pairs = levels // 2
    late = lambda i: (jnp.maximum(i - pairs, 0), 0)
    down = lambda i: (jnp.maximum(pairs - 1 - i, 0), 0, 0)
    slab = pl.BlockSpec((2, rows, width), down)
    end_late = pl.BlockSpec((tile, 128), late)
    ends_shape = jax.ShapeDtypeStruct((2, levels, width), F32)
    field, edges, ends, w_corr = pl.pallas_call(
        lambda *refs: forward_kernel(levels, tile, *refs),
        out_shape=(
            jax.ShapeDtypeStruct(w_star.shape, F32),
            jax.ShapeDtypeStruct((2, rows, width), F32),
            ends_shape,
            jax.ShapeDtypeStruct(w_rows.shape, F32),
        ),
        grid=(pairs + tiles,),
        in_specs=[SMEM, SMEM, HBM, slab] + [fixed(t) for t in (*x_tables, *to_modes)] + [flat(late)] * 4 + [end_late],
        out_specs=(
            HBM,
            pl.BlockSpec((2, tile, width), lambda i: (0, *late(i))),
            fixed(ends_shape),
            HBM,
        ),
        scratch_shapes=[
            pltpu.VMEM(w_star.shape, F32),
            pltpu.VMEM(w_rows.shape, F32),
            pltpu.VMEM((rows, width), F32),
            pltpu.VMEM((rows, width), F32),
            pltpu.VMEM((levels, 8, width), F32),
            pltpu.VMEM((levels, 8, width), F32),
            pltpu.SemaphoreType.DMA((2,)),
            pltpu.SemaphoreType.DMA((CHUNKS,)),
        ],
        compiler_params=PARAMS,
        name="forward",
    )(places, w_near, w_rows, horiz_div, *x_tables, *to_modes, root, inv, start, top, end)

    all_ends = lax.all_gather(ends, "px")
    packed = jax.ShapeDtypeStruct((group, 2, own_kx, rows), F32)
    working = [pltpu.VMEM((levels, 8, width), F32)] * 2
    edges = pl.pallas_call(
        lambda *refs: edge_kernel(levels, *refs),
        out_shape=packed,
        in_specs=[VMEM] * 11,
        out_specs=VMEM,
        scratch_shapes=working + [pltpu.VMEM((2, rows, width), F32)],
        compiler_params=PARAMS,
        name="edges",
    )(edges, all_ends, weights, vectors, root, inv, start, top, end, *to_modes)
    w_cell, edges = lax.optimization_barrier((w_cell, edges))
    places_late, edges = lax.optimization_barrier((places, edges))
    temp_own, temp_near = warm_air(temp_rows, ids, places_late, returned)
    edges = lax.all_to_all(edges, ("px", "py_low"), split_axis=0, concat_axis=0, tiled=True)
    edges, temp_near = lax.optimization_barrier((edges, temp_near))
    half_id = half.astype(jnp.int32).reshape(1)
    modes, alpha = pl.pallas_call(
        lambda *refs: gather_modes_kernel(levels, px_count, *refs),
        out_shape=(
            jax.ShapeDtypeStruct((blocks, 2, own_kx, y_cells), F32),
            jax.ShapeDtypeStruct((own_kx, y_cells), F32),
        ),
        in_specs=[SMEM] + [VMEM] * 8,
        out_specs=(VMEM, VMEM),
        compiler_params=PARAMS,
        name="gather_modes",
    )(half_id, edges, *y_tables, join_root)
    alpha, temp_own = lax.optimization_barrier((alpha, temp_own))
    new_temp = warm_facets(
        temp_own, w_cell, facet_temp[0], net_radiation[0], heat_capacity[0], heat_coef[0]
    )
    alpha = lax.ppermute(alpha, "py_half", [(0, 1), (1, 0)])
    alpha, new_temp = lax.optimization_barrier((alpha, new_temp))
    joined = pl.pallas_call(
        lambda *refs: join_kernel(levels, px_count, *refs),
        out_shape=packed,
        in_specs=[SMEM] + [VMEM] * 9,
        out_specs=VMEM,
        scratch_shapes=[pltpu.VMEM((blocks, 2, own_kx, y_cells), F32)],
        compiler_params=PARAMS,
        name="join",
    )(half_id, modes, alpha, *y_tables, join_root)
    joined, temp_near = lax.optimization_barrier((joined, temp_near))
    theta_new = pl.pallas_call(
        theta_kernel,
        out_shape=jax.ShapeDtypeStruct(temp_rows.shape, BF16),
        in_specs=[SMEM, SMEM, VMEM],
        out_specs=VMEM,
        scratch_shapes=[pltpu.VMEM(temp_rows.shape, F32)],
        compiler_params=PARAMS,
        cost_estimate=pl.CostEstimate(flops=temp_rows.size, bytes_accessed=8 * temp_rows.size, transcendentals=0),
        name="theta",
    )(places, temp_near, temp_rows).reshape(air_temp.shape)
    joined = lax.all_to_all(joined, ("px", "py_low"), split_axis=0, concat_axis=0, tiled=True)
    sides, more = pl.pallas_call(
        lambda *refs: spread_kernel(levels, *refs),
        out_shape=(jax.ShapeDtypeStruct((2, rows, width), F32), ends_shape),
        in_specs=[VMEM] * 8,
        out_specs=(VMEM, VMEM),
        scratch_shapes=working,
        compiler_params=SMALL,
        name="spread",
    )(joined, *to_modes, root, start, from_below, top, end)
    more = lax.all_gather(more, "px")

    early = lambda i: (jnp.minimum(i, tiles - 1), 0)
    up = lambda i: (jnp.maximum(i - tiles, 0), 0, 0)
    slab = pl.BlockSpec((2, rows, width), up)
    w_new = pl.pallas_call(
        lambda *refs: inverse_kernel(levels, tile, *refs),
        out_shape=jax.ShapeDtypeStruct(w_star.shape, F32),
        grid=(tiles + pairs,),
        in_specs=[
            SMEM,
            pl.BlockSpec((levels, tile, width), lambda i: (0, *early(i))),
            pl.BlockSpec((2, tile, width), lambda i: (0, *early(i))),
        ]
        + [fixed(a) for a in (all_ends, more, weights, vectors)]
        + [flat(early)] * 4
        + [pl.BlockSpec((tile, 128), early)]
        + [fixed(t) for t in (*x_tables, *to_rows)]
        + [slab, fixed(roof_level)],
        out_specs=slab,
        scratch_shapes=[pltpu.VMEM(w_star.shape, F32)] + working,
        compiler_params=PARAMS,
        name="inverse",
    )(
        place_y.astype(jnp.int32).reshape(1),
        field,
        sides,
        all_ends,
        more,
        weights,
        vectors,
        root,
        start,
        from_below,
        top,
        end,
        *x_tables,
        *to_rows,
        w_corr.reshape(w_star.shape),
        roof_level,
    )
    return (w_new, theta_new, new_temp[None])


def solution(mesh):
    px_count, py_count = mesh.devices.shape
    split_mesh = jax.sharding.Mesh(
        mesh.devices.reshape(px_count, 2, py_count // 2), ("px", "py_half", "py_low")
    )
    py, every = ("py_half", "py_low"), ("px", "py_half", "py_low")
    placed = (P(py, "px", None),) * 3 + (P("px", None),) + (P(every, None),) * 6
    return jax.shard_map(
        body,
        mesh=split_mesh,
        in_specs=placed,
        out_specs=(P(py, "px", None), P(py, "px", None), P(every, None)),
        check_vma=False,
    )
```
